256 devices in a mesh: wide: 32 (over x_hi, z, core), narrow: 8 (over y, x_lo).
Axes of the slice: x: 4 (x_hi: 2, x_lo: 2; x = x_hi * 2 + x_lo), y: 4, z: 8, core: 2. Of those that a mesh axis runs over, the one named last changes fastest.
Arguments:
- image_tokens: bfloat16 [64, 512, 1024], P('narrow', 'wide'), may hold values from -24 to 24
- qkv_weight: bfloat16 [1024, 3072], P('wide'), may hold values from -0.1875 to 0.1875
- block_list: int32 [8, 64], P('narrow', 'wide'), may hold values from 0 to 1, as said below
- block_count: int32 [8, 32], P('narrow', 'wide'), may hold values from 1 to 2, as said below
- out_grad: bfloat16 [64, 512, 1024], P('narrow', 'wide'), may hold values from -6 to 6
Outputs:
- attn_out: bfloat16 [64, 512, 1024], P('narrow', 'wide')
- grad_x: bfloat16 [64, 512, 1024], P('narrow', 'wide')
- grad_w: float32 [1024, 3072], P('wide')
The draws below stay inside these ranges and needn't reach their ends.
Inputs may be any that keep to these rules, and one draw needn't show every extreme that they name: `block_list`: each tile's 2 entries are distinct block numbers of that tile, 0 to 1, row-major over its blocks; entries past the tile's count are padding. `block_count`: some tile's list is full.
All inputs are finite; a program needn't handle non-finite values.
Results may differ from the reference program's by a relative error of at most 0.0065.
The reference program's roundings to bfloat16 on the way count: a program that leaves them out, or rounds other values in their place, can miss the bound.
Values may be sent and summed in bfloat16 or wider, within the bound.
A program may use at most 128 MiB of HBM per device.

```python
import jax
import jax.numpy as jnp
from jax import lax

D = 1024
HEADS = 16
HEAD = 64
WIN = 13
BLK = 8
TR = 8
TC = 16
NB = 2
MAXB = 2
GR = 64
GC = 512
TOKENS = 32768
N_WIDE = 32
N_NARROW = 8


def shared_tiles(key):
    base = jax.random.fold_in(key, 11)
    score_key, first_key, second_key = jax.random.split(base, 3)
    scores = jax.random.randint(score_key, (N_NARROW, N_WIDE, NB), 0, 65536) * NB + jnp.arange(NB, dtype=jnp.int32)
    order = jnp.argsort(scores, axis=-1)[:, :, :MAXB].astype(jnp.int32)
    first = jax.random.randint(first_key, (N_NARROW, N_WIDE), 0, MAXB + 1)
    second = jax.random.randint(second_key, (N_NARROW, N_WIDE), 0, MAXB + 1)
    counts = jnp.minimum(MAXB, 1 + first * second // MAXB).astype(jnp.int32)
    counts = counts.at[0, 0].set(MAXB)
    return (order, counts)


def draw_block_list(key, part):
    order, counts = shared_tiles(key)
    return order.reshape(N_NARROW, N_WIDE * MAXB)


def draw_block_count(key, part):
    order, counts = shared_tiles(key)
    return counts


def draw_image_tokens(key, part):
    first_key = jax.random.fold_in(jax.random.fold_in(key, 23), 0)
    shape = (GR, GC, D)
    values = jnp.clip(jax.random.normal(first_key, shape), -4.0, 4.0)
    return values.astype(jnp.float32).astype(jnp.bfloat16)


def levels(stream_key, shape, cuts, low, high):
    factor_of = 1.0
    for position, shards_of in cuts:
        draws = jax.random.uniform(jax.random.fold_in(jax.random.fold_in(stream_key, 6), position), (shards_of,), jnp.float32, low / len(cuts), high / len(cuts))
        factor_of = factor_of * jnp.repeat(jnp.exp(draws), shape[position] // shards_of).reshape((-1,) + (1,) * (len(shape) - 1 - position))
    return factor_of


def gaussian(rng, extent, scale, limit, pieces=(), kind=jnp.bfloat16):
    drawn = jax.random.normal(rng, extent, jnp.float32) * scale
    if len(pieces) > 0:
        drawn = levels(rng, extent, pieces, -0.22, 0.18) * drawn
    return jnp.clip(drawn, min=-limit, max=limit).astype(kind)


def setup_inputs(seed: int = 0) -> dict:
    splits = jax.random.split(jax.random.key(seed), 6)
    image_tokens = draw_image_tokens(jax.random.fold_in(splits[5], 71), 0)
    qkv_weight = gaussian(splits[1], (D, 3 * D), D ** -0.5, 0.1875, ((0, 32),))
    block_list = draw_block_list(jax.random.fold_in(splits[5], 71), 0)
    block_count = draw_block_count(jax.random.fold_in(splits[5], 71), 0)
    out_grad = gaussian(splits[4], (GR, GC, D), 1.0, 6.0, ((0, 8), (1, 32)))
    return {"image_tokens": image_tokens, "qkv_weight": qkv_weight, "block_list": block_list, "block_count": block_count, "out_grad": out_grad}


NEGATIVE = -1e30


def window_table():
    radius = WIN // 2
    region = BLK + 2 * radius
    inner = jnp.arange(BLK * BLK, dtype=jnp.int32)
    outer = jnp.arange(region * region, dtype=jnp.int32)
    down = outer[None, :] // region - radius - inner[:, None] // BLK
    across = outer[None, :] % region - radius - inner[:, None] % BLK
    return (jnp.abs(down) <= radius) & (jnp.abs(across) <= radius)


def row_blocks(field, index):
    strip = lax.dynamic_slice_in_dim(field, index * BLK, BLK, 0)
    shaped = strip.reshape((BLK, GC // BLK, BLK) + field.shape[2:])
    shaped = jnp.moveaxis(shaped, 1, 0)
    return shaped.reshape((GC // BLK, BLK * BLK) + field.shape[2:])


def row_regions(padded, index):
    radius = WIN // 2
    region = BLK + 2 * radius
    strip = lax.dynamic_slice_in_dim(padded, index * BLK, region, 0)
    columns = (jnp.arange(GC // BLK, dtype=jnp.int32) * BLK)[:, None] + jnp.arange(region, dtype=jnp.int32)[None, :]
    taken = jnp.moveaxis(strip[:, columns], 1, 0)
    return taken.reshape((GC // BLK, region * region) + padded.shape[2:])


def unblock(stacked):
    rest = stacked.shape[3:]
    shaped = stacked.reshape((GR // BLK, GC // BLK, BLK, BLK) + rest)
    shaped = jnp.swapaxes(shaped, 1, 2)
    return shaped.reshape((GR, GC) + rest)


def pad_grid(field):
    radius = WIN // 2
    widths = ((radius, radius), (radius, radius)) + ((0, 0),) * (field.ndim - 2)
    return jnp.pad(field, widths)


def query_side(query, keys, values, grad_out, allowed):
    scale = HEAD ** -0.5
    scores = jnp.einsum("bqhd,bkhd->bhqk", query.astype(jnp.float32), keys.astype(jnp.float32)) * scale
    scores = jnp.where(allowed[:, None], scores, NEGATIVE)
    top = jnp.max(scores, axis=-1, keepdims=True)
    total = jnp.sum(jnp.exp(scores - top), axis=-1, keepdims=True)
    logsum = top + jnp.log(total)
    probs = jnp.exp(scores - logsum)
    weights = probs.astype(jnp.bfloat16)
    output = jnp.einsum("bhqk,bkhd->bqhd", weights.astype(jnp.float32), values.astype(jnp.float32)).astype(jnp.bfloat16)
    delta = jnp.sum(grad_out.astype(jnp.float32) * output.astype(jnp.float32), axis=-1)
    dprobs = jnp.einsum("bqhd,bkhd->bhqk", grad_out.astype(jnp.float32), values.astype(jnp.float32))
    dscores = (probs * (dprobs - jnp.swapaxes(delta, 1, 2)[..., None]) * scale).astype(jnp.bfloat16)
    grad_query = jnp.einsum("bhqk,bkhd->bqhd", dscores.astype(jnp.float32), keys.astype(jnp.float32)).astype(jnp.bfloat16)
    return output, jnp.swapaxes(logsum[..., 0], 1, 2), delta, grad_query


def key_side(keys, values, query, grad_out, logsum, delta, allowed):
    scale = HEAD ** -0.5
    scores = jnp.einsum("bjhd,bihd->bhji", keys.astype(jnp.float32), query.astype(jnp.float32)) * scale
    shift = jnp.swapaxes(logsum, 1, 2)[:, :, None, :]
    probs = jnp.where(allowed[:, None], jnp.exp(scores - shift), 0.0)
    weights = probs.astype(jnp.bfloat16)
    grad_values = jnp.einsum("bhji,bihd->bjhd", weights.astype(jnp.float32), grad_out.astype(jnp.float32)).astype(jnp.bfloat16)
    dprobs = jnp.einsum("bjhd,bihd->bhji", values.astype(jnp.float32), grad_out.astype(jnp.float32))
    dscores = (probs * (dprobs - jnp.swapaxes(delta, 1, 2)[:, :, None, :]) * scale).astype(jnp.bfloat16)
    grad_keys = jnp.einsum("bhji,bihd->bjhd", dscores.astype(jnp.float32), query.astype(jnp.float32)).astype(jnp.bfloat16)
    return grad_keys, grad_values


def reference(image_tokens, qkv_weight, block_list, block_count, out_grad):
    flat = image_tokens.reshape(TOKENS, D)
    projected = jnp.dot(flat, qkv_weight, preferred_element_type=jnp.float32).astype(jnp.bfloat16)
    projected = projected.reshape(GR, GC, 3, HEADS, HEAD)
    query = projected[:, :, 0]
    keys = projected[:, :, 1]
    values = projected[:, :, 2]
    grad_out = out_grad.reshape(GR, GC, HEADS, HEAD)
    lists = block_list.reshape(N_NARROW, N_WIDE, MAXB)
    live = jnp.arange(MAXB, dtype=jnp.int32)[None, None, :] < block_count[:, :, None]
    hits = (lists[..., None] == jnp.arange(NB, dtype=jnp.int32)) & live[..., None]
    block_on = jnp.any(hits, axis=2).astype(jnp.float32).reshape(N_NARROW, N_WIDE, TR // BLK, TC // BLK)
    block_on = jnp.swapaxes(block_on, 1, 2).reshape(GR // BLK, GC // BLK)
    active = jnp.repeat(jnp.repeat(block_on, BLK, axis=0), BLK, axis=1)
    inside = pad_grid(jnp.ones((GR, GC), dtype=jnp.float32))
    table = window_table()
    pad_keys = pad_grid(keys)
    pad_values = pad_grid(values)

    def query_row(index):
        allowed = table[None] & (row_regions(inside, index) > 0)[:, None, :]
        return query_side(row_blocks(query, index), row_regions(pad_keys, index), row_regions(pad_values, index), row_blocks(grad_out, index), allowed)

    output, logsum, delta, grad_query = lax.map(query_row, jnp.arange(GR // BLK, dtype=jnp.int32))
    output = unblock(output) * active[:, :, None, None].astype(output.dtype)
    grad_query = unblock(grad_query) * active[:, :, None, None].astype(grad_query.dtype)
    logsum = unblock(logsum) * active[:, :, None]
    delta = unblock(delta) * active[:, :, None]
    pad_query = pad_grid(query)
    pad_grad = pad_grid(grad_out)
    pad_logsum = pad_grid(logsum)
    pad_delta = pad_grid(delta)
    pad_active = pad_grid(active)

    def key_row(index):
        allowed = table[None] & (row_regions(pad_active, index) > 0)[:, None, :]
        return key_side(row_blocks(keys, index), row_blocks(values, index), row_regions(pad_query, index), row_regions(pad_grad, index), row_regions(pad_logsum, index), row_regions(pad_delta, index), allowed)

    grad_keys, grad_values = lax.map(key_row, jnp.arange(GR // BLK, dtype=jnp.int32))
    grad_keys = unblock(grad_keys)
    grad_values = unblock(grad_values)
    grads = jnp.concatenate([grad_query.reshape(GR, GC, D), grad_keys.reshape(GR, GC, D), grad_values.reshape(GR, GC, D)], axis=-1).reshape(TOKENS, 3 * D)
    grad_x = jnp.dot(grads, qkv_weight.T, preferred_element_type=jnp.float32).astype(jnp.bfloat16).reshape(GR, GC, D)
    grad_w = jnp.dot(flat.T, grads, preferred_element_type=jnp.float32) * (TOKENS ** -0.5)
    return output.reshape(GR, GC, D), grad_x, grad_w
```

```python
import functools
import math

import jax
import jax.numpy as jnp
from jax import lax
from jax.experimental import pallas as pl
from jax.experimental.pallas import tpu as pltpu
from jax.sharding import PartitionSpec as P

MESH = pl.DeviceIdType.MESH
F32 = jnp.float32
BF16 = jnp.bfloat16
RADIUS = 6
NEGATIVE = -1e30
HUGE = 1e30
SCALE = 0.125
VMEM_LIMIT = 60 * 1024 * 1024
ANY = pl.BlockSpec(memory_space=pl.ANY)
VM = pl.BlockSpec(memory_space=pltpu.VMEM)

ROWS = {-1: (0, 6, 14), 0: (0, 8, 6), 1: (2, 6, 0)}


def place():
    wide = lax.axis_index("wide")
    narrow = lax.axis_index("narrow")
    return narrow, wide // 2, wide % 2


def device(narrow, chip, core):
    return {"wide": lax.rem(chip, 16) * 2 + core, "narrow": lax.rem(narrow, 8)}


def remote(src, dst, send, recv, to):
    return pltpu.make_async_remote_copy(
        src_ref=src, dst_ref=dst, send_sem=send, recv_sem=recv, device_id=to, device_id_type=MESH
    )


def greet(devices):
    barrier = pltpu.get_barrier_semaphore()
    for to in devices:
        pl.semaphore_signal(barrier, inc=1, device_id=to, device_id_type=MESH)
    pl.semaphore_wait(barrier, len(devices))


def half_of(core):
    return pl.ds(pl.multiple_of(core * 512, 512), 512)


def gather_kernel(
    x_ref, g_ref, w_ref, act_ref, xr_ref, gr_ref, wg_ref, acts_ref,
    h_send, h_recv, h_local, s_send, s_recv, a_send, a_recv, a_local,
    w_send, w_recv, w_local, p_send, p_recv, r_send, r_recv,
):
    n, chip, core = place()
    other = 1 - core
    z = lax.rem(chip, 8)
    xh = chip // 8
    step = 2 * core - 1
    side_chip = chip + step + 16
    up = device(n, xh * 8 + lax.rem(z + 1, 8), core)
    down = device(n, xh * 8 + lax.rem(z + 7, 8), core)
    partner = device(n, (1 - xh) * 8 + z, core)
    sibling = device(n, chip, other)

    peers = [up, down, partner, sibling]
    for dn in (-1, 0, 1):
        for dc in (-1, 0, 1):
            for c in (0, 1):
                if (dn, dc) != (0, 0):
                    peers.append(device(n + dn + 8, chip + dc + 16, c))
    greet(peers)

    sends = []
    own = []
    for t in range(3):
        here = wg_ref.at[t, xh, z, core]
        cp = pltpu.make_async_copy(
            w_ref.at[:, pl.ds(pl.multiple_of(t * 1024 + core * 512, 512), 512)], here, w_local.at[t]
        )
        cp.start()
        own.append(cp)
        cp = remote(
            w_ref.at[:, pl.ds(pl.multiple_of(t * 1024 + other * 512, 512), 512)],
            here, w_send.at[t], w_recv.at[t], sibling,
        )
        cp.start()
        sends.append(cp)

    tensors = ((g_ref, lambda c: gr_ref), (x_ref, lambda c: xr_ref.at[c]))
    locals_ = []
    for i, (src, dst) in enumerate(tensors):
        for dn in (-1, 0, 1):
            lo, count, at = ROWS[dn]
            for side in (0, 1):
                for rel in (0, 1):
                    c = core if rel == 0 else other
                    if side == 0:
                        source = src.at[pl.ds(lo, count), :, :, half_of(c)]
                        target = dst(c).at[pl.ds(at, count), pl.ds(1 + 2 * core, 2)]
                        slot = core
                        to = device(n + dn + 8, chip, c)
                    else:
                        source = src.at[pl.ds(lo, count), pl.ds(core, 1), :, half_of(c)]
                        target = dst(c).at[pl.ds(at, count), pl.ds(5 * other, 1)]
                        slot = 3 - core
                        to = device(n + dn + 8, side_chip, c)
                    if dn == 0 and side == 0 and rel == 0:
                        cp = pltpu.make_async_copy(source, target, h_local.at[i])
                        locals_.append(cp)
                    else:
                        cp = remote(
                            source, target, h_send.at[i, dn + 1, side, rel],
                            h_recv.at[i, dn + 1, slot], to,
                        )
                        sends.append(cp)
                    cp.start()

    act_copy = pltpu.make_async_copy(act_ref, acts_ref.at[core], a_local)
    act_copy.start()
    act_send = remote(act_ref, acts_ref.at[core], a_send, a_recv, sibling)
    act_send.start()
    sends.append(act_send)

    for t in range(3):
        own[t].wait()
        remote(
            w_ref.at[:, pl.ds(0, 512)], wg_ref.at[t, xh, z, other],
            w_send.at[t], w_recv.at[t], sibling,
        ).wait_recv()
    hops = {(0, 0): 4, (0, 1): 3, (1, 0): 3, (1, 1): 4}

    def slab(s, index):
        return wg_ref.at[:, xh if s == 0 else 1 - xh, lax.rem(index + 16, 8)]

    def forward(s, d, k):
        moved = slab(s, z - k if d == 0 else z + k)
        cp = remote(
            moved, moved, r_send.at[s, d, k], r_recv.at[s, d, k], up if d == 0 else down
        )
        cp.start()
        sends.append(cp)

    def arrived(s, d, k):
        landed = slab(s, z - 1 - k if d == 0 else z + 1 + k)
        remote(landed, landed, r_send.at[s, d, k], r_recv.at[s, d, k], up).wait_recv()

    mine = slab(0, z)
    cp = remote(mine, mine, p_send, p_recv, partner)
    cp.start()
    sends.append(cp)
    forward(0, 0, 0)
    forward(0, 1, 0)
    theirs = slab(1, z)
    remote(theirs, theirs, p_send, p_recv, partner).wait_recv()
    forward(1, 0, 0)
    forward(1, 1, 0)

    def finish_region(i, dst):
        locals_[i].wait()
        for dn in (-1, 0, 1):
            lo, count, at = ROWS[dn]
            for piece in range(4):
                if piece < 2:
                    if dn == 0 and piece == 1:
                        continue
                    slot = other if dn == 0 else piece
                    landed = dst.at[pl.ds(at, count), pl.ds(1 + 2 * slot, 2)]
                else:
                    slot = piece
                    landed = dst.at[pl.ds(at, count), pl.ds(0 if piece == 2 else 5, 1)]
                remote(
                    landed, landed, h_send.at[i, dn + 1, 0, 0], h_recv.at[i, dn + 1, slot], sibling
                ).wait_recv()

    for k in range(1, 5):
        for s in range(2):
            for d in range(2):
                if k <= hops[s, d]:
                    arrived(s, d, k - 1)
                if k < hops[s, d]:
                    forward(s, d, k)
        if k == 2:
            finish_region(1, xr_ref.at[core])
            cp = remote(xr_ref.at[core], xr_ref.at[core], s_send, s_recv, sibling)
            cp.start()
            sends.append(cp)
    finish_region(0, gr_ref)
    act_copy.wait()
    remote(act_ref, acts_ref.at[other], a_send, a_recv, sibling).wait_recv()
    remote(xr_ref.at[other], xr_ref.at[other], s_send, s_recv, sibling).wait_recv()
    for cp in sends:
        cp.wait_send()


def gather_all(x4, g4, weight, act):
    dma = pltpu.SemaphoreType.DMA
    return pl.pallas_call(
        gather_kernel,
        out_shape=(
            jax.ShapeDtypeStruct((2, 20, 6, 8, 512), BF16),
            jax.ShapeDtypeStruct((20, 6, 8, 512), BF16),
            jax.ShapeDtypeStruct((3, 2, 8, 2, 32, 512), BF16),
            jax.ShapeDtypeStruct((2, 128, 128), F32),
        ),
        in_specs=[VM] * 4,
        out_specs=(ANY,) * 4,
        scratch_shapes=[
            dma((2, 3, 2, 2)), dma((2, 3, 4)), dma((2,)), dma, dma, dma, dma, dma,
            dma((3,)), dma((3,)), dma((3,)), dma, dma, dma((2, 2, 4)), dma((2, 2, 4)),
        ],
        compiler_params=pltpu.CompilerParams(collective_id=0, has_side_effects=True),
        name="gather_all",
    )(x4, g4, weight, act)


def window_bias(hf):
    n, chip, _ = place()
    shape = (128, 640)
    inner = lax.broadcasted_iota(jnp.int32, shape, 0)
    outer = lax.broadcasted_iota(jnp.int32, shape, 1)
    row, col = outer // 32, outer % 32
    down = row - RADIUS - inner // 16
    across = col - 8 - inner % 16
    grid_row = n * 8 - RADIUS + row
    grid_col = chip * 32 - 8 + 16 * hf + col
    ok = (jnp.abs(down) <= RADIUS) & (jnp.abs(across) <= RADIUS)
    ok = ok & (grid_row >= 0) & (grid_row < 64) & (grid_col >= 0) & (grid_col < 512)
    return jnp.where(ok, 0.0, NEGATIVE)


def nt(a, b):
    return lax.dot_general(a, b, (((1,), (1,)), ((), ())), preferred_element_type=F32)


def nn(a, b):
    return jnp.dot(a, b, preferred_element_type=F32)


def tn(a, b):
    return lax.dot_general(a, b, (((0,), (0,)), ((), ())), preferred_element_type=F32)


def lanes_of(hp):
    return pl.ds(pl.multiple_of(hp * 128, 128), 128)


def head_masks():
    lane = lax.broadcasted_iota(jnp.int32, (128, 128), 1)
    low = lane < 64
    return low, (low.astype(F32).astype(BF16), (1.0 - low.astype(F32)).astype(BF16)), lane


def query_kernel(
    xr_ref, gr_ref, wg_ref, acts_ref,
    attn_ref, dq_ref, ld_ref, qr_ref, grs_ref, kown_ref, vown_ref, xown_ref,
    acc, kr, vr, qown, gown, ldacc, bias,
):
    def own_of(values, hf):
        return values[6:14, 1 + 2 * hf : 3 + 2 * hf].reshape(128, 512)

    for t, region in enumerate((qr_ref, kr, vr)):

        def chunk(i, carry, t=t, region=region):
            rows = pl.ds(pl.multiple_of(i * 192, 192), 192)
            out = nn(xr_ref[0, pl.ds(4 * i, 4)].reshape(192, 512), wg_ref[t, :512])
            out += nn(xr_ref[1, pl.ds(4 * i, 4)].reshape(192, 512), wg_ref[t, 512:])
            acc[pl.ds(4 * i, 4)] = out.reshape(4, 6, 8, 512)
            region[pl.ds(4 * i, 4)] = out.astype(BF16).reshape(4, 48, 512)
            return carry

        lax.fori_loop(0, 5, chunk, 0)
        for hf in range(2):
            own = acc[6:14, 1 + 2 * hf : 3 + 2 * hf].reshape(128, 512).astype(BF16)
            if t == 0:
                qown[hf] = own * SCALE
            elif t == 1:
                kown_ref[hf] = own * SCALE
            else:
                vown_ref[hf] = own

    def regroup(i, carry):
        rows = gr_ref[pl.ds(4 * i, 4)].astype(F32).reshape(192, 512)
        grs_ref[pl.ds(4 * i, 4)] = rows.astype(BF16).reshape(4, 48, 512)
        return carry

    lax.fori_loop(0, 5, regroup, 0)
    for hf in range(2):
        groups = pl.ds(1 + 2 * hf, 2)
        gown[hf] = gr_ref[6:14, groups].astype(F32).reshape(128, 512).astype(BF16)
        for c in range(2):
            xown_ref[hf, :, c * 512 : c * 512 + 512] = (
                xr_ref[c, 6:14, groups].astype(F32).reshape(128, 512).astype(BF16)
            )
        bias[...] = window_bias(hf)
        ldacc[...] = jnp.zeros_like(ldacc)

        def pair(hp, carry, hf=hf):
            lanes = lanes_of(hp)
            low, masks, lane = head_masks()
            keys = kr[:, 16 * hf : 16 * hf + 32, lanes].reshape(640, 128)
            values = vr[:, 16 * hf : 16 * hf + 32, lanes].reshape(640, 128)
            query = qown[hf, :, lanes]
            grad = gown[hf, :, lanes]
            active = acts_ref[hf]
            outs, dqs = [], []
            ld = ldacc[...]
            for j in range(2):
                s = nt(query * masks[j], keys) + bias[...]
                top = jnp.max(s, axis=1, keepdims=True)
                e = jnp.exp(s - top)
                total = jnp.sum(e, axis=1, keepdims=True)
                p = e * (1.0 / total)
                lse = top + jnp.log(total)
                out = nn(p.astype(BF16), values)
                out = out.astype(BF16).astype(F32)
                gm = grad * masks[j]
                delta = jnp.sum(gm.astype(F32) * out, axis=1, keepdims=True)
                dp = nt(gm, values)
                ds = (p * (dp - delta) * SCALE).astype(BF16)
                dqs.append(nn(ds, keys))
                outs.append(out)
                on = active > 0.0
                head = 2 * hp + j
                ld = jnp.where(lane == head, jnp.where(on, lse, HUGE), ld)
                ld = jnp.where(lane == head + 8, jnp.where(on, delta, 0.0), ld)
            ldacc[...] = ld
            attn_ref[hf, :, lanes] = (jnp.where(low, outs[0], outs[1]) * active).astype(BF16)
            dq_ref[hf, :, lanes] = (jnp.where(low, dqs[0], dqs[1]) * active).astype(BF16)
            return carry

        lax.fori_loop(0, 4, pair, 0)
        ld_ref[:, 2 * hf : 2 * hf + 2] = ldacc[...].reshape(8, 2, 8, 128)


def query_side(xr, gr, wg, acts):
    shape = jax.ShapeDtypeStruct
    return pl.pallas_call(
        query_kernel,
        out_shape=(
            shape((2, 128, 512), BF16), shape((2, 128, 512), BF16), shape((8, 4, 8, 128), F32),
            shape((20, 48, 512), BF16), shape((20, 48, 512), BF16),
            shape((2, 128, 512), BF16), shape((2, 128, 512), BF16), shape((2, 128, 1024), BF16),
        ),
        in_specs=[VM] * 4,
        out_specs=(VM,) * 8,
        scratch_shapes=[
            pltpu.VMEM((20, 6, 8, 512), F32), pltpu.VMEM((20, 48, 512), BF16),
            pltpu.VMEM((20, 48, 512), BF16), pltpu.VMEM((2, 128, 512), BF16),
            pltpu.VMEM((2, 128, 512), BF16), pltpu.VMEM((128, 128), F32),
            pltpu.VMEM((128, 640), F32),
        ],
        compiler_params=pltpu.CompilerParams(vmem_limit_bytes=VMEM_LIMIT),
        name="query_side",
    )(xr, gr, wg, acts)


def halo_kernel(ld_ref, out_ref, send, recv, local):
    n, chip, core = place()
    near = [(dn, dc) for dn in (-1, 0, 1) for dc in (-1, 0, 1) if (dn, dc) != (0, 0)]
    greet([device(n + dn + 8, chip + dc + 16, core) for dn, dc in near])
    columns = {-1: (0, 1, 5), 0: (0, 4, 1), 1: (3, 1, 0)}
    copies = []
    for dn, dc in near:
        lo, count, at = ROWS[dn]
        first, width, to = columns[dc]
        cp = remote(
            ld_ref.at[pl.ds(lo, count), pl.ds(first, width)],
            out_ref.at[pl.ds(at, count), pl.ds(to, width)],
            send.at[dn + 1, dc + 1], recv.at[dn + 1, dc + 1],
            device(n + dn + 8, chip + dc + 16, core),
        )
        cp.start()
        copies.append(cp)
    own = pltpu.make_async_copy(ld_ref, out_ref.at[pl.ds(6, 8), pl.ds(1, 4)], local)
    own.start()
    own.wait()
    for cp in copies:
        cp.wait()


def halo(ld):
    dma = pltpu.SemaphoreType.DMA
    return pl.pallas_call(
        halo_kernel,
        out_shape=jax.ShapeDtypeStruct((20, 6, 8, 128), F32),
        in_specs=[VM],
        out_specs=ANY,
        scratch_shapes=[dma((3, 3)), dma((3, 3)), dma],
        compiler_params=pltpu.CompilerParams(collective_id=1, has_side_effects=True),
        name="halo",
    )(ld)


def key_kernel(
    qr_ref, gr_ref, kown_ref, vown_ref, ldr_ref, dq_ref, xown_ref, wg_ref,
    gx_ref, gw_ref, dk, dv, lds, bias,
):
    for hf in range(2):
        bias[...] = window_bias(hf)
        for i in range(5):
            part = ldr_ref[4 * i : 4 * i + 4, 2 * hf : 2 * hf + 4].reshape(128, 128)
            lds[:, 128 * i : 128 * i + 128] = part.T

        def pair(hp, carry, hf=hf):
            lanes = lanes_of(hp)
            low, masks, _ = head_masks()
            query = qr_ref[:, 16 * hf : 16 * hf + 32, lanes].reshape(640, 128)
            grad = gr_ref[:, 16 * hf : 16 * hf + 32, lanes].reshape(640, 128)
            keys = kown_ref[hf, :, lanes]
            values = vown_ref[hf, :, lanes]
            dks, dvs = [], []
            for j in range(2):
                head = 2 * hp + j
                s = nt(keys * masks[j], query) + bias[...]
                p = jnp.exp(s - lds[pl.ds(head, 1), :])
                dvs.append(nn(p.astype(BF16), grad))
                dp = nt(values * masks[j], grad)
                ds = (p * (dp - lds[pl.ds(head + 8, 1), :]) * SCALE).astype(BF16)
                dks.append(nn(ds, query))
            dk[pl.ds(128 * hf, 128), lanes] = jnp.where(low, dks[0], dks[1]).astype(BF16)
            dv[pl.ds(128 * hf, 128), lanes] = jnp.where(low, dvs[0], dvs[1]).astype(BF16)
            return carry

        lax.fori_loop(0, 4, pair, 0)

    def columns(i, carry):
        at = pl.ds(pl.multiple_of(i * 128, 128), 128)
        tokens = xown_ref[:, :, at].reshape(256, 128)
        dq = dq_ref[...].reshape(256, 512)
        total = nt(dq, wg_ref[0, at]) + nt(dk[...], wg_ref[1, at]) + nt(dv[...], wg_ref[2, at])
        gx_ref[:, :, at] = total.reshape(2, 128, 128)
        gw_ref[0, at] = tn(tokens, dq)
        gw_ref[1, at] = tn(tokens, dk[...])
        gw_ref[2, at] = tn(tokens, dv[...])
        return carry

    lax.fori_loop(0, 8, columns, 0)


def key_side(qr, gr, kown, vown, ldr, dq, xown, wg):
    shape = jax.ShapeDtypeStruct
    return pl.pallas_call(
        key_kernel,
        out_shape=(shape((2, 128, 1024), F32), shape((3, 1024, 512), F32)),
        in_specs=[VM] * 8,
        out_specs=(VM,) * 2,
        scratch_shapes=[
            pltpu.VMEM((256, 512), BF16), pltpu.VMEM((256, 512), BF16),
            pltpu.VMEM((128, 640), F32), pltpu.VMEM((128, 640), F32),
        ],
        compiler_params=pltpu.CompilerParams(vmem_limit_bytes=VMEM_LIMIT),
        name="key_side",
    )(qr, gr, kown, vown, ldr, dq, xown, wg)


XPEERS = ((0, 1), (1, 0), (1, 1))


def reduce_kernel(
    p_ref, attn_ref, gx_ref, arx_ref, grx_ref, gw_ref,
    yb, xb, rb, ks, vs, qs, xb2, yb2, qxb, qx, qyb, kv, zb, fin,
    c_send, c_recv, y_send, y_recv, x_send, x_recv, r_send, r_recv,
    x2_send, x2_recv, y2_send, y2_recv, qx_send, qx_recv, qy_send, qy_recv,
    z_send, z_recv, f_send, f_recv, f_local,
):
    n, chip, core = place()
    other = 1 - core
    z = lax.rem(chip, 8)
    xh = chip // 8
    y = n // 2
    xl = lax.rem(n, 2)

    def at(xh_, z_, core_, y_, xl_):
        return device(y_ * 2 + xl_, xh_ * 8 + z_, core_)

    def ypeer(d):
        return lax.rem(y + d, 4)

    def zpeer(d):
        return lax.rem(z + d + 8, 8)

    def flip(value, by):
        return 1 - value if by else value

    peers = [at(xh, zpeer(d), core, y, xl) for d in range(1, 8)]
    peers += [at(1 - xh, z, core, y, flip(xl, b)) for b in (0, 1)]
    for c in (0, 1):
        for d in range(4):
            for b in (0, 1):
                if (c, d, b) != (0, 0, 0):
                    peers.append(at(xh, z, flip(core, c), ypeer(d), flip(xl, b)))
    greet(peers)

    sends = []

    def go(src, dst, send, recv, to):
        cp = remote(src, dst, send, recv, to)
        cp.start()
        sends.append(cp)

    def came(dst, send, recv):
        remote(dst, dst, send, recv, at(xh, z, other, y, xl)).wait_recv()

    def quarter(index):
        return pl.ds(pl.multiple_of(index * 128, 128), 128)

    def ring_chunk(zd, d, s):
        return p_ref.at[0, s, zd, :, :, pl.ds(256 * d, 256)]

    def ring_to(d):
        return at(xh, zpeer(1 if d == 0 else -1), core, y, xl)

    for s in range(2):
        for d in range(2):
            first = zpeer(-1 if d == 0 else 1)
            go(ring_chunk(first, d, s), rb.at[d, 0, s], r_send.at[d, 0, s], r_recv.at[d, 0, s], ring_to(d))
    for d in (1, 3, 2):
        go(
            p_ref.at[1, :, :, :, :, quarter(ypeer(d))], yb.at[d - 1],
            y_send.at[d - 1], y_recv.at[d - 1], at(xh, z, core, ypeer(d), xl),
        )
    for i, (a, b) in enumerate(XPEERS):
        go(
            p_ref.at[2, flip(xh, a), :, flip(xl, b)], xb.at[i], x_send.at[i], x_recv.at[i],
            at(flip(xh, a), z, core, y, flip(xl, b)),
        )
    sibling = at(xh, z, other, y, xl)
    go(attn_ref.at[other], arx_ref, c_send.at[0], c_recv.at[0], sibling)
    go(gx_ref.at[other], grx_ref, c_send.at[1], c_recv.at[1], sibling)

    def first_sums():
        for d in range(3):
            came(yb.at[d], y_send.at[d], y_recv.at[d])

        def add_k(i, carry):
            a, b = i // 8, lax.rem(i, 8)
            total = p_ref[1, a, b, :, :, quarter(y)] + yb[0, a, b]
            ks[a, b] = total + yb[1, a, b] + yb[2, a, b]
            return carry

        lax.fori_loop(0, 16, add_k, 0)
        for i, (a, b) in enumerate(XPEERS):
            go(
                ks.at[flip(xh, a), :, flip(xl, b)], xb2.at[i], x2_send.at[i], x2_recv.at[i],
                at(flip(xh, a), z, core, y, flip(xl, b)),
            )
        for i in range(3):
            came(xb.at[i], x_send.at[i], x_recv.at[i])

        def add_v(i, carry):
            vs[i] = p_ref[2, xh, i, xl] + xb[0, i] + xb[1, i] + xb[2, i]
            return carry

        lax.fori_loop(0, 8, add_v, 0)
        for d in (1, 3, 2):
            go(
                vs.at[:, :, quarter(ypeer(d))], yb2.at[d - 1], y2_send.at[d - 1], y2_recv.at[d - 1],
                at(xh, z, core, ypeer(d), xl),
            )

    for k in range(1, 8):
        for s in range(2):
            for d in range(2):
                came(rb.at[d, k - 1, s], r_send.at[d, k - 1, s], r_recv.at[d, k - 1, s])
                dest = zpeer(-1 - k if d == 0 else k + 1 - 8)
                cols = pl.ds(256 * d, 256)
                if k < 7:
                    rb[d, k - 1, s] = rb[d, k - 1, s] + p_ref[0, s, dest, :, :, cols]
                    go(
                        rb.at[d, k - 1, s], rb.at[d, k, s],
                        r_send.at[d, k, s], r_recv.at[d, k, s], ring_to(d),
                    )
                else:
                    qs[s, :, :, 256 * d : 256 * d + 256] = (
                        rb[d, k - 1, s] + p_ref[0, s, z, :, :, cols]
                    )
        if k == 5:
            first_sums()
    for i, (a, b) in enumerate(XPEERS):
        go(
            qs.at[flip(xh, a), flip(xl, b)], qxb.at[i], qx_send.at[i], qx_recv.at[i],
            at(flip(xh, a), z, core, y, flip(xl, b)),
        )
    for i in range(3):
        came(xb2.at[i], x2_send.at[i], x2_recv.at[i])
        came(yb2.at[i], y2_send.at[i], y2_recv.at[i])
    for i in range(8):
        kv[i, 0] = ks[xh, i, xl] + xb2[0, i] + xb2[1, i] + xb2[2, i]
        kv[i, 1] = vs[i, :, quarter(y)] + yb2[0, i] + yb2[1, i] + yb2[2, i]
    for d in (4, 3, 5, 2, 6, 1, 7):
        go(
            kv.at[zpeer(d)], zb.at[d - 1], z_send.at[d - 1], z_recv.at[d - 1],
            at(xh, zpeer(d), core, y, xl),
        )
    for i in range(3):
        came(qxb.at[i], qx_send.at[i], qx_recv.at[i])
    qx[...] = qs[xh, xl] + qxb[0] + qxb[1] + qxb[2]
    for d in (2, 1, 3):
        go(
            qx.at[:, quarter(ypeer(d))], qyb.at[d - 1], qy_send.at[d - 1], qy_recv.at[d - 1],
            at(xh, z, core, ypeer(d), xl),
        )
    for d in range(7):
        came(zb.at[d], z_send.at[d], z_recv.at[d])
    total = kv[z]
    for d in range(7):
        total = total + zb[d]
    fin[pl.ds(1, 2)] = total
    for d in range(3):
        came(qyb.at[d], qy_send.at[d], qy_recv.at[d])
    fin[0] = qx[:, quarter(y)] + qyb[0] + qyb[1] + qyb[2]

    for d in (2, 1, 3):
        for b in (0, 1):
            go(
                fin, gw_ref.at[core, y], f_send.at[d, b], f_recv.at[core, y],
                at(xh, z, xl, ypeer(d), flip(xl, b)),
            )
    go(fin, gw_ref.at[core, y], f_send.at[0, 1], f_recv.at[core, y], at(xh, z, xl, y, 1 - xl))
    last = remote(fin, gw_ref.at[core, y], f_send.at[0, 0], f_recv.at[core, y], at(xh, z, xl, y, xl))
    keep = pltpu.make_async_copy(fin, gw_ref.at[core, y], f_local)

    @pl.when(core == xl)
    def _():
        keep.start()
        keep.wait()

    @pl.when(core != xl)
    def _():
        last.start()
        last.wait_send()

    for c in range(2):
        for d in range(4):
            if (c, d) == (0, 0):
                @pl.when(core != xl)
                def _():
                    came(gw_ref.at[core, y], f_send.at[0, 0], f_recv.at[core, y])
            else:
                cc = flip(core, c)
                came(gw_ref.at[cc, ypeer(d)], f_send.at[0, 0], f_recv.at[cc, ypeer(d)])
    came(arx_ref, c_send.at[0], c_recv.at[0])
    came(grx_ref, c_send.at[1], c_recv.at[1])
    for cp in sends:
        cp.wait_send()


def reduce_all(partial, attn, gx):
    dma = pltpu.SemaphoreType.DMA
    vmem = lambda *shape: pltpu.VMEM(shape, F32)
    shape = jax.ShapeDtypeStruct
    return pl.pallas_call(
        reduce_kernel,
        out_shape=(
            shape((128, 512), BF16), shape((128, 1024), F32), shape((2, 4, 3, 32, 128), F32)
        ),
        in_specs=[VM] * 3,
        out_specs=(ANY,) * 3,
        scratch_shapes=[
            vmem(3, 2, 8, 2, 32, 128), vmem(3, 8, 32, 512), vmem(2, 7, 2, 2, 32, 256),
            vmem(2, 8, 2, 32, 128), vmem(8, 32, 512), vmem(2, 2, 32, 512),
            vmem(3, 8, 32, 128), vmem(3, 8, 32, 128), vmem(3, 32, 512), vmem(32, 512),
            vmem(3, 32, 128), vmem(8, 2, 32, 128), vmem(7, 2, 32, 128), vmem(3, 32, 128),
            dma((2,)), dma((2,)), dma((3,)), dma((3,)), dma((3,)), dma((3,)),
            dma((2, 7, 2)), dma((2, 7, 2)),
            dma((3,)), dma((3,)), dma((3,)), dma((3,)), dma((3,)), dma((3,)), dma((3,)), dma((3,)),
            dma((7,)), dma((7,)), dma((4, 2)), dma((2, 4)), dma,
        ],
        compiler_params=pltpu.CompilerParams(
            collective_id=2, has_side_effects=True, vmem_limit_bytes=VMEM_LIMIT
        ),
        name="reduce_all",
    )(partial, attn, gx)


def local(image_tokens, qkv_weight, block_list, block_count, out_grad):
    core = lax.axis_index("wide") % 2
    slots = block_list[0]
    live = jnp.arange(2, dtype=jnp.int32) < block_count[0, 0]
    on = jnp.any((slots[:, None] == jnp.arange(2, dtype=jnp.int32)[None]) & live[:, None], axis=0)
    on = on.astype(F32)
    act = jnp.broadcast_to(on[None, :, None, None], (8, 2, 8, 128)).reshape(128, 128)
    xr, gr, wg, acts = gather_all(
        image_tokens.reshape(8, 2, 8, 1024), out_grad.reshape(8, 2, 8, 1024), qkv_weight, act
    )
    wg = wg.reshape(3, 1024, 512)
    attn, dq, ld, qr, grs, kown, vown, xown = query_side(xr, gr, wg, acts)
    ldr = halo(ld)
    gx, partial = key_side(qr, grs, kown, vown, ldr, dq, xown, wg)
    arx, grx, gw = reduce_all(partial.reshape(3, 2, 8, 2, 32, 512), attn, gx)
    mine = lax.dynamic_index_in_dim(attn, core, 0, keepdims=False)
    attn_out = jnp.where(
        core == 0, jnp.concatenate([mine, arx], axis=-1), jnp.concatenate([arx, mine], axis=-1)
    )
    grad_x = (lax.dynamic_index_in_dim(gx, core, 0, keepdims=False) + grx).astype(BF16)
    factor = 1.0 / math.sqrt(32768.0)
    grad_w = jnp.transpose(gw, (3, 2, 0, 1, 4)).reshape(32, 3072) * factor
    return attn_out.reshape(8, 16, 1024), grad_x.reshape(8, 16, 1024), grad_w


def solution(mesh):
    placed = (
        P("narrow", "wide", None),
        P("wide", None),
        P("narrow", "wide"),
        P("narrow", "wide"),
        P("narrow", "wide", None),
    )
    return jax.shard_map(
        local,
        mesh=mesh,
        in_specs=placed,
        out_specs=(P("narrow", "wide", None), P("narrow", "wide", None), P("wide", None)),
        check_vma=False,
    )
```

```python
import functools
import math

import jax
import jax.numpy as jnp
from jax import lax
from jax.experimental import pallas as pl
from jax.experimental.pallas import tpu as pltpu
from jax.sharding import PartitionSpec as P

MESH = pl.DeviceIdType.MESH
F32 = jnp.float32
BF16 = jnp.bfloat16
RADIUS = 6
NEGATIVE = -1e30
HUGE = 1e30
SCALE = 0.125
VMEM_LIMIT = 60 * 1024 * 1024
ANY = pl.BlockSpec(memory_space=pl.ANY)
VM = pl.BlockSpec(memory_space=pltpu.VMEM)

ROWS = {-1: (0, 6, 14), 0: (0, 8, 6), 1: (2, 6, 0)}


def place():
    wide = lax.axis_index("wide")
    narrow = lax.axis_index("narrow")
    return narrow, wide // 2, wide % 2


def device(narrow, chip, core):
    return {"wide": lax.rem(chip, 16) * 2 + core, "narrow": lax.rem(narrow, 8)}


def remote(src, dst, send, recv, to):
    return pltpu.make_async_remote_copy(
        src_ref=src, dst_ref=dst, send_sem=send, recv_sem=recv, device_id=to, device_id_type=MESH
    )


def greet(devices):
    barrier = pltpu.get_barrier_semaphore()
    for to in devices:
        pl.semaphore_signal(barrier, inc=1, device_id=to, device_id_type=MESH)
    pl.semaphore_wait(barrier, len(devices))


def half_of(core):
    return pl.ds(pl.multiple_of(core * 512, 512), 512)


def gather_kernel(
    x_ref, g_ref, w_ref, act_ref, xr_ref, gr_ref, wg_ref, acts_ref,
    h_send, h_recv, h_local, s_send, s_recv, a_send, a_recv, a_local,
    w_send, w_recv, w_local, p_send, p_recv, r_send, r_recv,
):
    n, chip, core = place()
    other = 1 - core
    z = lax.rem(chip, 8)
    xh = chip // 8
    step = 2 * core - 1
    side_chip = chip + step + 16
    up = device(n, xh * 8 + lax.rem(z + 1, 8), core)
    down = device(n, xh * 8 + lax.rem(z + 7, 8), core)
    partner = device(n + 1 - 2 * lax.rem(n, 2), (1 - xh) * 8 + z, core)
    sibling = device(n, chip, other)

    peers = [up, down, partner, sibling]
    for dn in (-1, 0, 1):
        for dc in (-1, 0, 1):
            for c in (0, 1):
                if (dn, dc) != (0, 0):
                    peers.append(device(n + dn + 8, chip + dc + 16, c))
    greet(peers)

    sends = []
    own = []
    for t in range(3):
        here = wg_ref.at[t, xh, z, core]
        cp = pltpu.make_async_copy(
            w_ref.at[:, pl.ds(pl.multiple_of(t * 1024 + core * 512, 512), 512)], here, w_local.at[t]
        )
        cp.start()
        own.append(cp)
        cp = remote(
            w_ref.at[:, pl.ds(pl.multiple_of(t * 1024 + other * 512, 512), 512)],
            here, w_send.at[t], w_recv.at[t], sibling,
        )
        cp.start()
        sends.append(cp)

    for t in range(3):
        own[t].wait()
        remote(
            w_ref.at[:, pl.ds(0, 512)], wg_ref.at[t, xh, z, other],
            w_send.at[t], w_recv.at[t], sibling,
        ).wait_recv()
    hops = {(0, 0): 4, (0, 1): 3, (1, 0): 3, (1, 1): 4}

    def slab(s, index):
        return wg_ref.at[:, xh if s == 0 else 1 - xh, lax.rem(index + 16, 8)]

    def forward(s, d, k):
        moved = slab(s, z - k if d == 0 else z + k)
        cp = remote(
            moved, moved, r_send.at[s, d, k], r_recv.at[s, d, k], up if d == 0 else down
        )
        cp.start()
        sends.append(cp)

    def arrived(s, d, k):
        landed = slab(s, z - 1 - k if d == 0 else z + 1 + k)
        remote(landed, landed, r_send.at[s, d, k], r_recv.at[s, d, k], up).wait_recv()

    mine = slab(0, z)
    cp = remote(mine, mine, p_send, p_recv, partner)
    cp.start()
    sends.append(cp)
    forward(0, 0, 0)
    forward(0, 1, 0)
    tensors = ((g_ref, lambda c: gr_ref), (x_ref, lambda c: xr_ref.at[c]))
    locals_ = []
    for i, (src, dst) in enumerate(tensors):
        for dn in (-1, 0, 1):
            lo, count, at = ROWS[dn]
            for side in (0, 1):
                for rel in (0, 1):
                    c = core if rel == 0 else other
                    if side == 0:
                        source = src.at[pl.ds(lo, count), :, :, half_of(c)]
                        target = dst(c).at[pl.ds(at, count), pl.ds(1 + 2 * core, 2)]
                        slot = core
                        to = device(n + dn + 8, chip, c)
                    else:
                        source = src.at[pl.ds(lo, count), pl.ds(core, 1), :, half_of(c)]
                        target = dst(c).at[pl.ds(at, count), pl.ds(5 * other, 1)]
                        slot = 3 - core
                        to = device(n + dn + 8, side_chip, c)
                    if dn == 0 and side == 0 and rel == 0:
                        cp = pltpu.make_async_copy(source, target, h_local.at[i])
                        locals_.append(cp)
                    else:
                        cp = remote(
                            source, target, h_send.at[i, dn + 1, side, rel],
                            h_recv.at[i, dn + 1, slot], to,
                        )
                        sends.append(cp)
                    cp.start()

    act_copy = pltpu.make_async_copy(act_ref, acts_ref.at[core], a_local)
    act_copy.start()
    act_send = remote(act_ref, acts_ref.at[core], a_send, a_recv, sibling)
    act_send.start()
    sends.append(act_send)

    theirs = slab(1, z)
    remote(theirs, theirs, p_send, p_recv, partner).wait_recv()
    forward(1, 0, 0)
    forward(1, 1, 0)

    def finish_region(i, dst):
        locals_[i].wait()
        for dn in (-1, 0, 1):
            lo, count, at = ROWS[dn]
            for piece in range(4):
                if piece < 2:
                    if dn == 0 and piece == 1:
                        continue
                    slot = other if dn == 0 else piece
                    landed = dst.at[pl.ds(at, count), pl.ds(1 + 2 * slot, 2)]
                else:
                    slot = piece
                    landed = dst.at[pl.ds(at, count), pl.ds(0 if piece == 2 else 5, 1)]
                remote(
                    landed, landed, h_send.at[i, dn + 1, 0, 0], h_recv.at[i, dn + 1, slot], sibling
                ).wait_recv()

    for k in range(1, 5):
        for s in range(2):
            for d in range(2):
                if k <= hops[s, d]:
                    arrived(s, d, k - 1)
                if k < hops[s, d]:
                    forward(s, d, k)
        if k == 2:
            finish_region(1, xr_ref.at[core])
            cp = remote(xr_ref.at[core], xr_ref.at[core], s_send, s_recv, sibling)
            cp.start()
            sends.append(cp)
    finish_region(0, gr_ref)
    act_copy.wait()
    remote(act_ref, acts_ref.at[other], a_send, a_recv, sibling).wait_recv()
    remote(xr_ref.at[other], xr_ref.at[other], s_send, s_recv, sibling).wait_recv()
    for cp in sends:
        cp.wait_send()


def gather_all(x4, g4, weight, act):
    dma = pltpu.SemaphoreType.DMA
    return pl.pallas_call(
        gather_kernel,
        out_shape=(
            jax.ShapeDtypeStruct((2, 20, 6, 8, 512), BF16),
            jax.ShapeDtypeStruct((20, 6, 8, 512), BF16),
            jax.ShapeDtypeStruct((3, 2, 8, 2, 32, 512), BF16),
            jax.ShapeDtypeStruct((2, 128, 128), F32),
        ),
        in_specs=[VM] * 4,
        out_specs=(ANY,) * 4,
        scratch_shapes=[
            dma((2, 3, 2, 2)), dma((2, 3, 4)), dma((2,)), dma, dma, dma, dma, dma,
            dma((3,)), dma((3,)), dma((3,)), dma, dma, dma((2, 2, 4)), dma((2, 2, 4)),
        ],
        compiler_params=pltpu.CompilerParams(collective_id=0, has_side_effects=True),
        name="gather_all",
    )(x4, g4, weight, act)


def window_bias(hf):
    n, chip, _ = place()
    shape = (128, 640)
    inner = lax.broadcasted_iota(jnp.int32, shape, 0)
    outer = lax.broadcasted_iota(jnp.int32, shape, 1)
    row, col = outer // 32, outer % 32
    down = row - RADIUS - inner // 16
    across = col - 8 - inner % 16
    grid_row = n * 8 - RADIUS + row
    grid_col = chip * 32 - 8 + 16 * hf + col
    ok = (jnp.abs(down) <= RADIUS) & (jnp.abs(across) <= RADIUS)
    ok = ok & (grid_row >= 0) & (grid_row < 64) & (grid_col >= 0) & (grid_col < 512)
    return jnp.where(ok, 0.0, NEGATIVE)


def nt(a, b):
    return lax.dot_general(a, b, (((1,), (1,)), ((), ())), preferred_element_type=F32)


def nn(a, b):
    return jnp.dot(a, b, preferred_element_type=F32)


def tn(a, b):
    return lax.dot_general(a, b, (((0,), (0,)), ((), ())), preferred_element_type=F32)


def lanes_of(hp):
    return pl.ds(pl.multiple_of(hp * 128, 128), 128)


def head_masks():
    lane = lax.broadcasted_iota(jnp.int32, (128, 128), 1)
    low = lane < 64
    return low, (low.astype(F32).astype(BF16), (1.0 - low.astype(F32)).astype(BF16)), lane


def query_kernel(
    xr_ref, gr_ref, wg_ref, acts_ref,
    attn_ref, dq_ref, ld_ref, qr_ref, grs_ref, kown_ref, vown_ref, xt_ref,
    acc, kr, vr, qown, gown, ldacc, ldall, bias,
):
    def own_of(values, hf):
        return values[6:14, 1 + 2 * hf : 3 + 2 * hf].reshape(128, 512)

    for t, region in enumerate((qr_ref, kr, vr)):

        def chunk(i, carry, t=t, region=region):
            rows = pl.ds(pl.multiple_of(i * 192, 192), 192)
            out = nn(xr_ref[0, pl.ds(4 * i, 4)].reshape(192, 512), wg_ref[t, :512])
            out += nn(xr_ref[1, pl.ds(4 * i, 4)].reshape(192, 512), wg_ref[t, 512:])
            acc[pl.ds(4 * i, 4)] = out.reshape(4, 6, 8, 512)
            region[pl.ds(4 * i, 4)] = out.astype(BF16).reshape(4, 48, 512)
            return carry

        lax.fori_loop(0, 5, chunk, 0)
        for hf in range(2):
            own = acc[6:14, 1 + 2 * hf : 3 + 2 * hf].reshape(128, 512).astype(BF16)
            if t == 0:
                qown[hf] = own * SCALE
            elif t == 1:
                kown_ref[hf] = own * SCALE
            else:
                vown_ref[hf] = own

    def regroup(i, carry):
        rows = gr_ref[pl.ds(4 * i, 4)].astype(F32).reshape(192, 512)
        grs_ref[pl.ds(4 * i, 4)] = rows.astype(BF16).reshape(4, 48, 512)
        return carry

    lax.fori_loop(0, 5, regroup, 0)
    for hf in range(2):
        groups = pl.ds(1 + 2 * hf, 2)
        gown[hf] = gr_ref[6:14, groups].astype(F32).reshape(128, 512).astype(BF16)
        for c in range(2):
            tokens = xr_ref[c, 6:14, groups].astype(F32).reshape(128, 512)
            for i in range(4):
                xt_ref[512 * c + 128 * i : 512 * c + 128 * i + 128, 128 * hf : 128 * hf + 128] = (
                    tokens[:, 128 * i : 128 * i + 128].T.astype(BF16)
                )
        bias[...] = window_bias(hf)
        ldacc[...] = jnp.zeros_like(ldacc)

        def pair(hp, carry, hf=hf):
            lanes = lanes_of(hp)
            low, masks, lane = head_masks()
            keys = kr[:, 16 * hf : 16 * hf + 32, lanes].reshape(640, 128)
            values = vr[:, 16 * hf : 16 * hf + 32, lanes].reshape(640, 128)
            query = qown[hf, :, lanes]
            grad = gown[hf, :, lanes]
            active = acts_ref[hf]
            outs, dqs = [], []
            ld = ldacc[...]
            for j in range(2):
                s = nt(query * masks[j], keys) + bias[...]
                top = jnp.max(s, axis=1, keepdims=True)
                e = jnp.exp(s - top)
                total = jnp.sum(e, axis=1, keepdims=True)
                p = e * (1.0 / total)
                lse = top + jnp.log(total)
                out = nn(p.astype(BF16), values)
                out = out.astype(BF16).astype(F32)
                gm = grad * masks[j]
                delta = jnp.sum(gm.astype(F32) * out, axis=1, keepdims=True)
                dp = nt(gm, values)
                ds = (p * (dp - delta) * SCALE).astype(BF16)
                dqs.append(nn(ds, keys))
                outs.append(out)
                on = active > 0.0
                head = 2 * hp + j
                ld = jnp.where(lane == head, jnp.where(on, lse, HUGE), ld)
                ld = jnp.where(lane == head + 8, jnp.where(on, delta, 0.0), ld)
            ldacc[...] = ld
            attn_ref[hf, :, lanes] = (jnp.where(low, outs[0], outs[1]) * active).astype(BF16)
            dq_ref[hf, :, lanes] = (jnp.where(low, dqs[0], dqs[1]) * active).astype(BF16)
            return carry

        lax.fori_loop(0, 4, pair, 0)
        ldall[:, 16 * hf : 16 * hf + 16, :] = ldacc[...].reshape(8, 16, 128)
    for i in range(2):
        ld_ref[:, 128 * i : 128 * i + 128] = ldall[4 * i : 4 * i + 4].reshape(128, 128).T[:16]


def query_side(xr, gr, wg, acts):
    shape = jax.ShapeDtypeStruct
    return pl.pallas_call(
        query_kernel,
        out_shape=(
            shape((2, 128, 512), BF16), shape((2, 128, 512), BF16), shape((16, 256), F32),
            shape((20, 48, 512), BF16), shape((20, 48, 512), BF16),
            shape((2, 128, 512), BF16), shape((2, 128, 512), BF16), shape((1024, 256), BF16),
        ),
        in_specs=[VM] * 4,
        out_specs=(VM,) * 8,
        scratch_shapes=[
            pltpu.VMEM((20, 6, 8, 512), F32), pltpu.VMEM((20, 48, 512), BF16),
            pltpu.VMEM((20, 48, 512), BF16), pltpu.VMEM((2, 128, 512), BF16),
            pltpu.VMEM((2, 128, 512), BF16), pltpu.VMEM((128, 128), F32),
            pltpu.VMEM((8, 32, 128), F32), pltpu.VMEM((128, 640), F32),
        ],
        compiler_params=pltpu.CompilerParams(vmem_limit_bytes=VMEM_LIMIT),
        name="query_side",
    )(xr, gr, wg, acts)


XPEERS = ((0, 1), (1, 0), (1, 1))
NEAR = tuple((dn, dc) for dn in (-1, 0, 1) for dc in (-1, 0, 1) if (dn, dc) != (0, 0))
FIRST = ["x", "y", "z", "z"] + ["y", "x"] * 4
SLOT = [FIRST[:b].count(FIRST[b]) for b in range(12)]
LATE = [b for b in range(12) if FIRST[b] != "z"]
BATCHES = (LATE[:6], LATE[6:])


def block_of(t, hp):
    return hp if t == 0 else 4 + 2 * hp + (t - 1)


def back_kernel(
    qr_ref, gr_ref, kown_ref, vown_ref, ld_ref, dq_ref, xt_ref, wg_ref, attn_ref,
    attn_out, gx_out, gw_out,
    p, sx, sy, sz, rx, ry, rz, rx2, ry2, mz, rzx, rzy, cz, rc, fin,
    dk, dv, lds, ldb, bias, gx, gxr, gxo, wv,
    ld_send, ld_recv, w_sem, o_sem, a_send, a_recv, g_send, g_recv,
    x_send, x_recv, y_send, y_recv, z_send, z_recv,
    x2_send, x2_recv, y2_send, y2_recv, zx_send, zx_recv, zy_send, zy_recv,
    c_send, c_recv, f_send, f_recv, f_local,
):
    n, chip, core = place()
    other = 1 - core
    z = lax.rem(chip, 8)
    xh = chip // 8
    y = n // 2
    xl = lax.rem(n, 2)

    def at(xh_, z_, core_, y_, xl_):
        return device(y_ * 2 + xl_, xh_ * 8 + z_, core_)

    def ypeer(d):
        return lax.rem(y + d, 4)

    def zpeer(d):
        return lax.rem(z + d + 8, 8)

    def flip(value, by):
        return 1 - value if by else value

    sibling = at(xh, z, other, y, xl)
    peers = [device(n + dn + 8, chip + dc + 16, core) for dn, dc in NEAR]
    peers += [at(xh, zpeer(d), core, y, xl) for d in range(1, 8)]
    peers += [at(1 - xh, z, core, y, flip(xl, b)) for b in (0, 1)]
    for c in (0, 1):
        for d in range(4):
            for b in (0, 1):
                if (c, d, b) != (0, 0, 0):
                    peers.append(at(xh, z, flip(core, c), ypeer(d), flip(xl, b)))
    greet(peers)

    sends = []

    def go(src, dst, send, recv, to):
        cp = remote(src, dst, send, recv, to)
        cp.start()
        sends.append(cp)

    def came(dst, send, recv):
        remote(dst, dst, send, recv, sibling).wait_recv()

    def xpeer(i):
        a, b = XPEERS[i]
        return flip(xh, a), flip(xl, b), at(flip(xh, a), z, core, y, flip(xl, b))

    for dn, dc in NEAR:
        go(
            ld_ref, ldb.at[1 - dn, 1 - dc], ld_send.at[dn + 1, dc + 1], ld_recv.at[1 - dn, 1 - dc],
            device(n + dn + 8, chip + dc + 16, core),
        )
    weights = pltpu.make_async_copy(wg_ref, wv, w_sem)
    weights.start()

    def first(b):
        i = SLOT[b]
        if FIRST[b] == "x":
            for d in (2, 0, 1):
                a, l, to = xpeer(d)
                go(p.at[b, a, :, l], rx.at[i, d], x_send.at[i, d], x_recv.at[i, d], to)
        elif FIRST[b] == "y":
            for d in (2, 1, 3):
                to = at(xh, z, core, ypeer(d), xl)
                go(
                    p.at[b, :, :, :, ypeer(d)], ry.at[i, d - 1],
                    y_send.at[i, d - 1], y_recv.at[i, d - 1], to,
                )
        else:
            for d in (4, 3, 5, 2, 6, 1, 7):
                to = at(xh, zpeer(d), core, y, xl)
                go(
                    p.at[b, :, zpeer(d)], rz.at[i, d - 1],
                    z_send.at[i, d - 1], z_recv.at[i, d - 1], to,
                )

    def second(b):
        i = SLOT[b]
        if FIRST[b] == "x":
            for d in range(3):
                came(rx.at[i, d], x_send.at[i, d], x_recv.at[i, d])

            def add_x(j, carry):
                sx[i, j] = p[b, xh, j, xl] + rx[i, 0, j] + rx[i, 1, j] + rx[i, 2, j]
                return carry

            lax.fori_loop(0, 8, add_x, 0)
            for d in (2, 1, 3):
                go(
                    sx.at[i, :, ypeer(d)], ry2.at[i, d - 1], y2_send.at[i, d - 1],
                    y2_recv.at[i, d - 1], at(xh, z, core, ypeer(d), xl),
                )
        elif FIRST[b] == "y":
            for d in range(3):
                came(ry.at[i, d], y_send.at[i, d], y_recv.at[i, d])

            def add_y(j, carry):
                for a in range(2):
                    total = p[b, a, j, :, y] + ry[i, 0, a, j]
                    sy[i, a, j] = total + ry[i, 1, a, j] + ry[i, 2, a, j]
                return carry

            lax.fori_loop(0, 8, add_y, 0)
            for d in (2, 0, 1):
                a, l, to = xpeer(d)
                go(sy.at[i, a, :, l], rx2.at[i, d], x2_send.at[i, d], x2_recv.at[i, d], to)
        else:
            for d in range(7):
                came(rz.at[i, d], z_send.at[i, d], z_recv.at[i, d])
            for a in range(2):
                for l in range(2):
                    total = p[b, a, z, l]
                    for d in range(7):
                        total = total + rz[i, d, a, l]
                    sz[i, a, l] = total
            for d in (2, 0, 1):
                a, l, to = xpeer(d)
                go(sz.at[i, a, l], rzx.at[i, d], zx_send.at[i, d], zx_recv.at[i, d], to)

    def third(b):
        i = SLOT[b]
        if FIRST[b] == "x":
            for d in range(3):
                came(ry2.at[i, d], y2_send.at[i, d], y2_recv.at[i, d])
            for j in range(8):
                cz[j, LATE.index(b)] = sx[i, j, y] + ry2[i, 0, j] + ry2[i, 1, j] + ry2[i, 2, j]
        elif FIRST[b] == "y":
            for d in range(3):
                came(rx2.at[i, d], x2_send.at[i, d], x2_recv.at[i, d])
            for j in range(8):
                cz[j, LATE.index(b)] = sy[i, xh, j, xl] + rx2[i, 0, j] + rx2[i, 1, j] + rx2[i, 2, j]
        else:
            for d in range(3):
                came(rzx.at[i, d], zx_send.at[i, d], zx_recv.at[i, d])
            mz[i] = sz[i, xh, xl] + rzx[i, 0] + rzx[i, 1] + rzx[i, 2]
            for d in (2, 1, 3):
                go(
                    mz.at[i, ypeer(d)], rzy.at[i, d - 1], zy_send.at[i, d - 1],
                    zy_recv.at[i, d - 1], at(xh, z, core, ypeer(d), xl),
                )

    def spread(h):
        lo, count = LATE.index(BATCHES[h][0]), len(BATCHES[h])
        for d in (4, 3, 5, 2, 6, 1, 7):
            go(
                cz.at[zpeer(d), pl.ds(lo, count)], rc.at[d - 1, pl.ds(lo, count)],
                c_send.at[h, d - 1], c_recv.at[h, d - 1], at(xh, zpeer(d), core, y, xl),
            )

    factor = 1.0 / math.sqrt(32768.0)

    def keep(b, total):
        t, hp = (0, b) if b < 4 else ((b - 4) % 2 + 1, (b - 4) // 2)
        fin[t, :, 128 * hp : 128 * hp + 128] = total * factor

    def last(h):
        lo, count = LATE.index(BATCHES[h][0]), len(BATCHES[h])
        for d in range(7):
            landed = rc.at[d, pl.ds(lo, count)]
            came(landed, c_send.at[h, d], c_recv.at[h, d])
        for b in BATCHES[h]:
            i = LATE.index(b)
            total = cz[z, i]
            for d in range(7):
                total = total + rc[d, i]
            keep(b, total)

    def last_z(b):
        i = SLOT[b]
        for d in range(3):
            came(rzy.at[i, d], zy_send.at[i, d], zy_recv.at[i, d])
        keep(b, mz[i, y] + rzy[i, 0] + rzy[i, 1] + rzy[i, 2])

    def product(blocks, columns):
        def rows(i, carry):
            out = nn(xt_ref[pl.ds(pl.multiple_of(i * 256, 256), 256), :], columns)
            out = out.reshape(4, 2, 4, 8, 128 * len(blocks))
            for j, b in enumerate(blocks):
                p[b, i // 2, pl.ds(4 * lax.rem(i, 2), 4)] = out[..., 128 * j : 128 * j + 128]
            return carry

        lax.fori_loop(0, 4, rows, 0)

    dq = dq_ref[...].reshape(256, 512)
    for half in range(2):
        product((2 * half, 2 * half + 1), dq[:, 256 * half : 256 * half + 256])
        first(2 * half)
        first(2 * half + 1)
    go(attn_ref.at[other], attn_out.at[:, half_of(core)], a_send, a_recv, sibling)
    attn_own = pltpu.make_async_copy(attn_ref.at[core], attn_out.at[:, half_of(core)], o_sem.at[0])
    attn_own.start()

    for hf in range(2):
        bias[hf] = window_bias(hf)
    ldb[1, 1] = ld_ref[...]
    for dn, dc in NEAR:
        came(ldb.at[1 - dn, 1 - dc], ld_send.at[dn + 1, dc + 1], ld_recv.at[1 - dn, 1 - dc])
    column = lax.rem(lax.broadcasted_iota(jnp.int32, (16, 256), 1), 32)
    for hf in range(2):
        parts = []
        for r in range(3):
            left, mid, right = ldb[r, 0], ldb[r, 1], ldb[r, 2]
            if hf == 0:
                part = jnp.where(column < 8, pltpu.roll(left, 232, 1), pltpu.roll(mid, 8, 1))
            else:
                part = jnp.where(column < 24, pltpu.roll(mid, 248, 1), pltpu.roll(right, 24, 1))
            parts.append(part)
        lds[hf] = pltpu.roll(jnp.concatenate(parts, axis=1), 768 - 64, 1)[:, :640]

    low, masks, _ = head_masks()
    for hp in range(4):
        lanes = slice(128 * hp, 128 * hp + 128)

        def side(hf, carry, hp=hp, lanes=lanes):
            window = pl.ds(pl.multiple_of(16 * hf, 16), 32)
            query = qr_ref[:, window, lanes].reshape(640, 128)
            grad = gr_ref[:, window, lanes].reshape(640, 128)
            keys = kown_ref[hf, :, lanes]
            values = vown_ref[hf, :, lanes]
            dks, dvs = [], []
            for j in range(2):
                head = 2 * hp + j
                s = nt(keys * masks[j], query) + bias[hf]
                e = jnp.exp(s - lds[hf, head : head + 1, :])
                dvs.append(nn(e.astype(BF16), grad))
                dp = nt(values * masks[j], grad)
                ds = (e * (dp - lds[hf, head + 8 : head + 9, :]) * SCALE).astype(BF16)
                dks.append(nn(ds, query))
            dk[hp, hf] = jnp.where(low, dks[0], dks[1]).astype(BF16)
            dv[hp, hf] = jnp.where(low, dvs[0], dvs[1]).astype(BF16)
            return carry

        lax.fori_loop(0, 2, side, 0)
        both = jnp.concatenate([dk[hp].reshape(256, 128), dv[hp].reshape(256, 128)], axis=1)
        blocks = (block_of(1, hp), block_of(2, hp))
        product(blocks, both)
        first(blocks[0])
        first(blocks[1])
        if hp == 1:
            second(0)
            second(1)
        if hp == 2:
            second(block_of(1, 0))
            second(block_of(2, 0))
            second(2)
            second(3)
            third(0)
            third(1)

    weights.wait()

    def gradients(t):
        source = dk if t == 1 else dv
        return jnp.concatenate([source[h].reshape(256, 128) for h in range(4)], axis=1)

    all_k, all_v = gradients(1), gradients(2)

    def input_columns(i, carry):
        rows = pl.ds(pl.multiple_of(i * 256, 256), 256)
        total = nt(dq, wv[0, rows]) + nt(all_k, wv[1, rows]) + nt(all_v, wv[2, rows])
        gx[:, :, rows] = total.reshape(2, 128, 256)
        return carry

    lax.fori_loop(0, 4, input_columns, 0)
    go(gx.at[other], gxr, g_send, g_recv, sibling)

    second(block_of(1, 1))
    second(block_of(2, 1))
    third(block_of(1, 0))
    third(block_of(2, 0))
    third(2)
    third(3)
    third(block_of(1, 1))
    third(block_of(2, 1))
    spread(0)
    came(gxr, g_send, g_recv)
    gxo[...] = (gx[core] + gxr[...]).astype(BF16)
    gx_own = pltpu.make_async_copy(gxo, gx_out, o_sem.at[1])
    gx_own.start()
    second(block_of(1, 2))
    second(block_of(2, 2))
    second(block_of(1, 3))
    second(block_of(2, 3))
    last_z(2)
    last_z(3)
    third(block_of(1, 2))
    third(block_of(2, 2))
    last(0)
    third(block_of(1, 3))
    third(block_of(2, 3))
    spread(1)
    last(1)

    mine = pl.ds(pl.multiple_of(8 * y, 8), 8)

    def columns(t, c):
        return pl.ds(pl.multiple_of(t * 1024 + c * 512, 512), 512)

    for t in range(3):
        spot = gw_out.at[mine, columns(t, core)]
        for d in (2, 1, 3):
            for b in (0, 1):
                go(
                    fin.at[t], spot, f_send.at[d, b, t], f_recv.at[core, y, t],
                    at(xh, z, xl, ypeer(d), flip(xl, b)),
                )
        go(fin.at[t], spot, f_send.at[0, 1, t], f_recv.at[core, y, t], at(xh, z, xl, y, 1 - xl))
        away = remote(
            fin.at[t], spot, f_send.at[0, 0, t], f_recv.at[core, y, t], at(xh, z, xl, y, xl)
        )
        here = pltpu.make_async_copy(fin.at[t], spot, f_local.at[t])

        @pl.when(core == xl)
        def _():
            here.start()
            here.wait()

        @pl.when(core != xl)
        def _():
            away.start()
            away.wait_send()

    attn_own.wait()
    gx_own.wait()
    came(attn_out.at[:, half_of(other)], a_send, a_recv)
    for t in range(3):
        for c in range(2):
            for d in range(4):
                cc, yy = flip(core, c), ypeer(d)
                spot = gw_out.at[pl.ds(pl.multiple_of(8 * yy, 8), 8), columns(t, cc)]
                if (c, d) == (0, 0):

                    @pl.when(core != xl)
                    def _():
                        came(spot, f_send.at[0, 0, t], f_recv.at[cc, yy, t])
                else:
                    came(spot, f_send.at[0, 0, t], f_recv.at[cc, yy, t])
    for cp in sends:
        cp.wait_send()


def back(qr, gr, kown, vown, ld, dq, xt, wg, attn):
    dma = pltpu.SemaphoreType.DMA
    vmem = lambda *shape: pltpu.VMEM(shape, F32)
    shape = jax.ShapeDtypeStruct
    nx, ny, nz, nl = FIRST.count("x"), FIRST.count("y"), FIRST.count("z"), len(LATE)
    return pl.pallas_call(
        back_kernel,
        out_shape=(
            shape((128, 1024), BF16), shape((128, 1024), BF16), shape((32, 3072), F32),
        ),
        in_specs=[VM] * 7 + [ANY, VM],
        out_specs=(ANY,) * 3,
        scratch_shapes=[
            vmem(12, 2, 8, 2, 4, 8, 128),
            vmem(nx, 8, 4, 8, 128), vmem(ny, 2, 8, 2, 8, 128), vmem(nz, 2, 2, 4, 8, 128),
            vmem(nx, 3, 8, 4, 8, 128), vmem(ny, 3, 2, 8, 2, 8, 128), vmem(nz, 7, 2, 2, 4, 8, 128),
            vmem(ny, 3, 8, 8, 128), vmem(nx, 3, 8, 8, 128),
            vmem(nz, 4, 8, 128), vmem(nz, 3, 4, 8, 128), vmem(nz, 3, 8, 128),
            vmem(8, nl, 8, 128), vmem(7, nl, 8, 128), vmem(3, 8, 512),
            pltpu.VMEM((4, 2, 128, 128), BF16), pltpu.VMEM((4, 2, 128, 128), BF16),
            vmem(2, 16, 640), vmem(3, 3, 16, 256), vmem(2, 128, 640),
            vmem(2, 128, 1024), vmem(128, 1024), pltpu.VMEM((128, 1024), BF16),
            pltpu.VMEM((3, 1024, 512), BF16),
            dma((3, 3)), dma((3, 3)), dma, dma((2,)), dma, dma, dma, dma,
            dma((nx, 3)), dma((nx, 3)), dma((ny, 3)), dma((ny, 3)), dma((nz, 7)), dma((nz, 7)),
            dma((ny, 3)), dma((ny, 3)), dma((nx, 3)), dma((nx, 3)),
            dma((nz, 3)), dma((nz, 3)), dma((nz, 3)), dma((nz, 3)),
            dma((2, 7)), dma((2, 7)), dma((4, 2, 3)), dma((2, 4, 3)), dma((3,)),
        ],
        compiler_params=pltpu.CompilerParams(
            collective_id=2, has_side_effects=True, vmem_limit_bytes=VMEM_LIMIT
        ),
        name="back",
    )(qr, gr, kown, vown, ld, dq, xt, wg, attn)


def local(image_tokens, qkv_weight, block_list, block_count, out_grad):
    slots = block_list[0]
    live = jnp.arange(2, dtype=jnp.int32) < block_count[0, 0]
    on = jnp.any((slots[:, None] == jnp.arange(2, dtype=jnp.int32)[None]) & live[:, None], axis=0)
    on = on.astype(F32)
    act = jnp.broadcast_to(on[None, :, None, None], (8, 2, 8, 128)).reshape(128, 128)
    xr, gr, wg, acts = gather_all(
        image_tokens.reshape(8, 2, 8, 1024), out_grad.reshape(8, 2, 8, 1024), qkv_weight, act
    )
    wg = wg.reshape(3, 1024, 512)
    attn, dq, ld, qr, grs, kown, vown, xt = query_side(xr, gr, wg, acts)
    attn_out, grad_x, grad_w = back(qr, grs, kown, vown, ld, dq, xt, wg, attn)
    return attn_out.reshape(8, 16, 1024), grad_x.reshape(8, 16, 1024), grad_w


def solution(mesh):
    placed = (
        P("narrow", "wide", None),
        P("wide", None),
        P("narrow", "wide"),
        P("narrow", "wide"),
        P("narrow", "wide", None),
    )
    return jax.shard_map(
        local,
        mesh=mesh,
        in_specs=placed,
        out_specs=(P("narrow", "wide", None), P("narrow", "wide", None), P("wide", None)),
        check_vma=False,
    )
```

```python
import functools
import math

import jax
import jax.numpy as jnp
from jax import lax
from jax.experimental import pallas as pl
from jax.experimental.pallas import tpu as pltpu
from jax.sharding import PartitionSpec as P

MESH = pl.DeviceIdType.MESH
F32 = jnp.float32
BF16 = jnp.bfloat16
RADIUS = 6
NEGATIVE = -1e30
HUGE = 1e30
SCALE = 0.125
VMEM_LIMIT = 60 * 1024 * 1024
ANY = pl.BlockSpec(memory_space=pl.ANY)
VM = pl.BlockSpec(memory_space=pltpu.VMEM)

ROWS = {-1: (0, 6, 14), 0: (0, 8, 6), 1: (2, 6, 0)}


def place():
    wide = lax.axis_index("wide")
    narrow = lax.axis_index("narrow")
    return narrow, wide // 2, wide % 2


def device(narrow, chip, core):
    return {"wide": lax.rem(chip, 16) * 2 + core, "narrow": lax.rem(narrow, 8)}


def remote(src, dst, send, recv, to):
    return pltpu.make_async_remote_copy(
        src_ref=src, dst_ref=dst, send_sem=send, recv_sem=recv, device_id=to, device_id_type=MESH
    )


def greet(devices):
    barrier = pltpu.get_barrier_semaphore()
    for to in devices:
        pl.semaphore_signal(barrier, inc=1, device_id=to, device_id_type=MESH)
    pl.semaphore_wait(barrier, len(devices))


def half_of(core):
    return pl.ds(pl.multiple_of(core * 512, 512), 512)


def gather_kernel(
    x_ref, g_ref, w_ref, act_ref, xr_ref, gr_ref, wg_ref, acts_ref, xall_ref,
    h_send, h_recv, h_local, s_send, s_recv, a_send, a_recv, a_local,
    w_send, w_recv, w_local, p_send, p_recv, r_send, r_recv, e_send, e_recv,
):
    n, chip, core = place()
    other = 1 - core
    z = lax.rem(chip, 8)
    xh = chip // 8
    step = 2 * core - 1
    side_chip = chip + step + 16
    up = device(n, xh * 8 + lax.rem(z + 1, 8), core)
    down = device(n, xh * 8 + lax.rem(z + 7, 8), core)
    partner = device(n + 1 - 2 * lax.rem(n, 2), (1 - xh) * 8 + z, core)
    sibling = device(n, chip, other)

    peers = [up, down, partner, sibling]
    for dn in (-1, 0, 1):
        for dc in (-1, 0, 1):
            for c in (0, 1):
                if (dn, dc) != (0, 0):
                    peers.append(device(n + dn + 8, chip + dc + 16, c))
    for d in (1, 2, 3):
        for c in (0, 1):
            peers.append(device(n + 2 * d, chip, c))
    greet(peers)

    sends = []
    own = []
    for t in range(3):
        here = wg_ref.at[t, xh, z, core]
        cp = pltpu.make_async_copy(
            w_ref.at[:, pl.ds(pl.multiple_of(t * 1024 + core * 512, 512), 512)], here, w_local.at[t]
        )
        cp.start()
        own.append(cp)
        cp = remote(
            w_ref.at[:, pl.ds(pl.multiple_of(t * 1024 + other * 512, 512), 512)],
            here, w_send.at[t], w_recv.at[t], sibling,
        )
        cp.start()
        sends.append(cp)

    for t in range(3):
        own[t].wait()
        remote(
            w_ref.at[:, pl.ds(0, 512)], wg_ref.at[t, xh, z, other],
            w_send.at[t], w_recv.at[t], sibling,
        ).wait_recv()
    hops = {(0, 0): 4, (0, 1): 3, (1, 0): 3, (1, 1): 4}

    def slab(t, s, index):
        return wg_ref.at[t, xh if s == 0 else 1 - xh, lax.rem(index + 16, 8)]

    def forward(s, d, k, t):
        moved = slab(t, s, z - k if d == 0 else z + k)
        cp = remote(
            moved, moved, r_send.at[s, d, k, t], r_recv.at[s, d, k, t], up if d == 0 else down
        )
        cp.start()
        sends.append(cp)

    def arrived(s, d, k, t):
        landed = slab(t, s, z - 1 - k if d == 0 else z + 1 + k)
        remote(landed, landed, r_send.at[s, d, k, t], r_recv.at[s, d, k, t], up).wait_recv()

    for t in range(3):
        mine = slab(t, 0, z)
        cp = remote(mine, mine, p_send.at[t], p_recv.at[t], partner)
        cp.start()
        sends.append(cp)
        forward(0, 0, 0, t)
        forward(0, 1, 0, t)
    tensors = ((g_ref, lambda c: gr_ref), (x_ref, lambda c: xr_ref.at[c]))
    locals_ = []
    for i, (src, dst) in enumerate(tensors):
        for dn in (-1, 0, 1):
            lo, count, at = ROWS[dn]
            for side in (0, 1):
                for rel in (0, 1):
                    c = core if rel == 0 else other
                    if side == 0:
                        source = src.at[pl.ds(lo, count), :, :, half_of(c)]
                        target = dst(c).at[pl.ds(at, count), pl.ds(1 + 2 * core, 2)]
                        slot = core
                        to = device(n + dn + 8, chip, c)
                    else:
                        source = src.at[pl.ds(lo, count), pl.ds(core, 1), :, half_of(c)]
                        target = dst(c).at[pl.ds(at, count), pl.ds(5 * other, 1)]
                        slot = 3 - core
                        to = device(n + dn + 8, side_chip, c)
                    if dn == 0 and side == 0 and rel == 0:
                        cp = pltpu.make_async_copy(source, target, h_local.at[i])
                        locals_.append(cp)
                    else:
                        cp = remote(
                            source, target, h_send.at[i, dn + 1, side, rel],
                            h_recv.at[i, dn + 1, slot], to,
                        )
                        sends.append(cp)
                    cp.start()

    act_copy = pltpu.make_async_copy(act_ref, acts_ref.at[core], a_local)
    act_copy.start()
    act_send = remote(act_ref, acts_ref.at[core], a_send, a_recv, sibling)
    act_send.start()
    sends.append(act_send)

    for t in range(3):
        theirs = slab(t, 1, z)
        remote(theirs, theirs, p_send.at[t], p_recv.at[t], partner).wait_recv()
        forward(1, 0, 0, t)
        forward(1, 1, 0, t)

    for d in (2, 1, 3):
        want = lax.rem(n // 2 + d, 4) // 2
        for rel in (0, 1):
            cp = remote(
                x_ref.at[:, :, :, half_of(want)], xall_ref.at[3 - d, core],
                e_send.at[d - 1, rel], e_recv.at[3 - d, core],
                device(n + 2 * d, chip, core if rel == 0 else other),
            )
            cp.start()
            sends.append(cp)

    def finish_region(i, dst):
        locals_[i].wait()
        for dn in (-1, 0, 1):
            lo, count, at = ROWS[dn]
            for piece in range(4):
                if piece < 2:
                    if dn == 0 and piece == 1:
                        continue
                    slot = other if dn == 0 else piece
                    landed = dst.at[pl.ds(at, count), pl.ds(1 + 2 * slot, 2)]
                else:
                    slot = piece
                    landed = dst.at[pl.ds(at, count), pl.ds(0 if piece == 2 else 5, 1)]
                remote(
                    landed, landed, h_send.at[i, dn + 1, 0, 0], h_recv.at[i, dn + 1, slot], sibling
                ).wait_recv()

    for k in range(1, 5):
        for s in range(2):
            for t in range(3):
                for d in range(2):
                    if k <= hops[s, d]:
                        arrived(s, d, k - 1, t)
                    if k < hops[s, d]:
                        forward(s, d, k, t)
        if k == 2:
            finish_region(1, xr_ref.at[core])
            cp = remote(xr_ref.at[core], xr_ref.at[core], s_send, s_recv, sibling)
            cp.start()
            sends.append(cp)
    finish_region(0, gr_ref)
    act_copy.wait()
    remote(act_ref, acts_ref.at[other], a_send, a_recv, sibling).wait_recv()
    remote(xr_ref.at[other], xr_ref.at[other], s_send, s_recv, sibling).wait_recv()
    for r in range(3):
        for c in range(2):
            landed = xall_ref.at[r, c]
            remote(landed, landed, e_send.at[r, c], e_recv.at[r, c], sibling).wait_recv()
    for cp in sends:
        cp.wait_send()


def gather_all(x4, g4, weight, act):
    dma = pltpu.SemaphoreType.DMA
    return pl.pallas_call(
        gather_kernel,
        out_shape=(
            jax.ShapeDtypeStruct((2, 20, 6, 8, 512), BF16),
            jax.ShapeDtypeStruct((20, 6, 8, 512), BF16),
            jax.ShapeDtypeStruct((3, 2, 8, 2, 32, 512), BF16),
            jax.ShapeDtypeStruct((2, 128, 128), F32),
            jax.ShapeDtypeStruct((3, 2, 8, 2, 8, 512), BF16),
        ),
        in_specs=[VM] * 4,
        out_specs=(ANY,) * 5,
        scratch_shapes=[
            dma((2, 3, 2, 2)), dma((2, 3, 4)), dma((2,)), dma, dma, dma, dma, dma,
            dma((3,)), dma((3,)), dma((3,)), dma((3,)), dma((3,)),
            dma((2, 2, 4, 3)), dma((2, 2, 4, 3)), dma((3, 2)), dma((3, 2)),
        ],
        compiler_params=pltpu.CompilerParams(collective_id=0, has_side_effects=True),
        name="gather_all",
    )(x4, g4, weight, act)


def window_bias(hf):
    n, chip, _ = place()
    shape = (128, 640)
    inner = lax.broadcasted_iota(jnp.int32, shape, 0)
    outer = lax.broadcasted_iota(jnp.int32, shape, 1)
    row, col = outer // 32, outer % 32
    down = row - RADIUS - inner // 16
    across = col - 8 - inner % 16
    grid_row = n * 8 - RADIUS + row
    grid_col = chip * 32 - 8 + 16 * hf + col
    ok = (jnp.abs(down) <= RADIUS) & (jnp.abs(across) <= RADIUS)
    ok = ok & (grid_row >= 0) & (grid_row < 64) & (grid_col >= 0) & (grid_col < 512)
    return jnp.where(ok, 0.0, NEGATIVE)


def nt(a, b):
    return lax.dot_general(a, b, (((1,), (1,)), ((), ())), preferred_element_type=F32)


def nn(a, b):
    return jnp.dot(a, b, preferred_element_type=F32)


def tn(a, b):
    return lax.dot_general(a, b, (((0,), (0,)), ((), ())), preferred_element_type=F32)


def lanes_of(hp):
    return pl.ds(pl.multiple_of(hp * 128, 128), 128)


def head_masks():
    lane = lax.broadcasted_iota(jnp.int32, (128, 128), 1)
    low = lane < 64
    return low, (low.astype(F32).astype(BF16), (1.0 - low.astype(F32)).astype(BF16)), lane


def query_kernel(
    xr_ref, gr_ref, wg_ref, acts_ref, xall_ref,
    attn_ref, dq_ref, ld_ref, qr_ref, grs_ref, kown_ref, vown_ref, xt_ref,
    acc, kr, vr, qown, gown, ldacc, ldall, bias,
):
    row_half = lax.axis_index("narrow") // 4

    for t, region in enumerate((qr_ref, kr, vr)):

        def chunk(i, carry, t=t, region=region):
            out = nn(xr_ref[0, pl.ds(4 * i, 4)].reshape(192, 512), wg_ref[t, :512])
            out += nn(xr_ref[1, pl.ds(4 * i, 4)].reshape(192, 512), wg_ref[t, 512:])
            acc[pl.ds(4 * i, 4)] = out.reshape(4, 6, 8, 512)
            region[pl.ds(4 * i, 4)] = out.astype(BF16).reshape(4, 48, 512)
            return carry

        lax.fori_loop(0, 5, chunk, 0)
        for hf in range(2):
            own = acc[6:14, 1 + 2 * hf : 3 + 2 * hf].reshape(128, 512).astype(BF16)
            if t == 0:
                qown[hf] = own * SCALE
            elif t == 1:
                kown_ref[hf] = own * SCALE
            else:
                vown_ref[hf] = own

    def regroup(i, carry):
        rows = gr_ref[pl.ds(4 * i, 4)].astype(F32).reshape(192, 512)
        grs_ref[pl.ds(4 * i, 4)] = rows.astype(BF16).reshape(4, 48, 512)
        return carry

    lax.fori_loop(0, 5, regroup, 0)
    for hf in range(2):
        groups = pl.ds(1 + 2 * hf, 2)
        gown[hf] = gr_ref[6:14, groups].astype(F32).reshape(128, 512).astype(BF16)
        for r in range(4):
            if r == 0:
                tokens = xr_ref[row_half, 6:14, groups]
            else:
                tokens = xall_ref[r - 1, hf]
            tokens = tokens.astype(F32).reshape(128, 512)
            at = 256 * r + 128 * hf
            for i in range(4):
                xt_ref[128 * i : 128 * i + 128, at : at + 128] = (
                    tokens[:, 128 * i : 128 * i + 128].T.astype(BF16)
                )
        bias[...] = window_bias(hf)
        ldacc[...] = jnp.zeros_like(ldacc)

        def pair(hp, carry, hf=hf):
            lanes = lanes_of(hp)
            low, masks, lane = head_masks()
            keys = kr[:, 16 * hf : 16 * hf + 32, lanes].reshape(640, 128)
            values = vr[:, 16 * hf : 16 * hf + 32, lanes].reshape(640, 128)
            query = qown[hf, :, lanes]
            grad = gown[hf, :, lanes]
            active = acts_ref[hf]
            outs, dqs = [], []
            ld = ldacc[...]
            for j in range(2):
                s = nt(query * masks[j], keys) + bias[...]
                top = jnp.max(s, axis=1, keepdims=True)
                e = jnp.exp(s - top)
                total = jnp.sum(e, axis=1, keepdims=True)
                p = e * (1.0 / total)
                lse = top + jnp.log(total)
                out = nn(p.astype(BF16), values)
                out = out.astype(BF16).astype(F32)
                gm = grad * masks[j]
                delta = jnp.sum(gm.astype(F32) * out, axis=1, keepdims=True)
                dp = nt(gm, values)
                ds = (p * (dp - delta) * SCALE).astype(BF16)
                dqs.append(nn(ds, keys))
                outs.append(out)
                on = active > 0.0
                head = 2 * hp + j
                ld = jnp.where(lane == head, jnp.where(on, lse, HUGE), ld)
                ld = jnp.where(lane == head + 8, jnp.where(on, delta, 0.0), ld)
            ldacc[...] = ld
            attn_ref[hf, :, lanes] = (jnp.where(low, outs[0], outs[1]) * active).astype(BF16)
            dq_ref[hp, hf] = (jnp.where(low, dqs[0], dqs[1]) * active).astype(BF16)
            return carry

        lax.fori_loop(0, 4, pair, 0)
        ldall[:, 16 * hf : 16 * hf + 16, :] = ldacc[...].reshape(8, 16, 128)
    for i in range(2):
        ld_ref[:, 128 * i : 128 * i + 128] = ldall[4 * i : 4 * i + 4].reshape(128, 128).T[:16]


def query_side(xr, gr, wg, acts, xall):
    shape = jax.ShapeDtypeStruct
    return pl.pallas_call(
        query_kernel,
        out_shape=(
            shape((2, 128, 512), BF16), shape((4, 2, 128, 128), BF16), shape((16, 256), F32),
            shape((20, 48, 512), BF16), shape((20, 48, 512), BF16),
            shape((2, 128, 512), BF16), shape((2, 128, 512), BF16), shape((512, 1024), BF16),
        ),
        in_specs=[VM] * 5,
        out_specs=(VM,) * 8,
        scratch_shapes=[
            pltpu.VMEM((20, 6, 8, 512), F32), pltpu.VMEM((20, 48, 512), BF16),
            pltpu.VMEM((20, 48, 512), BF16), pltpu.VMEM((2, 128, 512), BF16),
            pltpu.VMEM((2, 128, 512), BF16), pltpu.VMEM((128, 128), F32),
            pltpu.VMEM((8, 32, 128), F32), pltpu.VMEM((128, 640), F32),
        ],
        compiler_params=pltpu.CompilerParams(vmem_limit_bytes=VMEM_LIMIT),
        name="query_side",
    )(xr, gr, wg, acts, xall)


XPEERS = ((0, 1), (1, 0), (1, 1))
NEAR = tuple((dn, dc) for dn in (-1, 0, 1) for dc in (-1, 0, 1) if (dn, dc) != (0, 0))


def back_kernel(
    qr_ref, gr_ref, kown_ref, vown_ref, ld_ref, dq_ref, xt_ref, wg_ref, attn_ref,
    attn_out, gx_out, gw_out,
    gall, p, rx, cz, rc, fin_q, fin_kv, kv, lds, ldb, bias, gx, gxr, gxo, wv,
    ld_send, ld_recv, w_sem, o_sem, a_send, a_recv, g_send, g_recv,
    q_send, q_recv, k_send, k_recv, x_send, x_recv, c_send, c_recv, f_send, f_recv, f_local,
):
    n, chip, core = place()
    other = 1 - core
    z = lax.rem(chip, 8)
    xh = chip // 8
    y = n // 2
    xl = lax.rem(n, 2)
    row_half = y // 2
    col_half = lax.rem(y, 2)

    def at(xh_, z_, core_, y_, xl_):
        return device(y_ * 2 + xl_, xh_ * 8 + z_, core_)

    def ypeer(d):
        return lax.rem(y + d, 4)

    def zpeer(d):
        return lax.rem(z + d + 8, 8)

    def flip(value, by):
        return 1 - value if by else value

    sibling = at(xh, z, other, y, xl)
    peers = [device(n + dn + 8, chip + dc + 16, core) for dn, dc in NEAR]
    peers += [at(xh, zpeer(d), core, y, xl) for d in range(1, 8)]
    for a in (0, 1):
        for c in (0, 1):
            for d in range(4):
                for b in (0, 1):
                    if (a, c, d, b) != (0, 0, 0, 0):
                        peers.append(at(flip(xh, a), z, flip(core, c), ypeer(d), flip(xl, b)))
    greet(peers)

    sends = []

    def go(src, dst, send, recv, to):
        cp = remote(src, dst, send, recv, to)
        cp.start()
        sends.append(cp)

    def came(dst, send, recv):
        remote(dst, dst, send, recv, sibling).wait_recv()

    for dn, dc in NEAR:
        go(
            ld_ref, ldb.at[1 - dn, 1 - dc], ld_send.at[dn + 1, dc + 1], ld_recv.at[1 - dn, 1 - dc],
            device(n + dn + 8, chip + dc + 16, core),
        )
    for d in (2, 1, 3):
        go(
            dq_ref.at[pl.ds(2 * lax.rem(ypeer(d), 2), 2)], gall.at[4 - d, pl.ds(0, 2)],
            q_send.at[d - 1], q_recv.at[3 - d], at(xh, z, core, ypeer(d), xl),
        )
    weights = pltpu.make_async_copy(wg_ref, wv, w_sem)
    weights.start()
    go(attn_ref.at[other], attn_out.at[:, half_of(core)], a_send, a_recv, sibling)
    attn_own = pltpu.make_async_copy(attn_ref.at[core], attn_out.at[:, half_of(core)], o_sem.at[0])
    attn_own.start()

    def share(hp):
        for d in (2, 1, 3):
            go(
                kv.at[hp, lax.rem(ypeer(d), 2)], gall.at[4 - d, 2 + hp],
                k_send.at[hp, d - 1], k_recv.at[hp, 3 - d], at(xh, z, core, ypeer(d), xl),
            )

    def product(first, count):
        if count == 2:
            columns = jnp.concatenate(
                [gall[:, first + j].reshape(1024, 128) for j in range(count)], axis=1
            )
        else:
            columns = gall[:, first].reshape(1024, 128)

        def rows(i, carry):
            out = nn(xt_ref[pl.ds(pl.multiple_of(i * 128, 128), 128), :], columns)
            out = out.reshape(2, 2, 2, 2, 8, 128 * count)
            for j in range(count):
                p[first + j, pl.ds(2 * i, 2)] = out[..., 128 * j : 128 * j + 128]
            return carry

        lax.fori_loop(0, 4, rows, 0)
        for b in range(first, first + count):
            for i in (2, 0, 1):
                a, l = flip(xh, XPEERS[i][0]), flip(xl, XPEERS[i][1])
                go(
                    p.at[b, :, l, a], rx.at[b, i], x_send.at[b, i], x_recv.at[b, i],
                    at(a, z, core, y, l),
                )

    def product_q():
        for r in range(3):
            came(gall.at[r + 1, pl.ds(0, 2)], q_send.at[r], q_recv.at[r])
        for j in range(2):
            gall[0, j] = dq_ref[2 * col_half + j]
        product(0, 2)

    def product_kv(hp):
        for r in range(3):
            came(gall.at[r + 1, 2 + hp], k_send.at[hp, r], k_recv.at[hp, r])
        gall[0, 2 + hp] = kv[hp, col_half]
        product(2 + hp, 1)

    def sum_x(b):
        for i in range(3):
            came(rx.at[b, i], x_send.at[b, i], x_recv.at[b, i])
        for j in range(8):
            cz[j, b] = p[b, j, xl, xh] + rx[b, 0, j] + rx[b, 1, j] + rx[b, 2, j]

    batches = ((0, 4), (4, 2))

    def spread(h):
        lo, count = batches[h]
        for d in (4, 3, 5, 2, 6, 1, 7):
            go(
                cz.at[zpeer(d), pl.ds(lo, count)], rc.at[d - 1, pl.ds(lo, count)],
                c_send.at[h, d - 1], c_recv.at[h, d - 1], at(xh, zpeer(d), core, y, xl),
            )

    factor = 1.0 / math.sqrt(32768.0)

    def sum_z(h):
        lo, count = batches[h]
        for d in range(7):
            came(rc.at[d, pl.ds(lo, count)], c_send.at[h, d], c_recv.at[h, d])
        for b in range(lo, lo + count):
            total = cz[z, b]
            for d in range(7):
                total = total + rc[d, b]
            total = total.reshape(16, 128) * factor
            if b < 2:
                fin_q[:, 128 * b : 128 * b + 128] = total
            else:
                fin_kv[:, 128 * (b - 2) : 128 * (b - 1)] = total

    for hf in range(2):
        bias[hf] = window_bias(hf)
    ldb[1, 1] = ld_ref[...]
    for dn, dc in NEAR:
        came(ldb.at[1 - dn, 1 - dc], ld_send.at[dn + 1, dc + 1], ld_recv.at[1 - dn, 1 - dc])
    column = lax.rem(lax.broadcasted_iota(jnp.int32, (16, 256), 1), 32)
    for hf in range(2):
        parts = []
        for r in range(3):
            left, mid, right = ldb[r, 0], ldb[r, 1], ldb[r, 2]
            if hf == 0:
                part = jnp.where(column < 8, pltpu.roll(left, 232, 1), pltpu.roll(mid, 8, 1))
            else:
                part = jnp.where(column < 24, pltpu.roll(mid, 248, 1), pltpu.roll(right, 24, 1))
            parts.append(part)
        lds[hf] = pltpu.roll(jnp.concatenate(parts, axis=1), 768 - 64, 1)[:, :640]

    low, masks, _ = head_masks()

    def key_side(hp):
        lanes = slice(128 * hp, 128 * hp + 128)

        def side(hf, carry):
            window = pl.ds(pl.multiple_of(16 * hf, 16), 32)
            query = qr_ref[:, window, lanes].reshape(640, 128)
            grad = gr_ref[:, window, lanes].reshape(640, 128)
            keys = kown_ref[hf, :, lanes]
            values = vown_ref[hf, :, lanes]
            dks, dvs = [], []
            for j in range(2):
                head = 2 * hp + j
                s = nt(keys * masks[j], query) + bias[hf]
                e = jnp.exp(s - lds[hf, head : head + 1, :])
                dvs.append(nn(e.astype(BF16), grad))
                dp = nt(values * masks[j], grad)
                ds = (e * (dp - lds[hf, head + 8 : head + 9, :]) * SCALE).astype(BF16)
                dks.append(nn(ds, query))
            kv[hp, 0, hf] = jnp.where(low, dks[0], dks[1]).astype(BF16)
            kv[hp, 1, hf] = jnp.where(low, dvs[0], dvs[1]).astype(BF16)
            return carry

        lax.fori_loop(0, 2, side, 0)
        share(hp)

    key_side(0)
    product_q()
    key_side(1)
    product_kv(0)
    key_side(2)
    product_kv(1)
    sum_x(0)
    sum_x(1)
    key_side(3)
    product_kv(2)
    sum_x(2)
    sum_x(3)
    spread(0)

    weights.wait()
    all_q = jnp.concatenate([dq_ref[h].reshape(256, 128) for h in range(4)], axis=1)
    all_k = jnp.concatenate([kv[h, 0].reshape(256, 128) for h in range(4)], axis=1)
    all_v = jnp.concatenate([kv[h, 1].reshape(256, 128) for h in range(4)], axis=1)

    def input_columns(i, carry):
        rows = pl.ds(pl.multiple_of(i * 256, 256), 256)
        total = nt(all_q, wv[0, rows]) + nt(all_k, wv[1, rows]) + nt(all_v, wv[2, rows])
        gx[:, :, rows] = total.reshape(2, 128, 256)
        return carry

    product_kv(3)
    lax.fori_loop(0, 4, input_columns, 0)
    go(gx.at[other], gxr, g_send, g_recv, sibling)
    sum_x(4)
    sum_x(5)
    spread(1)
    came(gxr, g_send, g_recv)
    gxo[...] = (gx[core] + gxr[...]).astype(BF16)
    gx_own = pltpu.make_async_copy(gxo, gx_out, o_sem.at[1])
    gx_own.start()
    sum_z(0)
    sum_z(1)

    def spots(c, part, a):
        rows = pl.ds(pl.multiple_of(16 * a, 16), 16)
        q_at = pl.multiple_of(c * 512 + part * 256, 256)
        kv_at = pl.multiple_of((1 + part) * 1024 + c * 512, 512)
        return gw_out.at[rows, pl.ds(q_at, 256)], gw_out.at[rows, pl.ds(kv_at, 512)]

    mine = spots(core, col_half, xh)
    for i, fin in enumerate((fin_q, fin_kv)):
        recv = f_recv.at[i, core, col_half, xh]
        for d in (2, 1, 3):
            for b in (0, 1):
                go(fin, mine[i], f_send.at[i, d, b], recv, at(row_half, z, xl, ypeer(d), flip(xl, b)))
        go(fin, mine[i], f_send.at[i, 0, 1], recv, at(row_half, z, xl, y, 1 - xl))
        away = remote(fin, mine[i], f_send.at[i, 0, 0], recv, at(row_half, z, xl, y, xl))
        here = pltpu.make_async_copy(fin, mine[i], f_local.at[i])
        is_here = (core == xl) & (row_half == xh)

        @pl.when(is_here)
        def _():
            here.start()
            here.wait()

        @pl.when(jnp.logical_not(is_here))
        def _():
            away.start()
            away.wait_send()

    attn_own.wait()
    gx_own.wait()
    came(attn_out.at[:, half_of(other)], a_send, a_recv)
    for c in range(2):
        for part in range(2):
            for a in range(2):
                landed = spots(c, part, a)
                own = (
                    (c == core) & (part == col_half) & (a == xh) & (row_half == xh) & (xl == core)
                )
                for i in range(2):

                    @pl.when(jnp.logical_not(own))
                    def _():
                        came(landed[i], f_send.at[i, 0, 0], f_recv.at[i, c, part, a])

    for cp in sends:
        cp.wait_send()


def back(qr, gr, kown, vown, ld, dq, xt, wg, attn):
    dma = pltpu.SemaphoreType.DMA
    vmem = lambda *shape: pltpu.VMEM(shape, F32)
    half = lambda *shape: pltpu.VMEM(shape, BF16)
    shape = jax.ShapeDtypeStruct
    return pl.pallas_call(
        back_kernel,
        out_shape=(
            shape((128, 1024), BF16), shape((128, 1024), BF16), shape((32, 3072), F32),
        ),
        in_specs=[VM] * 7 + [ANY, VM],
        out_specs=(ANY,) * 3,
        scratch_shapes=[
            half(4, 6, 2, 128, 128), vmem(6, 8, 2, 2, 2, 8, 128), vmem(6, 3, 8, 2, 8, 128),
            vmem(8, 6, 2, 8, 128), vmem(7, 6, 2, 8, 128), vmem(16, 256), vmem(16, 512),
            half(4, 2, 2, 128, 128), vmem(2, 16, 640), vmem(3, 3, 16, 256), vmem(2, 128, 640),
            vmem(2, 128, 1024), vmem(128, 1024), half(128, 1024), half(3, 1024, 512),
            dma((3, 3)), dma((3, 3)), dma, dma((2,)), dma, dma, dma, dma,
            dma((3,)), dma((3,)), dma((4, 3)), dma((4, 3)), dma((6, 3)), dma((6, 3)),
            dma((2, 7)), dma((2, 7)), dma((2, 4, 2)), dma((2, 2, 2, 2)), dma((2,)),
        ],
        compiler_params=pltpu.CompilerParams(
            collective_id=2, has_side_effects=True, vmem_limit_bytes=VMEM_LIMIT
        ),
        name="back",
    )(qr, gr, kown, vown, ld, dq, xt, wg, attn)


def local(image_tokens, qkv_weight, block_list, block_count, out_grad):
    slots = block_list[0]
    live = jnp.arange(2, dtype=jnp.int32) < block_count[0, 0]
    on = jnp.any((slots[:, None] == jnp.arange(2, dtype=jnp.int32)[None]) & live[:, None], axis=0)
    on = on.astype(F32)
    act = jnp.broadcast_to(on[None, :, None, None], (8, 2, 8, 128)).reshape(128, 128)
    xr, gr, wg, acts, xall = gather_all(
        image_tokens.reshape(8, 2, 8, 1024), out_grad.reshape(8, 2, 8, 1024), qkv_weight, act
    )
    wg = wg.reshape(3, 1024, 512)
    attn, dq, ld, qr, grs, kown, vown, xt = query_side(xr, gr, wg, acts, xall)
    attn_out, grad_x, grad_w = back(qr, grs, kown, vown, ld, dq, xt, wg, attn)
    return attn_out.reshape(8, 16, 1024), grad_x.reshape(8, 16, 1024), grad_w


def solution(mesh):
    placed = (
        P("narrow", "wide", None),
        P("wide", None),
        P("narrow", "wide"),
        P("narrow", "wide"),
        P("narrow", "wide", None),
    )
    return jax.shard_map(
        local,
        mesh=mesh,
        in_specs=placed,
        out_specs=(P("narrow", "wide", None), P("narrow", "wide", None), P("wide", None)),
        check_vma=False,
    )
```

```python
import functools
import math

import jax
import jax.numpy as jnp
from jax import lax
from jax.experimental import pallas as pl
from jax.experimental.pallas import tpu as pltpu
from jax.sharding import PartitionSpec as P

MESH = pl.DeviceIdType.MESH
F32 = jnp.float32
BF16 = jnp.bfloat16
RADIUS = 6
NEGATIVE = -1e30
HUGE = 1e30
SCALE = 0.125
VMEM_LIMIT = 60 * 1024 * 1024
ANY = pl.BlockSpec(memory_space=pl.ANY)
VM = pl.BlockSpec(memory_space=pltpu.VMEM)

ROWS = {-1: (0, 6, 14), 0: (0, 8, 6), 1: (2, 6, 0)}


def place():
    wide = lax.axis_index("wide")
    narrow = lax.axis_index("narrow")
    return narrow, wide // 2, wide % 2


def device(narrow, chip, core):
    return {"wide": lax.rem(chip, 16) * 2 + core, "narrow": lax.rem(narrow, 8)}


def remote(src, dst, send, recv, to):
    return pltpu.make_async_remote_copy(
        src_ref=src, dst_ref=dst, send_sem=send, recv_sem=recv, device_id=to, device_id_type=MESH
    )


def greet(devices):
    barrier = pltpu.get_barrier_semaphore()
    for to in devices:
        pl.semaphore_signal(barrier, inc=1, device_id=to, device_id_type=MESH)
    pl.semaphore_wait(barrier, len(devices))


def half_of(core):
    return pl.ds(pl.multiple_of(core * 512, 512), 512)


def window_bias(hf):
    n, chip, _ = place()
    shape = (128, 640)
    inner = lax.broadcasted_iota(jnp.int32, shape, 0)
    outer = lax.broadcasted_iota(jnp.int32, shape, 1)
    row, col = outer // 32, outer % 32
    down = row - RADIUS - inner // 16
    across = col - 8 - inner % 16
    grid_row = n * 8 - RADIUS + row
    grid_col = chip * 32 - 8 + 16 * hf + col
    ok = (jnp.abs(down) <= RADIUS) & (jnp.abs(across) <= RADIUS)
    ok = ok & (grid_row >= 0) & (grid_row < 64) & (grid_col >= 0) & (grid_col < 512)
    return jnp.where(ok, 0.0, NEGATIVE)


def nt(a, b):
    return lax.dot_general(a, b, (((1,), (1,)), ((), ())), preferred_element_type=F32)


def nn(a, b):
    return jnp.dot(a, b, preferred_element_type=F32)


def tn(a, b):
    return lax.dot_general(a, b, (((0,), (0,)), ((), ())), preferred_element_type=F32)


def lanes_of(hp):
    return pl.ds(pl.multiple_of(hp * 128, 128), 128)


def head_masks():
    lane = lax.broadcasted_iota(jnp.int32, (128, 128), 1)
    low = lane < 64
    return low, (low.astype(F32).astype(BF16), (1.0 - low.astype(F32)).astype(BF16)), lane


XPEERS = ((0, 1), (1, 0), (1, 1))
NEAR = tuple((dn, dc) for dn in (-1, 0, 1) for dc in (-1, 0, 1) if (dn, dc) != (0, 0))


def layer_kernel(
    x_ref, g_ref, w_ref, list_ref, count_ref,
    attn_out, gx_out, gw_out,
    xr_ref, gr_ref, wg_ref, xall_ref, acts,
    acc, qr_ref, kr, vr, grs_ref, qown, kown_ref, vown_ref, gown, ldacc, ldall, ld_ref,
    dq_ref, attn_ref, xt_ref,
    gall, p, rx, cz, rc, fin_q, fin_kv, kv, lds, ldb, bias, gx, gxr, gxo,
    h_send, h_recv, h_local, s_send, s_recv, act_send, act_recv,
    w_send, w_recv, w_local, p_send, p_recv, r_send, r_recv, e_send, e_recv,
    ld_send, ld_recv, o_sem, a_send, a_recv, g_send, g_recv,
    q_send, q_recv, k_send, k_recv, x_send, x_recv, c_send, c_recv, f_send, f_recv, f_local,
):
    n, chip, core = place()
    other = 1 - core
    z = lax.rem(chip, 8)
    xh = chip // 8
    y = n // 2
    xl = lax.rem(n, 2)
    row_half = y // 2
    col_half = lax.rem(y, 2)

    def at(xh_, z_, core_, y_, xl_):
        return device(y_ * 2 + xl_, xh_ * 8 + z_, core_)

    def ypeer(d):
        return lax.rem(y + d, 4)

    def zpeer(d):
        return lax.rem(z + d + 8, 8)

    def flip(value, by):
        return 1 - value if by else value

    for block in range(2):
        on = jnp.float32(0.0)
        for i in range(2):
            hit = (count_ref[0, 0] > i) & (list_ref[0, i] == block)
            on = jnp.maximum(on, jnp.where(hit, 1.0, 0.0))
        acts[core, block : block + 1, :] = jnp.full((1, 128), on, F32)

    sibling = at(xh, z, other, y, xl)
    up = at(xh, zpeer(1), core, y, xl)
    down = at(xh, zpeer(-1), core, y, xl)
    partner = at(1 - xh, z, core, y, 1 - xl)
    peers = [device(n + dn + 8, chip + dc + 16, c) for dn, dc in NEAR for c in (0, 1)]
    peers += [at(xh, zpeer(d), core, y, xl) for d in range(1, 8)]
    for a in (0, 1):
        for c in (0, 1):
            for d in range(4):
                for b in (0, 1):
                    if (a, c, d, b) != (0, 0, 0, 0):
                        peers.append(at(flip(xh, a), z, flip(core, c), ypeer(d), flip(xl, b)))
    greet(peers)

    sends = []

    def go(src, dst, send, recv, to):
        cp = remote(src, dst, send, recv, to)
        cp.start()
        sends.append(cp)

    def came(dst, send, recv):
        remote(dst, dst, send, recv, sibling).wait_recv()

    own = []
    for t in range(3):
        here = wg_ref.at[t, xh, z, core]
        go(
            w_ref.at[:, pl.ds(pl.multiple_of(t * 1024 + other * 512, 512), 512)],
            here, w_send.at[t], w_recv.at[t], sibling,
        )
        cp = pltpu.make_async_copy(
            w_ref.at[:, pl.ds(pl.multiple_of(t * 1024 + core * 512, 512), 512)], here, w_local.at[t]
        )
        cp.start()
        own.append(cp)
    go(acts.at[core], acts.at[core], act_send, act_recv, sibling)

    hops = {(0, 0): 4, (0, 1): 3, (1, 0): 3, (1, 1): 4}

    def slab(t, s, index):
        return wg_ref.at[t, xh if s == 0 else 1 - xh, lax.rem(index + 16, 8)]

    def forward(s, d, k, t):
        moved = slab(t, s, z - k if d == 0 else z + k)
        go(moved, moved, r_send.at[s, d, k, t], r_recv.at[s, d, k, t], up if d == 0 else down)

    def arrived(s, d, k, t):
        came(
            slab(t, s, z - 1 - k if d == 0 else z + 1 + k),
            r_send.at[s, d, k, t], r_recv.at[s, d, k, t],
        )

    for t in range(3):
        own[t].wait()
        came(wg_ref.at[t, xh, z, other], w_send.at[t], w_recv.at[t])
        mine = slab(t, 0, z)
        go(mine, mine, p_send.at[t], p_recv.at[t], partner)
        forward(0, 0, 0, t)
        forward(0, 1, 0, t)

    side_chip = chip + 2 * core - 1 + 16
    tensors = ((x_ref, lambda c: xr_ref.at[c]), (g_ref, lambda c: gr_ref))
    locals_ = []

    def send_region(i, dns):
        src, dst = tensors[i]
        for dn in dns:
            lo, count, to_row = ROWS[dn]
            for side in (0, 1):
                for rel in (0, 1):
                    c = core if rel == 0 else other
                    if side == 0:
                        source = src.at[pl.ds(lo, count), :, :, half_of(c)]
                        target = dst(c).at[pl.ds(to_row, count), pl.ds(1 + 2 * core, 2)]
                        slot = core
                        to = device(n + dn + 8, chip, c)
                    else:
                        source = src.at[pl.ds(lo, count), pl.ds(core, 1), :, half_of(c)]
                        target = dst(c).at[pl.ds(to_row, count), pl.ds(5 * other, 1)]
                        slot = 3 - core
                        to = device(n + dn + 8, side_chip, c)
                    if dn == 0 and side == 0 and rel == 0:
                        cp = pltpu.make_async_copy(source, target, h_local.at[i])
                        cp.start()
                        locals_.append(cp)
                    else:
                        go(
                            source, target, h_send.at[i, dn + 1, side, rel],
                            h_recv.at[i, dn + 1, slot], to,
                        )

    def region_came(i, dst, dn, piece):
        lo, count, to_row = ROWS[dn]
        if piece < 2:
            slot = other if dn == 0 else piece
            landed = dst.at[pl.ds(to_row, count), pl.ds(1 + 2 * slot, 2)]
        else:
            slot = piece
            landed = dst.at[pl.ds(to_row, count), pl.ds(0 if piece == 2 else 5, 1)]
        came(landed, h_send.at[i, dn + 1, 0, 0], h_recv.at[i, dn + 1, slot])

    pieces = [(dn, piece) for dn in (-1, 0, 1) for piece in range(4) if (dn, piece) != (0, 1)]
    send_region(0, (-1, 1, 0))
    for t in range(3):
        came(slab(t, 1, z), p_send.at[t], p_recv.at[t])
        forward(1, 0, 0, t)
        forward(1, 1, 0, t)
    send_region(1, (0,))
    for d in (2, 1, 3):
        want = ypeer(d) // 2
        for rel in (0, 1):
            go(
                x_ref.at[:, :, :, half_of(want)], xall_ref.at[3 - d, core],
                e_send.at[d - 1, rel], e_recv.at[3 - d, core],
                at(xh, z, core if rel == 0 else other, ypeer(d), xl),
            )

    def project(part, first):
        for t, region in enumerate((qr_ref, kr, vr)):

            def chunk(i, carry, t=t, region=region):
                rows = pl.ds(4 * i, 4)
                out = nn(xr_ref[part, rows].reshape(192, 512), wg_ref[t, part].reshape(512, 512))
                if first:
                    acc[t, rows] = out.reshape(4, 6, 8, 512)
                else:
                    out = out.reshape(4, 6, 8, 512) + acc[t, rows]
                    acc[t, rows] = out
                    region[rows] = out.astype(BF16).reshape(4, 48, 512)
                return carry

            lax.fori_loop(0, 5, chunk, 0)

    def hop(s, k):
        for t in range(3):
            for d in range(2):
                if k <= hops[s, d]:
                    arrived(s, d, k - 1, t)
                if k < hops[s, d]:
                    forward(s, d, k, t)

    hop(0, 1)
    hop(1, 1)
    hop(0, 2)
    locals_[0].wait()
    for dn, piece in pieces:
        region_came(0, xr_ref.at[core], dn, piece)
    go(xr_ref.at[core], xr_ref.at[core], s_send, s_recv, sibling)
    hop(1, 2)
    send_region(1, (-1, 1))
    hop(0, 3)
    hop(1, 3)
    hop(0, 4)
    for hf in range(2):
        bias[hf] = window_bias(hf)
    came(xr_ref.at[other], s_send, s_recv)
    project(xh, True)
    hop(1, 4)
    project(1 - xh, False)
    for t in range(3):
        for hf in range(2):
            own_t = acc[t, 6:14, 1 + 2 * hf : 3 + 2 * hf].reshape(128, 512).astype(BF16)
            if t == 0:
                qown[hf] = own_t * SCALE
            elif t == 1:
                kown_ref[hf] = own_t * SCALE
            else:
                vown_ref[hf] = own_t

    locals_[1].wait()
    region_came(1, gr_ref, 0, 0)
    came(acts.at[other], act_send, act_recv)
    inner = lax.broadcasted_iota(jnp.int32, (128, 128), 0)
    for hf in range(2):
        groups = pl.ds(1 + 2 * hf, 2)
        gown[hf] = gr_ref[6:14, groups].astype(F32).reshape(128, 512).astype(BF16)
        ldacc[...] = jnp.zeros_like(ldacc)
        active = jnp.where(lax.rem(inner, 16) < 8, acts[hf, 0:1, :], acts[hf, 1:2, :])

        def pair(hp, carry, hf=hf, active=active):
            lanes = lanes_of(hp)
            low, masks, lane = head_masks()
            keys = kr[:, 16 * hf : 16 * hf + 32, lanes].reshape(640, 128)
            values = vr[:, 16 * hf : 16 * hf + 32, lanes].reshape(640, 128)
            query = qown[hf, :, lanes]
            grad = gown[hf, :, lanes]
            outs, dqs = [], []
            ld = ldacc[...]
            for j in range(2):
                s = nt(query * masks[j], keys) + bias[hf]
                top = jnp.max(s, axis=1, keepdims=True)
                e = jnp.exp(s - top)
                total = jnp.sum(e, axis=1, keepdims=True)
                p = e * (1.0 / total)
                lse = top + jnp.log(total)
                out = nn(p.astype(BF16), values)
                out = out.astype(BF16).astype(F32)
                gm = grad * masks[j]
                delta = jnp.sum(gm.astype(F32) * out, axis=1, keepdims=True)
                dp = nt(gm, values)
                ds = (p * (dp - delta) * SCALE).astype(BF16)
                dqs.append(nn(ds, keys))
                outs.append(out)
                on = active > 0.0
                head = 2 * hp + j
                ld = jnp.where(lane == head, jnp.where(on, lse, HUGE), ld)
                ld = jnp.where(lane == head + 8, jnp.where(on, delta, 0.0), ld)
            ldacc[...] = ld
            attn_ref[hf, :, lanes] = (jnp.where(low, outs[0], outs[1]) * active).astype(BF16)
            dq_ref[hp, hf] = (jnp.where(low, dqs[0], dqs[1]) * active).astype(BF16)
            return carry

        lax.fori_loop(0, 4, pair, 0)
        ldall[:, 16 * hf : 16 * hf + 16, :] = ldacc[...].reshape(8, 16, 128)
    for i in range(2):
        ld_ref[:, 128 * i : 128 * i + 128] = ldall[4 * i : 4 * i + 4].reshape(128, 128).T[:16]

    for dn, dc in NEAR:
        go(
            ld_ref, ldb.at[1 - dn, 1 - dc], ld_send.at[dn + 1, dc + 1], ld_recv.at[1 - dn, 1 - dc],
            device(n + dn + 8, chip + dc + 16, core),
        )
    for d in (2, 1, 3):
        go(
            dq_ref.at[pl.ds(2 * lax.rem(ypeer(d), 2), 2)], gall.at[4 - d, pl.ds(0, 2)],
            q_send.at[d - 1], q_recv.at[3 - d], at(xh, z, core, ypeer(d), xl),
        )
    go(attn_ref.at[other], attn_out.at[:, half_of(core)], a_send, a_recv, sibling)
    attn_own = pltpu.make_async_copy(attn_ref.at[core], attn_out.at[:, half_of(core)], o_sem.at[0])
    attn_own.start()

    def share(hp):
        for d in (2, 1, 3):
            go(
                kv.at[hp, lax.rem(ypeer(d), 2)], gall.at[4 - d, 2 + hp],
                k_send.at[hp, d - 1], k_recv.at[hp, 3 - d], at(xh, z, core, ypeer(d), xl),
            )

    def product(first, count):
        if count == 2:
            columns = jnp.concatenate(
                [gall[:, first + j].reshape(1024, 128) for j in range(count)], axis=1
            )
        else:
            columns = gall[:, first].reshape(1024, 128)

        def rows(i, carry):
            out = nn(xt_ref[pl.ds(pl.multiple_of(i * 128, 128), 128), :], columns)
            out = out.reshape(2, 2, 2, 2, 8, 128 * count)
            for j in range(count):
                p[first + j, pl.ds(2 * i, 2)] = out[..., 128 * j : 128 * j + 128]
            return carry

        lax.fori_loop(0, 4, rows, 0)
        for b in range(first, first + count):
            for i in (2, 0, 1):
                a, l = flip(xh, XPEERS[i][0]), flip(xl, XPEERS[i][1])
                go(
                    p.at[b, :, l, a], rx.at[b, i], x_send.at[b, i], x_recv.at[b, i],
                    at(a, z, core, y, l),
                )

    def product_q():
        for r in range(3):
            came(gall.at[r + 1, pl.ds(0, 2)], q_send.at[r], q_recv.at[r])
        for j in range(2):
            gall[0, j] = dq_ref[2 * col_half + j]
        product(0, 2)

    def product_kv(hp):
        for r in range(3):
            came(gall.at[r + 1, 2 + hp], k_send.at[hp, r], k_recv.at[hp, r])
        gall[0, 2 + hp] = kv[hp, col_half]
        product(2 + hp, 1)

    def sum_x(b):
        for i in range(3):
            came(rx.at[b, i], x_send.at[b, i], x_recv.at[b, i])
        for j in range(8):
            cz[j, b] = p[b, j, xl, xh] + rx[b, 0, j] + rx[b, 1, j] + rx[b, 2, j]

    batches = ((0, 4), (4, 2))

    def spread(h):
        lo, count = batches[h]
        for d in (4, 3, 5, 2, 6, 1, 7):
            go(
                cz.at[zpeer(d), pl.ds(lo, count)], rc.at[d - 1, pl.ds(lo, count)],
                c_send.at[h, d - 1], c_recv.at[h, d - 1], at(xh, zpeer(d), core, y, xl),
            )

    factor = 1.0 / math.sqrt(32768.0)

    def sum_z(h):
        lo, count = batches[h]
        for d in range(7):
            came(rc.at[d, pl.ds(lo, count)], c_send.at[h, d], c_recv.at[h, d])
        for b in range(lo, lo + count):
            total = cz[z, b]
            for d in range(7):
                total = total + rc[d, b]
            total = total.reshape(16, 128) * factor
            if b < 2:
                fin_q[:, 128 * b : 128 * b + 128] = total
            else:
                fin_kv[:, 128 * (b - 2) : 128 * (b - 1)] = total

    for dn, piece in pieces:
        if (dn, piece) != (0, 0):
            region_came(1, gr_ref, dn, piece)

    def regroup(i, carry):
        rows = gr_ref[pl.ds(4 * i, 4)].astype(F32).reshape(192, 512)
        grs_ref[pl.ds(4 * i, 4)] = rows.astype(BF16).reshape(4, 48, 512)
        return carry

    lax.fori_loop(0, 5, regroup, 0)
    for r in range(3):
        for c in range(2):
            came(xall_ref.at[r, c], e_send.at[r, c], e_recv.at[r, c])
    for hf in range(2):
        groups = pl.ds(1 + 2 * hf, 2)
        for r in range(4):
            if r == 0:
                tokens = xr_ref[row_half, 6:14, groups]
            else:
                tokens = xall_ref[r - 1, hf]
            tokens = tokens.astype(F32).reshape(128, 512)
            to_lane = 256 * r + 128 * hf
            for i in range(4):
                xt_ref[128 * i : 128 * i + 128, to_lane : to_lane + 128] = (
                    tokens[:, 128 * i : 128 * i + 128].T.astype(BF16)
                )
    ldb[1, 1] = ld_ref[...]
    for dn, dc in NEAR:
        came(ldb.at[1 - dn, 1 - dc], ld_send.at[dn + 1, dc + 1], ld_recv.at[1 - dn, 1 - dc])
    column = lax.rem(lax.broadcasted_iota(jnp.int32, (16, 256), 1), 32)
    for hf in range(2):
        parts = []
        for r in range(3):
            left, mid, right = ldb[r, 0], ldb[r, 1], ldb[r, 2]
            if hf == 0:
                part = jnp.where(column < 8, pltpu.roll(left, 232, 1), pltpu.roll(mid, 8, 1))
            else:
                part = jnp.where(column < 24, pltpu.roll(mid, 248, 1), pltpu.roll(right, 24, 1))
            parts.append(part)
        lds[hf] = pltpu.roll(jnp.concatenate(parts, axis=1), 768 - 64, 1)[:, :640]

    low, masks, _ = head_masks()

    def key_side(hp):
        lanes = slice(128 * hp, 128 * hp + 128)

        def side(hf, carry):
            window = pl.ds(pl.multiple_of(16 * hf, 16), 32)
            query = qr_ref[:, window, lanes].reshape(640, 128)
            grad = grs_ref[:, window, lanes].reshape(640, 128)
            keys = kown_ref[hf, :, lanes]
            values = vown_ref[hf, :, lanes]
            dks, dvs = [], []
            for j in range(2):
                head = 2 * hp + j
                s = nt(keys * masks[j], query) + bias[hf]
                e = jnp.exp(s - lds[hf, head : head + 1, :])
                dvs.append(nn(e.astype(BF16), grad))
                dp = nt(values * masks[j], grad)
                ds = (e * (dp - lds[hf, head + 8 : head + 9, :]) * SCALE).astype(BF16)
                dks.append(nn(ds, query))
            kv[hp, 0, hf] = jnp.where(low, dks[0], dks[1]).astype(BF16)
            kv[hp, 1, hf] = jnp.where(low, dvs[0], dvs[1]).astype(BF16)
            return carry

        lax.fori_loop(0, 2, side, 0)
        share(hp)

    key_side(0)
    product_q()
    key_side(1)
    product_kv(0)
    key_side(2)
    product_kv(1)
    sum_x(0)
    sum_x(1)
    key_side(3)
    product_kv(2)
    sum_x(2)
    sum_x(3)
    spread(0)

    all_q = jnp.concatenate([dq_ref[h].reshape(256, 128) for h in range(4)], axis=1)
    all_k = jnp.concatenate([kv[h, 0].reshape(256, 128) for h in range(4)], axis=1)
    all_v = jnp.concatenate([kv[h, 1].reshape(256, 128) for h in range(4)], axis=1)

    def input_columns(i, carry):
        rows = pl.ds(pl.multiple_of(i * 256, 256), 256)
        part = [wg_ref[t, i // 2, pl.ds(4 * lax.rem(i, 2), 4)].reshape(256, 512) for t in range(3)]
        total = nt(all_q, part[0]) + nt(all_k, part[1]) + nt(all_v, part[2])
        gx[:, :, rows] = total.reshape(2, 128, 256)
        return carry

    product_kv(3)
    lax.fori_loop(0, 4, input_columns, 0)
    go(gx.at[other], gxr, g_send, g_recv, sibling)
    sum_x(4)
    sum_x(5)
    spread(1)
    came(gxr, g_send, g_recv)
    gxo[...] = (gx[core] + gxr[...]).astype(BF16)
    gx_own = pltpu.make_async_copy(gxo, gx_out, o_sem.at[1])
    gx_own.start()
    sum_z(0)
    sum_z(1)

    def spots(c, part, a):
        rows = pl.ds(pl.multiple_of(16 * a, 16), 16)
        q_at = pl.multiple_of(c * 512 + part * 256, 256)
        kv_at = pl.multiple_of((1 + part) * 1024 + c * 512, 512)
        return gw_out.at[rows, pl.ds(q_at, 256)], gw_out.at[rows, pl.ds(kv_at, 512)]

    mine = spots(core, col_half, xh)
    for i, fin in enumerate((fin_q, fin_kv)):
        recv = f_recv.at[i, core, col_half, xh]
        for d in (2, 1, 3):
            for b in (0, 1):
                go(fin, mine[i], f_send.at[i, d, b], recv, at(row_half, z, xl, ypeer(d), flip(xl, b)))
        go(fin, mine[i], f_send.at[i, 0, 1], recv, at(row_half, z, xl, y, 1 - xl))
        away = remote(fin, mine[i], f_send.at[i, 0, 0], recv, at(row_half, z, xl, y, xl))
        here = pltpu.make_async_copy(fin, mine[i], f_local.at[i])
        is_here = (core == xl) & (row_half == xh)

        @pl.when(is_here)
        def _():
            here.start()
            here.wait()

        @pl.when(jnp.logical_not(is_here))
        def _():
            away.start()
            away.wait_send()

    attn_own.wait()
    gx_own.wait()
    came(attn_out.at[:, half_of(other)], a_send, a_recv)
    for c in range(2):
        for part in range(2):
            for a in range(2):
                landed = spots(c, part, a)
                own = (
                    (c == core) & (part == col_half) & (a == xh) & (row_half == xh) & (xl == core)
                )
                for i in range(2):

                    @pl.when(jnp.logical_not(own))
                    def _():
                        came(landed[i], f_send.at[i, 0, 0], f_recv.at[i, c, part, a])

    for cp in sends:
        cp.wait_send()


def layer(x4, g4, weight, block_list, block_count):
    dma = pltpu.SemaphoreType.DMA
    vmem = lambda *shape: pltpu.VMEM(shape, F32)
    half = lambda *shape: pltpu.VMEM(shape, BF16)
    shape = jax.ShapeDtypeStruct
    smem = pl.BlockSpec(memory_space=pltpu.SMEM)
    return pl.pallas_call(
        layer_kernel,
        out_shape=(
            shape((128, 1024), BF16), shape((128, 1024), BF16), shape((32, 3072), F32),
        ),
        in_specs=[VM] * 3 + [smem] * 2,
        out_specs=(ANY,) * 3,
        scratch_shapes=[
            half(2, 20, 6, 8, 512), half(20, 6, 8, 512), half(3, 2, 8, 2, 32, 512),
            half(3, 2, 8, 2, 8, 512), vmem(2, 8, 128),
            vmem(3, 20, 6, 8, 512), half(20, 48, 512), half(20, 48, 512), half(20, 48, 512),
            half(20, 48, 512), half(2, 128, 512), half(2, 128, 512), half(2, 128, 512),
            half(2, 128, 512), vmem(128, 128), vmem(8, 32, 128), vmem(16, 256),
            half(4, 2, 128, 128), half(2, 128, 512), half(512, 1024),
            half(4, 6, 2, 128, 128), vmem(6, 8, 2, 2, 2, 8, 128), vmem(6, 3, 8, 2, 8, 128),
            vmem(8, 6, 2, 8, 128), vmem(7, 6, 2, 8, 128), vmem(16, 256), vmem(16, 512),
            half(4, 2, 2, 128, 128), vmem(2, 16, 640), vmem(3, 3, 16, 256), vmem(2, 128, 640),
            vmem(2, 128, 1024), vmem(128, 1024), half(128, 1024),
            dma((2, 3, 2, 2)), dma((2, 3, 4)), dma((2,)), dma, dma, dma, dma,
            dma((3,)), dma((3,)), dma((3,)), dma((3,)), dma((3,)),
            dma((2, 2, 4, 3)), dma((2, 2, 4, 3)), dma((3, 2)), dma((3, 2)),
            dma((3, 3)), dma((3, 3)), dma((2,)), dma, dma, dma, dma,
            dma((3,)), dma((3,)), dma((4, 3)), dma((4, 3)), dma((6, 3)), dma((6, 3)),
            dma((2, 7)), dma((2, 7)), dma((2, 4, 2)), dma((2, 2, 2, 2)), dma((2,)),
        ],
        compiler_params=pltpu.CompilerParams(
            collective_id=0, has_side_effects=True, vmem_limit_bytes=VMEM_LIMIT
        ),
        name="layer",
    )(x4, g4, weight, block_list, block_count)


def local(image_tokens, qkv_weight, block_list, block_count, out_grad):
    attn_out, grad_x, grad_w = layer(
        image_tokens.reshape(8, 2, 8, 1024), out_grad.reshape(8, 2, 8, 1024), qkv_weight,
        block_list, block_count,
    )
    return attn_out.reshape(8, 16, 1024), grad_x.reshape(8, 16, 1024), grad_w


def solution(mesh):
    placed = (
        P("narrow", "wide", None),
        P("wide", None),
        P("narrow", "wide"),
        P("narrow", "wide"),
        P("narrow", "wide", None),
    )
    return jax.shard_map(
        local,
        mesh=mesh,
        in_specs=placed,
        out_specs=(P("narrow", "wide", None), P("narrow", "wide", None), P("wide", None)),
        check_vma=False,
    )
```

```python
import functools
import math

import jax
import jax.numpy as jnp
from jax import lax
from jax.experimental import pallas as pl
from jax.experimental.pallas import tpu as pltpu
from jax.sharding import PartitionSpec as P

MESH = pl.DeviceIdType.MESH
F32 = jnp.float32
BF16 = jnp.bfloat16
RADIUS = 6
NEGATIVE = -1e30
HUGE = 1e30
SCALE = 0.125
VMEM_LIMIT = 60 * 1024 * 1024
ANY = pl.BlockSpec(memory_space=pl.ANY)
VM = pl.BlockSpec(memory_space=pltpu.VMEM)

ROWS = {-1: (0, 6, 14), 0: (0, 8, 6), 1: (2, 6, 0)}


def place():
    wide = lax.axis_index("wide")
    narrow = lax.axis_index("narrow")
    return narrow, wide // 2, wide % 2


def device(narrow, chip, core):
    return {"wide": lax.rem(chip, 16) * 2 + core, "narrow": lax.rem(narrow, 8)}


def remote(src, dst, send, recv, to):
    return pltpu.make_async_remote_copy(
        src_ref=src, dst_ref=dst, send_sem=send, recv_sem=recv, device_id=to, device_id_type=MESH
    )


def greet(devices):
    barrier = pltpu.get_barrier_semaphore()
    for to in devices:
        pl.semaphore_signal(barrier, inc=1, device_id=to, device_id_type=MESH)
    pl.semaphore_wait(barrier, len(devices))


def half_of(core):
    return pl.ds(pl.multiple_of(core * 512, 512), 512)


def window_bias(hf):
    n, chip, _ = place()
    shape = (128, 640)
    inner = lax.broadcasted_iota(jnp.int32, shape, 0)
    outer = lax.broadcasted_iota(jnp.int32, shape, 1)
    row, col = outer // 32, outer % 32
    down = row - RADIUS - inner // 16
    across = col - 8 - inner % 16
    grid_row = n * 8 - RADIUS + row
    grid_col = chip * 32 - 8 + 16 * hf + col
    ok = (jnp.abs(down) <= RADIUS) & (jnp.abs(across) <= RADIUS)
    ok = ok & (grid_row >= 0) & (grid_row < 64) & (grid_col >= 0) & (grid_col < 512)
    return jnp.where(ok, 0.0, NEGATIVE)


def nt(a, b):
    return lax.dot_general(a, b, (((1,), (1,)), ((), ())), preferred_element_type=F32)


def nn(a, b):
    return jnp.dot(a, b, preferred_element_type=F32)


def tn(a, b):
    return lax.dot_general(a, b, (((0,), (0,)), ((), ())), preferred_element_type=F32)


def stacked(pair, masks):
    return jnp.concatenate([pair * masks[0], pair * masks[1]], axis=0)


def head_masks():
    lane = lax.broadcasted_iota(jnp.int32, (128, 128), 1)
    low = lane < 64
    return low, (low.astype(F32).astype(BF16), (1.0 - low.astype(F32)).astype(BF16)), lane


XPEERS = ((0, 1), (1, 0), (1, 1))
NEAR = tuple((dn, dc) for dn in (-1, 0, 1) for dc in (-1, 0, 1) if (dn, dc) != (0, 0))


Q_BLOCKS = (0, 3)
KV_BLOCKS = (1, 2, 4, 5)


def layer_kernel(
    x_ref, g_ref, w_ref, list_ref, count_ref,
    attn_out, gx_out, gw_out,
    xr_ref, gr_ref, wg_ref, xall_ref, acts,
    acc, qr_ref, kr, vr, grs_ref, qown, kown_ref, vown_ref, gown, on_tokens, ldall, ld_ref,
    dq_ref, attn_ref, xt_ref,
    gall, p, rx, cz, rc, fin_q, fin_kv, kv, lds, ldb, bias, gx, gxr, gxo,
    h_send, h_recv, h_local, s_send, s_recv, act_send, act_recv,
    w_send, w_recv, w_local, p_send, p_recv, r_send, r_recv, e_send, e_recv,
    ld_send, ld_recv, o_sem, a_send, a_recv, g_send, g_recv,
    q_send, q_recv, k_send, k_recv, x_send, x_recv, c_send, c_recv, f_send, f_recv, f_local,
):
    n, chip, core = place()
    other = 1 - core
    z = lax.rem(chip, 8)
    xh = chip // 8
    y = n // 2
    xl = lax.rem(n, 2)
    row_half = y // 2
    col_half = lax.rem(y, 2)

    def at(xh_, z_, core_, y_, xl_):
        return device(y_ * 2 + xl_, xh_ * 8 + z_, core_)

    def ypeer(d):
        return lax.rem(y + d, 4)

    def zpeer(d):
        return lax.rem(z + d + 8, 8)

    def flip(value, by):
        return 1 - value if by else value

    for block in range(2):
        on = jnp.float32(0.0)
        for i in range(2):
            hit = (count_ref[0, 0] > i) & (list_ref[0, i] == block)
            on = jnp.maximum(on, jnp.where(hit, 1.0, 0.0))
        acts[core, block : block + 1, :] = jnp.full((1, 128), on, F32)

    sibling = at(xh, z, other, y, xl)
    up = at(xh, zpeer(1), core, y, xl)
    down = at(xh, zpeer(-1), core, y, xl)
    partner = at(1 - xh, z, core, y, 1 - xl)
    peers = [device(n + dn + 8, chip + dc + 16, c) for dn, dc in NEAR for c in (0, 1)]
    peers += [at(xh, zpeer(d), core, y, xl) for d in range(1, 8)]
    for a in (0, 1):
        for c in (0, 1):
            for d in range(4):
                for b in (0, 1):
                    if (a, c, d, b) != (0, 0, 0, 0):
                        peers.append(at(flip(xh, a), z, flip(core, c), ypeer(d), flip(xl, b)))
    greet(peers)

    sends = []

    def go(src, dst, send, recv, to):
        cp = remote(src, dst, send, recv, to)
        cp.start()
        sends.append(cp)

    def came(dst, send, recv):
        remote(dst, dst, send, recv, sibling).wait_recv()

    own = []
    for t in range(3):
        here = wg_ref.at[t, xh, z, core]
        go(
            w_ref.at[:, pl.ds(pl.multiple_of(t * 1024 + other * 512, 512), 512)],
            here, w_send.at[t], w_recv.at[t], sibling,
        )
        cp = pltpu.make_async_copy(
            w_ref.at[:, pl.ds(pl.multiple_of(t * 1024 + core * 512, 512), 512)], here, w_local.at[t]
        )
        cp.start()
        own.append(cp)
    go(acts.at[core], acts.at[core], act_send, act_recv, sibling)

    hops = {(0, 0): 4, (0, 1): 3, (1, 0): 3, (1, 1): 4}

    def slab(t, s, index):
        return wg_ref.at[t, xh if s == 0 else 1 - xh, lax.rem(index + 16, 8)]

    def forward(s, d, k, t):
        moved = slab(t, s, z - k if d == 0 else z + k)
        go(moved, moved, r_send.at[s, d, k, t], r_recv.at[s, d, k, t], up if d == 0 else down)

    def arrived(s, d, k, t):
        came(
            slab(t, s, z - 1 - k if d == 0 else z + 1 + k),
            r_send.at[s, d, k, t], r_recv.at[s, d, k, t],
        )

    for t in range(3):
        own[t].wait()
        came(wg_ref.at[t, xh, z, other], w_send.at[t], w_recv.at[t])
        mine = slab(t, 0, z)
        go(mine, mine, p_send.at[t], p_recv.at[t], partner)
        forward(0, 0, 0, t)
        forward(0, 1, 0, t)

    side_chip = chip + 2 * core - 1 + 16
    tensors = ((x_ref, lambda c: xr_ref.at[c]), (g_ref, lambda c: gr_ref))
    locals_ = []

    def send_region(i, dns):
        src, dst = tensors[i]
        for dn in dns:
            lo, count, to_row = ROWS[dn]
            for side in (0, 1):
                for rel in (0, 1):
                    c = core if rel == 0 else other
                    if side == 0:
                        source = src.at[pl.ds(lo, count), :, :, half_of(c)]
                        target = dst(c).at[pl.ds(to_row, count), pl.ds(1 + 2 * core, 2)]
                        slot = core
                        to = device(n + dn + 8, chip, c)
                    else:
                        source = src.at[pl.ds(lo, count), pl.ds(core, 1), :, half_of(c)]
                        target = dst(c).at[pl.ds(to_row, count), pl.ds(5 * other, 1)]
                        slot = 3 - core
                        to = device(n + dn + 8, side_chip, c)
                    if dn == 0 and side == 0 and rel == 0:
                        cp = pltpu.make_async_copy(source, target, h_local.at[i])
                        cp.start()
                        locals_.append(cp)
                    else:
                        go(
                            source, target, h_send.at[i, dn + 1, side, rel],
                            h_recv.at[i, dn + 1, slot], to,
                        )

    def region_came(i, dst, dn, piece):
        lo, count, to_row = ROWS[dn]
        if piece < 2:
            slot = other if dn == 0 else piece
            landed = dst.at[pl.ds(to_row, count), pl.ds(1 + 2 * slot, 2)]
        else:
            slot = piece
            landed = dst.at[pl.ds(to_row, count), pl.ds(0 if piece == 2 else 5, 1)]
        came(landed, h_send.at[i, dn + 1, 0, 0], h_recv.at[i, dn + 1, slot])

    pieces = [(dn, piece) for dn in (-1, 0, 1) for piece in range(4) if (dn, piece) != (0, 1)]
    send_region(0, (-1, 1, 0))
    for t in range(3):
        came(slab(t, 1, z), p_send.at[t], p_recv.at[t])
        forward(1, 0, 0, t)
        forward(1, 1, 0, t)
    send_region(1, (0,))
    for d in (2, 1, 3):
        want = ypeer(d) // 2
        for rel in (0, 1):
            go(
                x_ref.at[:, :, :, half_of(want)], xall_ref.at[3 - d, core],
                e_send.at[d - 1, rel], e_recv.at[3 - d, core],
                at(xh, z, core if rel == 0 else other, ypeer(d), xl),
            )

    def project(part, first):
        for t, region in enumerate((qr_ref, kr, vr)):

            def chunk(i, carry, t=t, region=region):
                rows = pl.ds(4 * i, 4)
                out = nn(xr_ref[part, rows].reshape(192, 512), wg_ref[t, part].reshape(512, 512))
                if first:
                    acc[t, rows] = out.reshape(4, 6, 8, 512)
                else:
                    out = out.reshape(4, 6, 8, 512) + acc[t, rows]
                    acc[t, rows] = out
                    region[rows] = out.astype(BF16).reshape(4, 48, 512)
                return carry

            lax.fori_loop(0, 5, chunk, 0)

    def hop(s, k):
        for t in range(3):
            for d in range(2):
                if k <= hops[s, d]:
                    arrived(s, d, k - 1, t)
                if k < hops[s, d]:
                    forward(s, d, k, t)

    hop(0, 1)
    hop(1, 1)
    hop(0, 2)
    locals_[0].wait()
    for dn, piece in pieces:
        region_came(0, xr_ref.at[core], dn, piece)
    go(xr_ref.at[core], xr_ref.at[core], s_send, s_recv, sibling)
    hop(1, 2)
    send_region(1, (-1, 1))
    hop(0, 3)
    hop(1, 3)
    hop(0, 4)
    for hf in range(2):
        bias[hf] = window_bias(hf)
    came(xr_ref.at[other], s_send, s_recv)
    project(xh, True)
    hop(1, 4)
    project(1 - xh, False)
    for t in range(3):
        for hf in range(2):
            own_t = acc[t, 6:14, 1 + 2 * hf : 3 + 2 * hf].reshape(128, 512).astype(BF16)
            if t == 0:
                qown[hf] = own_t * SCALE
            elif t == 1:
                kown_ref[hf] = own_t * SCALE
            else:
                vown_ref[hf] = own_t

    locals_[1].wait()
    region_came(1, gr_ref, 0, 0)
    came(acts.at[other], act_send, act_recv)
    inner = lax.broadcasted_iota(jnp.int32, (128, 128), 0)
    for hf in range(2):
        groups = pl.ds(1 + 2 * hf, 2)
        gown[hf] = gr_ref[6:14, groups].astype(F32).reshape(128, 512).astype(BF16)
        on_tokens[hf] = jnp.where(lax.rem(inner, 16) < 8, acts[hf, 0:1, :], acts[hf, 1:2, :])

    low, masks, lane = head_masks()

    def query_side(hp):
        lanes = slice(128 * hp, 128 * hp + 128)

        def side(hf, carry):
            window = pl.ds(pl.multiple_of(16 * hf, 16), 32)
            keys = kr[:, window, lanes].reshape(640, 128)
            values = vr[:, window, lanes].reshape(640, 128)
            query = qown[hf, :, lanes]
            grad = gown[hf, :, lanes]
            active = on_tokens[hf]
            on = active > 0.0
            s = nt(stacked(query, masks), keys)
            s = (s.reshape(2, 128, 640) + bias[hf]).reshape(256, 640)
            top = jnp.max(s, axis=1, keepdims=True)
            e = jnp.exp(s - top)
            total = jnp.sum(e, axis=1, keepdims=True)
            e = e * (1.0 / total)
            lse = top + jnp.log(total)
            out = nn(e.astype(BF16), values).astype(BF16).astype(F32)
            gm = stacked(grad, masks)
            delta = jnp.sum(gm.astype(F32) * out, axis=1, keepdims=True)
            dp = nt(gm, values)
            ds = (e * (dp - delta) * SCALE).astype(BF16)
            dqs = nn(ds, keys)
            ld = jnp.zeros((128, 128), F32)
            for j in range(2):
                rows = slice(128 * j, 128 * j + 128)
                ld = jnp.where(lane == j, jnp.where(on, lse[rows], HUGE), ld)
                ld = jnp.where(lane == j + 2, jnp.where(on, delta[rows], 0.0), ld)
            ldall[:, pl.ds(pl.multiple_of(16 * hf, 16), 16), :] = ld.reshape(8, 16, 128)
            attn_ref[hf, :, lanes] = (jnp.where(low, out[:128], out[128:]) * active).astype(BF16)
            dq_ref[hp, hf] = (jnp.where(low, dqs[:128], dqs[128:]) * active).astype(BF16)
            return carry

        lax.fori_loop(0, 2, side, 0)
        for i in range(2):
            ld_ref[hp, :, 128 * i : 128 * i + 128] = (
                ldall[4 * i : 4 * i + 4].reshape(128, 128).T[:8]
            )
        ldb[hp, 1, 1] = ld_ref[hp]
        for dn, dc in NEAR:
            go(
                ld_ref.at[hp], ldb.at[hp, 1 - dn, 1 - dc], ld_send.at[hp, dn + 1, dc + 1],
                ld_recv.at[hp, 1 - dn, 1 - dc], device(n + dn + 8, chip + dc + 16, core),
            )

    def share_q(j):
        for d in (2, 1, 3):
            go(
                dq_ref.at[2 * j + lax.rem(ypeer(d), 2)], gall.at[4 - d, Q_BLOCKS[j]],
                q_send.at[j, d - 1], q_recv.at[j, 3 - d], at(xh, z, core, ypeer(d), xl),
            )

    def share(hp):
        for d in (2, 1, 3):
            go(
                kv.at[hp, lax.rem(ypeer(d), 2)], gall.at[4 - d, KV_BLOCKS[hp]],
                k_send.at[hp, d - 1], k_recv.at[hp, 3 - d], at(xh, z, core, ypeer(d), xl),
            )

    def product(b):
        columns = gall[:, b].reshape(1024, 128)

        def rows(i, carry):
            out = nn(xt_ref[pl.ds(pl.multiple_of(i * 128, 128), 128), :], columns)
            p[b, pl.ds(2 * i, 2)] = out.reshape(2, 2, 2, 2, 8, 128)
            return carry

        lax.fori_loop(0, 4, rows, 0)
        for i in (2, 0, 1):
            a, l = flip(xh, XPEERS[i][0]), flip(xl, XPEERS[i][1])
            go(p.at[b, :, l, a], rx.at[b, i], x_send.at[b, i], x_recv.at[b, i], at(a, z, core, y, l))

    def product_q(j):
        b = Q_BLOCKS[j]
        for r in range(3):
            came(gall.at[r + 1, b], q_send.at[j, r], q_recv.at[j, r])
        gall[0, b] = dq_ref[2 * j + col_half]
        product(b)

    def product_kv(hp):
        b = KV_BLOCKS[hp]
        for r in range(3):
            came(gall.at[r + 1, b], k_send.at[hp, r], k_recv.at[hp, r])
        gall[0, b] = kv[hp, col_half]
        product(b)

    def sum_x(b):
        for i in range(3):
            came(rx.at[b, i], x_send.at[b, i], x_recv.at[b, i])
        for j in range(8):
            cz[j, b] = p[b, j, xl, xh] + rx[b, 0, j] + rx[b, 1, j] + rx[b, 2, j]

    batches = ((0, 4), (4, 2))

    def spread(h):
        lo, count = batches[h]
        for d in (4, 3, 5, 2, 6, 1, 7):
            go(
                cz.at[zpeer(d), pl.ds(lo, count)], rc.at[d - 1, pl.ds(lo, count)],
                c_send.at[h, d - 1], c_recv.at[h, d - 1], at(xh, zpeer(d), core, y, xl),
            )

    factor = 1.0 / math.sqrt(32768.0)

    def sum_z(h):
        lo, count = batches[h]
        for d in range(7):
            came(rc.at[d, pl.ds(lo, count)], c_send.at[h, d], c_recv.at[h, d])
        for b in range(lo, lo + count):
            total = cz[z, b]
            for d in range(7):
                total = total + rc[d, b]
            total = total.reshape(16, 128) * factor
            if b in Q_BLOCKS:
                fin_q[Q_BLOCKS.index(b)] = total
            else:
                hp = KV_BLOCKS.index(b)
                fin_kv[hp // 2, :, 128 * (hp % 2) : 128 * (hp % 2) + 128] = total

    column = lax.rem(lax.broadcasted_iota(jnp.int32, (8, 256), 1), 32)

    def totals_came(hp):
        for dn, dc in NEAR:
            came(
                ldb.at[hp, 1 - dn, 1 - dc], ld_send.at[hp, dn + 1, dc + 1],
                ld_recv.at[hp, 1 - dn, 1 - dc],
            )
        for hf in range(2):
            parts = []
            for r in range(3):
                left, mid, right = ldb[hp, r, 0], ldb[hp, r, 1], ldb[hp, r, 2]
                if hf == 0:
                    part = jnp.where(column < 8, pltpu.roll(left, 232, 1), pltpu.roll(mid, 8, 1))
                else:
                    part = jnp.where(column < 24, pltpu.roll(mid, 248, 1), pltpu.roll(right, 24, 1))
                parts.append(part)
            lds[hp, hf] = pltpu.roll(jnp.concatenate(parts, axis=1), 768 - 64, 1)[:, :640]

    def key_side(hp):
        lanes = slice(128 * hp, 128 * hp + 128)
        totals_came(hp)

        def side(hf, carry):
            window = pl.ds(pl.multiple_of(16 * hf, 16), 32)
            query = qr_ref[:, window, lanes].reshape(640, 128)
            grad = grs_ref[:, window, lanes].reshape(640, 128)
            keys = kown_ref[hf, :, lanes]
            values = vown_ref[hf, :, lanes]
            s = nt(stacked(keys, masks), query).reshape(2, 128, 640) + bias[hf]
            e = jnp.exp(s - lds[hp, hf, 0:2].reshape(2, 1, 640))
            dvs = nn(e.astype(BF16).reshape(256, 640), grad)
            dp = nt(stacked(values, masks), grad).reshape(2, 128, 640)
            ds = (e * (dp - lds[hp, hf, 2:4].reshape(2, 1, 640)) * SCALE).astype(BF16)
            dks = nn(ds.reshape(256, 640), query)
            kv[hp, 0, hf] = jnp.where(low, dks[:128], dks[128:]).astype(BF16)
            kv[hp, 1, hf] = jnp.where(low, dvs[:128], dvs[128:]).astype(BF16)
            return carry

        lax.fori_loop(0, 2, side, 0)
        share(hp)

    def spots(c, part, a):
        rows = pl.ds(pl.multiple_of(16 * a, 16), 16)
        q_at = c * 512 + part * 128
        kv_at = (1 + part) * 1024 + c * 512
        return [
            gw_out.at[rows, pl.ds(pl.multiple_of(first, 128), count)]
            for first, count in ((q_at, 128), (q_at + 256, 128), (kv_at, 256), (kv_at + 256, 256))
        ]

    finals = [fin_q.at[0], fin_q.at[1], fin_kv.at[0], fin_kv.at[1]]
    mine_at = spots(core, col_half, xh)
    is_here = (core == xl) & (row_half == xh)

    def deliver(which):
        for i in which:
            fin, spot, recv = finals[i], mine_at[i], f_recv.at[i, core, col_half, xh]
            for d in (2, 1, 3):
                for b in (0, 1):
                    go(fin, spot, f_send.at[i, d, b], recv, at(row_half, z, xl, ypeer(d), flip(xl, b)))
            go(fin, spot, f_send.at[i, 0, 1], recv, at(row_half, z, xl, y, 1 - xl))
            away = remote(fin, spot, f_send.at[i, 0, 0], recv, at(row_half, z, xl, y, xl))
            here = pltpu.make_async_copy(fin, spot, f_local.at[i])

            @pl.when(is_here)
            def _():
                here.start()
                here.wait()

            @pl.when(jnp.logical_not(is_here))
            def _():
                away.start()
                away.wait_send()

    query_side(0)
    query_side(1)
    share_q(0)
    for dn, piece in pieces:
        if (dn, piece) != (0, 0):
            region_came(1, gr_ref, dn, piece)

    def regroup(i, carry):
        rows = gr_ref[pl.ds(4 * i, 4)].astype(F32).reshape(192, 512)
        grs_ref[pl.ds(4 * i, 4)] = rows.astype(BF16).reshape(4, 48, 512)
        return carry

    lax.fori_loop(0, 5, regroup, 0)
    for r in range(3):
        for c in range(2):
            came(xall_ref.at[r, c], e_send.at[r, c], e_recv.at[r, c])
    for hf in range(2):
        groups = pl.ds(1 + 2 * hf, 2)
        for r in range(4):
            if r == 0:
                tokens = xr_ref[row_half, 6:14, groups]
            else:
                tokens = xall_ref[r - 1, hf]
            tokens = tokens.astype(F32).reshape(128, 512)
            to_lane = 256 * r + 128 * hf
            for i in range(4):
                xt_ref[128 * i : 128 * i + 128, to_lane : to_lane + 128] = (
                    tokens[:, 128 * i : 128 * i + 128].T.astype(BF16)
                )
    key_side(0)
    query_side(2)
    product_q(0)
    key_side(1)
    product_kv(0)
    query_side(3)
    share_q(1)
    go(attn_ref.at[other], attn_out.at[:, half_of(core)], a_send, a_recv, sibling)
    attn_own = pltpu.make_async_copy(attn_ref.at[core], attn_out.at[:, half_of(core)], o_sem.at[0])
    attn_own.start()
    product_kv(1)
    key_side(2)
    product_q(1)
    sum_x(0)
    sum_x(1)
    key_side(3)
    product_kv(2)
    sum_x(2)
    sum_x(3)
    spread(0)

    all_q = jnp.concatenate([dq_ref[h].reshape(256, 128) for h in range(4)], axis=1)
    all_k = jnp.concatenate([kv[h, 0].reshape(256, 128) for h in range(4)], axis=1)
    all_v = jnp.concatenate([kv[h, 1].reshape(256, 128) for h in range(4)], axis=1)

    def input_columns(i, carry):
        rows = pl.ds(pl.multiple_of(i * 256, 256), 256)
        part = [wg_ref[t, i // 2, pl.ds(4 * lax.rem(i, 2), 4)].reshape(256, 512) for t in range(3)]
        total = nt(all_q, part[0]) + nt(all_k, part[1]) + nt(all_v, part[2])
        gx[:, :, rows] = total.reshape(2, 128, 256)
        return carry

    lax.fori_loop(0, 4, input_columns, 0)
    go(gx.at[other], gxr, g_send, g_recv, sibling)
    product_kv(3)
    sum_z(0)
    deliver(range(3))
    sum_x(4)
    sum_x(5)
    spread(1)
    came(gxr, g_send, g_recv)
    gxo[...] = (gx[core] + gxr[...]).astype(BF16)
    gx_own = pltpu.make_async_copy(gxo, gx_out, o_sem.at[1])
    gx_own.start()
    sum_z(1)
    deliver((3,))

    attn_own.wait()
    gx_own.wait()
    came(attn_out.at[:, half_of(other)], a_send, a_recv)
    for c in range(2):
        for part in range(2):
            for a in range(2):
                landed = spots(c, part, a)
                own = (
                    (c == core) & (part == col_half) & (a == xh) & (row_half == xh) & (xl == core)
                )
                for i in range(4):

                    @pl.when(jnp.logical_not(own))
                    def _():
                        came(landed[i], f_send.at[i, 0, 0], f_recv.at[i, c, part, a])

    for cp in sends:
        cp.wait_send()


def layer(x4, g4, weight, block_list, block_count):
    dma = pltpu.SemaphoreType.DMA
    vmem = lambda *shape: pltpu.VMEM(shape, F32)
    half = lambda *shape: pltpu.VMEM(shape, BF16)
    shape = jax.ShapeDtypeStruct
    smem = pl.BlockSpec(memory_space=pltpu.SMEM)
    return pl.pallas_call(
        layer_kernel,
        out_shape=(
            shape((128, 1024), BF16), shape((128, 1024), BF16), shape((32, 3072), F32),
        ),
        in_specs=[VM] * 3 + [smem] * 2,
        out_specs=(ANY,) * 3,
        scratch_shapes=[
            half(2, 20, 6, 8, 512), half(20, 6, 8, 512), half(3, 2, 8, 2, 32, 512),
            half(3, 2, 8, 2, 8, 512), vmem(2, 8, 128),
            vmem(3, 20, 6, 8, 512), half(20, 48, 512), half(20, 48, 512), half(20, 48, 512),
            half(20, 48, 512), half(2, 128, 512), half(2, 128, 512), half(2, 128, 512),
            half(2, 128, 512), vmem(2, 128, 128), vmem(8, 32, 128), vmem(4, 8, 256),
            half(4, 2, 128, 128), half(2, 128, 512), half(512, 1024),
            half(4, 6, 2, 128, 128), vmem(6, 8, 2, 2, 2, 8, 128), vmem(6, 3, 8, 2, 8, 128),
            vmem(8, 6, 2, 8, 128), vmem(7, 6, 2, 8, 128), vmem(2, 16, 128), vmem(2, 16, 256),
            half(4, 2, 2, 128, 128), vmem(4, 2, 8, 640), vmem(4, 3, 3, 8, 256), vmem(2, 128, 640),
            vmem(2, 128, 1024), vmem(128, 1024), half(128, 1024),
            dma((2, 3, 2, 2)), dma((2, 3, 4)), dma((2,)), dma, dma, dma, dma,
            dma((3,)), dma((3,)), dma((3,)), dma((3,)), dma((3,)),
            dma((2, 2, 4, 3)), dma((2, 2, 4, 3)), dma((3, 2)), dma((3, 2)),
            dma((4, 3, 3)), dma((4, 3, 3)), dma((2,)), dma, dma, dma, dma,
            dma((2, 3)), dma((2, 3)), dma((4, 3)), dma((4, 3)), dma((6, 3)), dma((6, 3)),
            dma((2, 7)), dma((2, 7)), dma((4, 4, 2)), dma((4, 2, 2, 2)), dma((4,)),
        ],
        compiler_params=pltpu.CompilerParams(
            collective_id=0, has_side_effects=True, vmem_limit_bytes=VMEM_LIMIT
        ),
        name="layer",
    )(x4, g4, weight, block_list, block_count)


def local(image_tokens, qkv_weight, block_list, block_count, out_grad):
    attn_out, grad_x, grad_w = layer(
        image_tokens.reshape(8, 2, 8, 1024), out_grad.reshape(8, 2, 8, 1024), qkv_weight,
        block_list, block_count,
    )
    return attn_out.reshape(8, 16, 1024), grad_x.reshape(8, 16, 1024), grad_w


def solution(mesh):
    placed = (
        P("narrow", "wide", None),
        P("wide", None),
        P("narrow", "wide"),
        P("narrow", "wide"),
        P("narrow", "wide", None),
    )
    return jax.shard_map(
        local,
        mesh=mesh,
        in_specs=placed,
        out_specs=(P("narrow", "wide", None), P("narrow", "wide", None), P("wide", None)),
        check_vma=False,
    )
```

```python
import functools
import math

import jax
import jax.numpy as jnp
from jax import lax
from jax.experimental import pallas as pl
from jax.experimental.pallas import tpu as pltpu
from jax.sharding import PartitionSpec as P

MESH = pl.DeviceIdType.MESH
F32 = jnp.float32
BF16 = jnp.bfloat16
RADIUS = 6
NEGATIVE = -1e30
HUGE = 1e30
SCALE = 0.125
VMEM_LIMIT = 60 * 1024 * 1024
ANY = pl.BlockSpec(memory_space=pl.ANY)
VM = pl.BlockSpec(memory_space=pltpu.VMEM)

ROWS = {-1: (0, 6, 14), 0: (0, 8, 6), 1: (2, 6, 0)}


def place():
    wide = lax.axis_index("wide")
    narrow = lax.axis_index("narrow")
    return narrow, wide // 2, wide % 2


def device(narrow, chip, core):
    return {"wide": lax.rem(chip, 16) * 2 + core, "narrow": lax.rem(narrow, 8)}


def remote(src, dst, send, recv, to):
    return pltpu.make_async_remote_copy(
        src_ref=src, dst_ref=dst, send_sem=send, recv_sem=recv, device_id=to, device_id_type=MESH
    )


def greet(devices):
    barrier = pltpu.get_barrier_semaphore()
    for to in devices:
        pl.semaphore_signal(barrier, inc=1, device_id=to, device_id_type=MESH)
    pl.semaphore_wait(barrier, len(devices))


def half_of(core):
    return pl.ds(pl.multiple_of(core * 512, 512), 512)


def window_bias(hf):
    n, chip, _ = place()
    shape = (128, 640)
    inner = lax.broadcasted_iota(jnp.int32, shape, 0)
    outer = lax.broadcasted_iota(jnp.int32, shape, 1)
    row, col = outer // 32, outer % 32
    down = row - RADIUS - inner // 16
    across = col - 8 - inner % 16
    grid_row = n * 8 - RADIUS + row
    grid_col = chip * 32 - 8 + 16 * hf + col
    ok = (jnp.abs(down) <= RADIUS) & (jnp.abs(across) <= RADIUS)
    ok = ok & (grid_row >= 0) & (grid_row < 64) & (grid_col >= 0) & (grid_col < 512)
    return jnp.where(ok, 0.0, NEGATIVE)


def nt(a, b):
    return lax.dot_general(a, b, (((1,), (1,)), ((), ())), preferred_element_type=F32)


def nn(a, b):
    return jnp.dot(a, b, preferred_element_type=F32)


def tn(a, b):
    return lax.dot_general(a, b, (((0,), (0,)), ((), ())), preferred_element_type=F32)


def stacked(pair, masks):
    return jnp.concatenate([pair * masks[0], pair * masks[1]], axis=0)


def head_masks():
    lane = lax.broadcasted_iota(jnp.int32, (128, 128), 1)
    low = lane < 64
    return low, (low.astype(F32).astype(BF16), (1.0 - low.astype(F32)).astype(BF16)), lane


XPEERS = ((0, 1), (1, 0), (1, 1))
NEAR = tuple((dn, dc) for dn in (-1, 0, 1) for dc in (-1, 0, 1) if (dn, dc) != (0, 0))


Q_BLOCKS = (0, 3)
KV_BLOCKS = (1, 2, 4, 5)


def layer_kernel(
    x_ref, g_ref, w_ref, list_ref, count_ref,
    attn_out, gx_out, gw_out,
    xr_ref, gr_ref, wg_ref, xall_ref, acts,
    acc, qr_ref, kr, vr, grs_ref, qown, kown_ref, vown_ref, gown, on_tokens, ldall, ld_ref,
    dq_ref, attn_ref, xt_ref,
    gall, p, rx, cz, rc, fin_q, fin_kv, kv, lds, ldb, bias, gx, gxr, gxo,
    h_send, h_recv, h_local, s_send, s_recv, act_send, act_recv,
    w_send, w_recv, w_local, p_send, p_recv, r_send, r_recv, e_send, e_recv,
    ld_send, ld_recv, o_sem, a_send, a_recv, g_send, g_recv,
    q_send, q_recv, k_send, k_recv, x_send, x_recv, c_send, c_recv, f_send, f_recv, f_local,
):
    n, chip, core = place()
    other = 1 - core
    z = lax.rem(chip, 8)
    xh = chip // 8
    y = n // 2
    xl = lax.rem(n, 2)
    row_half = y // 2
    col_half = lax.rem(y, 2)

    def at(xh_, z_, core_, y_, xl_):
        return device(y_ * 2 + xl_, xh_ * 8 + z_, core_)

    def ypeer(d):
        return lax.rem(y + d, 4)

    def zpeer(d):
        return lax.rem(z + d + 8, 8)

    def flip(value, by):
        return 1 - value if by else value

    for block in range(2):
        on = jnp.float32(0.0)
        for i in range(2):
            hit = (count_ref[0, 0] > i) & (list_ref[0, i] == block)
            on = jnp.maximum(on, jnp.where(hit, 1.0, 0.0))
        acts[core, block : block + 1, :] = jnp.full((1, 128), on, F32)

    sibling = at(xh, z, other, y, xl)
    up = at(xh, zpeer(1), core, y, xl)
    down = at(xh, zpeer(-1), core, y, xl)
    partner = at(1 - xh, z, core, y, 1 - xl)
    peers = [device(n + dn + 8, chip + dc + 16, c) for dn, dc in NEAR for c in (0, 1)]
    peers += [at(xh, zpeer(d), core, y, xl) for d in range(1, 8)]
    for a in (0, 1):
        for c in (0, 1):
            for d in range(4):
                for b in (0, 1):
                    if (a, c, d, b) != (0, 0, 0, 0):
                        peers.append(at(flip(xh, a), z, flip(core, c), ypeer(d), flip(xl, b)))
    greet(peers)

    sends = []

    def go(src, dst, send, recv, to):
        cp = remote(src, dst, send, recv, to)
        cp.start()
        sends.append(cp)

    def came(dst, send, recv):
        remote(dst, dst, send, recv, sibling).wait_recv()

    own = []
    for t in range(3):
        here = wg_ref.at[t, xh, z, core]
        go(
            w_ref.at[:, pl.ds(pl.multiple_of(t * 1024 + other * 512, 512), 512)],
            here, w_send.at[t], w_recv.at[t], sibling,
        )
        cp = pltpu.make_async_copy(
            w_ref.at[:, pl.ds(pl.multiple_of(t * 1024 + core * 512, 512), 512)], here, w_local.at[t]
        )
        cp.start()
        own.append(cp)
    go(acts.at[core], acts.at[core], act_send, act_recv, sibling)

    hops = {(0, 0): 4, (0, 1): 3, (1, 0): 3, (1, 1): 4}

    def slab(t, s, index):
        return wg_ref.at[t, xh if s == 0 else 1 - xh, lax.rem(index + 16, 8)]

    def forward(s, d, k, t):
        moved = slab(t, s, z - k if d == 0 else z + k)
        go(moved, moved, r_send.at[s, d, k, t], r_recv.at[s, d, k, t], up if d == 0 else down)

    def arrived(s, d, k, t):
        came(
            slab(t, s, z - 1 - k if d == 0 else z + 1 + k),
            r_send.at[s, d, k, t], r_recv.at[s, d, k, t],
        )

    for t in range(3):
        own[t].wait()
        came(wg_ref.at[t, xh, z, other], w_send.at[t], w_recv.at[t])
        mine = slab(t, 0, z)
        go(mine, mine, p_send.at[t], p_recv.at[t], partner)
        forward(0, 0, 0, t)
        forward(0, 1, 0, t)

    side_chip = chip + 2 * core - 1 + 16
    tensors = ((x_ref, lambda c: xr_ref.at[c]), (g_ref, lambda c: gr_ref))
    locals_ = []

    def send_region(i, dns):
        src, dst = tensors[i]
        for dn in dns:
            lo, count, to_row = ROWS[dn]
            for side in (0, 1):
                for rel in (0, 1):
                    c = core if rel == 0 else other
                    if side == 0:
                        source = src.at[pl.ds(lo, count), :, :, half_of(c)]
                        target = dst(c).at[pl.ds(to_row, count), pl.ds(1 + 2 * core, 2)]
                        slot = core
                        to = device(n + dn + 8, chip, c)
                    else:
                        source = src.at[pl.ds(lo, count), pl.ds(core, 1), :, half_of(c)]
                        target = dst(c).at[pl.ds(to_row, count), pl.ds(5 * other, 1)]
                        slot = 3 - core
                        to = device(n + dn + 8, side_chip, c)
                    if dn == 0 and side == 0 and rel == 0:
                        cp = pltpu.make_async_copy(source, target, h_local.at[i])
                        cp.start()
                        locals_.append(cp)
                    else:
                        go(
                            source, target, h_send.at[i, dn + 1, side, rel],
                            h_recv.at[i, dn + 1, slot], to,
                        )

    def region_came(i, dst, dn, piece):
        lo, count, to_row = ROWS[dn]
        if piece < 2:
            slot = other if dn == 0 else piece
            landed = dst.at[pl.ds(to_row, count), pl.ds(1 + 2 * slot, 2)]
        else:
            slot = piece
            landed = dst.at[pl.ds(to_row, count), pl.ds(0 if piece == 2 else 5, 1)]
        came(landed, h_send.at[i, dn + 1, 0, 0], h_recv.at[i, dn + 1, slot])

    pieces = [(dn, piece) for dn in (-1, 0, 1) for piece in range(4) if (dn, piece) != (0, 1)]
    send_region(0, (-1, 1, 0))
    for t in range(3):
        came(slab(t, 1, z), p_send.at[t], p_recv.at[t])
        forward(1, 0, 0, t)
        forward(1, 1, 0, t)
    send_region(1, (0,))
    for d in (2, 1, 3):
        want = ypeer(d) // 2
        for rel in (0, 1):
            go(
                x_ref.at[:, :, :, half_of(want)], xall_ref.at[3 - d, core],
                e_send.at[d - 1, rel], e_recv.at[3 - d, core],
                at(xh, z, core if rel == 0 else other, ypeer(d), xl),
            )

    def project(part, first):
        for t, region in enumerate((qr_ref, kr, vr)):

            def chunk(i, carry, t=t, region=region):
                rows = pl.ds(4 * i, 4)
                out = nn(xr_ref[part, rows].reshape(192, 512), wg_ref[t, part].reshape(512, 512))
                if first:
                    acc[t, rows] = out.reshape(4, 6, 8, 512)
                else:
                    out = out.reshape(4, 6, 8, 512) + acc[t, rows]
                    acc[t, rows] = out
                    region[rows] = out.astype(BF16).reshape(4, 48, 512)
                return carry

            lax.fori_loop(0, 5, chunk, 0)

    def hop(s, k):
        for t in range(3):
            for d in range(2):
                if k <= hops[s, d]:
                    arrived(s, d, k - 1, t)
                if k < hops[s, d]:
                    forward(s, d, k, t)

    hop(0, 1)
    hop(1, 1)
    hop(0, 2)
    locals_[0].wait()
    for dn, piece in pieces:
        region_came(0, xr_ref.at[core], dn, piece)
    go(xr_ref.at[core], xr_ref.at[core], s_send, s_recv, sibling)
    hop(1, 2)
    send_region(1, (-1, 1))
    hop(0, 3)
    hop(1, 3)
    hop(0, 4)
    for hf in range(2):
        bias[hf] = window_bias(hf)
    came(xr_ref.at[other], s_send, s_recv)
    project(xh, True)
    hop(1, 4)
    project(1 - xh, False)
    for t in range(3):
        for hf in range(2):
            own_t = acc[t, 6:14, 1 + 2 * hf : 3 + 2 * hf].reshape(128, 512).astype(BF16)
            if t == 0:
                qown[hf] = own_t * SCALE
            elif t == 1:
                kown_ref[hf] = own_t * SCALE
            else:
                vown_ref[hf] = own_t

    locals_[1].wait()
    region_came(1, gr_ref, 0, 0)
    came(acts.at[other], act_send, act_recv)
    inner = lax.broadcasted_iota(jnp.int32, (128, 128), 0)
    for hf in range(2):
        groups = pl.ds(1 + 2 * hf, 2)
        gown[hf] = gr_ref[6:14, groups].astype(F32).reshape(128, 512).astype(BF16)
        on_tokens[hf] = jnp.where(lax.rem(inner, 16) < 8, acts[hf, 0:1, :], acts[hf, 1:2, :])

    low, masks, lane = head_masks()

    def query_side(hp):
        lanes = slice(128 * hp, 128 * hp + 128)

        def side(hf, carry):
            window = pl.ds(pl.multiple_of(16 * hf, 16), 32)
            keys = kr[:, window, lanes].reshape(640, 128)
            values = vr[:, window, lanes].reshape(640, 128)
            query = qown[hf, :, lanes]
            grad = gown[hf, :, lanes]
            active = on_tokens[hf]
            on = active > 0.0
            s = nt(stacked(query, masks), keys)
            s = (s.reshape(2, 128, 640) + bias[hf]).reshape(256, 640)
            top = jnp.max(s, axis=1, keepdims=True)
            e = jnp.exp(s - top)
            total = jnp.sum(e, axis=1, keepdims=True)
            e = e * (1.0 / total)
            lse = top + jnp.log(total)
            out = nn(e.astype(BF16), values).astype(BF16).astype(F32)
            gm = stacked(grad, masks)
            delta = jnp.sum(gm.astype(F32) * out, axis=1, keepdims=True)
            dp = nt(gm, values)
            ds = (e * (dp - delta) * SCALE).astype(BF16)
            dqs = nn(ds, keys)
            ld = jnp.zeros((128, 128), F32)
            for j in range(2):
                rows = slice(128 * j, 128 * j + 128)
                ld = jnp.where(lane == j, jnp.where(on, lse[rows], HUGE), ld)
                ld = jnp.where(lane == j + 2, jnp.where(on, delta[rows], 0.0), ld)
            ldall[:, pl.ds(pl.multiple_of(16 * hf, 16), 16), :] = ld.reshape(8, 16, 128)
            attn_ref[hf, :, lanes] = (jnp.where(low, out[:128], out[128:]) * active).astype(BF16)
            dq_ref[hp, hf] = (jnp.where(low, dqs[:128], dqs[128:]) * active).astype(BF16)
            return carry

        lax.fori_loop(0, 2, side, 0)
        for i in range(2):
            ld_ref[hp, :, 128 * i : 128 * i + 128] = (
                ldall[4 * i : 4 * i + 4].reshape(128, 128).T[:8]
            )
        ldb[hp, 1, 1] = ld_ref[hp]
        for dn, dc in NEAR:
            go(
                ld_ref.at[hp], ldb.at[hp, 1 - dn, 1 - dc], ld_send.at[hp, dn + 1, dc + 1],
                ld_recv.at[hp, 1 - dn, 1 - dc], device(n + dn + 8, chip + dc + 16, core),
            )

    def share_q(j):
        for d in (2, 1, 3):
            go(
                dq_ref.at[2 * j + lax.rem(ypeer(d), 2)], gall.at[4 - d, Q_BLOCKS[j]],
                q_send.at[j, d - 1], q_recv.at[j, 3 - d], at(xh, z, core, ypeer(d), xl),
            )

    def share(hp):
        for d in (2, 1, 3):
            go(
                kv.at[hp, lax.rem(ypeer(d), 2)], gall.at[4 - d, KV_BLOCKS[hp]],
                k_send.at[hp, d - 1], k_recv.at[hp, 3 - d], at(xh, z, core, ypeer(d), xl),
            )

    def product(b):
        columns = gall[:, b].reshape(1024, 128)

        def rows(i, carry):
            out = nn(xt_ref[pl.ds(pl.multiple_of(i * 128, 128), 128), :], columns)
            p[b, pl.ds(2 * i, 2)] = out.reshape(2, 2, 2, 2, 8, 128)
            return carry

        lax.fori_loop(0, 4, rows, 0)
        for i in (2, 0, 1):
            a, l = flip(xh, XPEERS[i][0]), flip(xl, XPEERS[i][1])
            go(p.at[b, :, l, a], rx.at[b, i], x_send.at[b, i], x_recv.at[b, i], at(a, z, core, y, l))

    def product_q(j):
        b = Q_BLOCKS[j]
        for r in range(3):
            came(gall.at[r + 1, b], q_send.at[j, r], q_recv.at[j, r])
        gall[0, b] = dq_ref[2 * j + col_half]
        product(b)

    def product_kv(hp):
        b = KV_BLOCKS[hp]
        for r in range(3):
            came(gall.at[r + 1, b], k_send.at[hp, r], k_recv.at[hp, r])
        gall[0, b] = kv[hp, col_half]
        product(b)

    def sum_x(b):
        for i in range(3):
            came(rx.at[b, i], x_send.at[b, i], x_recv.at[b, i])
        for j in range(8):
            cz[j, b] = p[b, j, xl, xh] + rx[b, 0, j] + rx[b, 1, j] + rx[b, 2, j]

    batches = ((0, 4), (4, 2))

    def spread(h):
        lo, count = batches[h]
        for d in (4, 3, 5, 2, 6, 1, 7):
            go(
                cz.at[zpeer(d), pl.ds(lo, count)], rc.at[d - 1, pl.ds(lo, count)],
                c_send.at[h, d - 1], c_recv.at[h, d - 1], at(xh, zpeer(d), core, y, xl),
            )

    factor = 1.0 / math.sqrt(32768.0)

    def sum_z(h):
        lo, count = batches[h]
        for d in range(7):
            came(rc.at[d, pl.ds(lo, count)], c_send.at[h, d], c_recv.at[h, d])
        for b in range(lo, lo + count):
            total = cz[z, b]
            for d in range(7):
                total = total + rc[d, b]
            total = total.reshape(16, 128) * factor
            if b in Q_BLOCKS:
                fin_q[Q_BLOCKS.index(b)] = total
            else:
                hp = KV_BLOCKS.index(b)
                fin_kv[hp // 2, :, 128 * (hp % 2) : 128 * (hp % 2) + 128] = total

    column = lax.rem(lax.broadcasted_iota(jnp.int32, (8, 256), 1), 32)

    def totals_came(hp):
        for dn, dc in NEAR:
            came(
                ldb.at[hp, 1 - dn, 1 - dc], ld_send.at[hp, dn + 1, dc + 1],
                ld_recv.at[hp, 1 - dn, 1 - dc],
            )
        for hf in range(2):
            parts = []
            for r in range(3):
                left, mid, right = ldb[hp, r, 0], ldb[hp, r, 1], ldb[hp, r, 2]
                if hf == 0:
                    part = jnp.where(column < 8, pltpu.roll(left, 232, 1), pltpu.roll(mid, 8, 1))
                else:
                    part = jnp.where(column < 24, pltpu.roll(mid, 248, 1), pltpu.roll(right, 24, 1))
                parts.append(part)
            lds[hp, hf] = pltpu.roll(jnp.concatenate(parts, axis=1), 768 - 64, 1)[:, :640]

    def key_side(hp):
        lanes = slice(128 * hp, 128 * hp + 128)
        totals_came(hp)

        def side(hf, carry):
            window = pl.ds(pl.multiple_of(16 * hf, 16), 32)
            query = qr_ref[:, window, lanes].reshape(640, 128)
            grad = grs_ref[:, window, lanes].reshape(640, 128)
            keys = kown_ref[hf, :, lanes]
            values = vown_ref[hf, :, lanes]
            s = nt(stacked(keys, masks), query).reshape(2, 128, 640) + bias[hf]
            e = jnp.exp(s - lds[hp, hf, 0:2].reshape(2, 1, 640))
            dvs = nn(e.astype(BF16).reshape(256, 640), grad)
            dp = nt(stacked(values, masks), grad).reshape(2, 128, 640)
            ds = (e * (dp - lds[hp, hf, 2:4].reshape(2, 1, 640)) * SCALE).astype(BF16)
            dks = nn(ds.reshape(256, 640), query)
            kv[hp, 0, hf] = jnp.where(low, dks[:128], dks[128:]).astype(BF16)
            kv[hp, 1, hf] = jnp.where(low, dvs[:128], dvs[128:]).astype(BF16)
            return carry

        lax.fori_loop(0, 2, side, 0)
        share(hp)

    def spots(c, part, a):
        rows = pl.ds(pl.multiple_of(16 * a, 16), 16)
        q_at = c * 512 + part * 128
        kv_at = (1 + part) * 1024 + c * 512
        return [
            gw_out.at[rows, pl.ds(pl.multiple_of(first, 128), count)]
            for first, count in ((q_at, 128), (q_at + 256, 128), (kv_at, 256), (kv_at + 256, 256))
        ]

    finals = [fin_q.at[0], fin_q.at[1], fin_kv.at[0], fin_kv.at[1]]
    mine_at = spots(core, col_half, xh)
    is_here = (core == xl) & (row_half == xh)
    kept = []

    def deliver(which):
        for i in which:
            fin, spot, recv = finals[i], mine_at[i], f_recv.at[i, core, col_half, xh]
            for d in (2, 1, 3):
                for b in (0, 1):
                    go(fin, spot, f_send.at[i, d, b], recv, at(row_half, z, xl, ypeer(d), flip(xl, b)))
            go(fin, spot, f_send.at[i, 0, 1], recv, at(row_half, z, xl, y, 1 - xl))
            away = remote(fin, spot, f_send.at[i, 0, 0], recv, at(row_half, z, xl, y, xl))
            here = pltpu.make_async_copy(fin, spot, f_local.at[i])

            kept.append((here, away))

            @pl.when(is_here)
            def _():
                here.start()

            @pl.when(jnp.logical_not(is_here))
            def _():
                away.start()

    query_side(0)
    query_side(1)
    share_q(0)
    for dn, piece in pieces:
        if (dn, piece) != (0, 0):
            region_came(1, gr_ref, dn, piece)

    def regroup(i, carry):
        rows = gr_ref[pl.ds(4 * i, 4)].astype(F32).reshape(192, 512)
        grs_ref[pl.ds(4 * i, 4)] = rows.astype(BF16).reshape(4, 48, 512)
        return carry

    lax.fori_loop(0, 5, regroup, 0)
    for r in range(3):
        for c in range(2):
            came(xall_ref.at[r, c], e_send.at[r, c], e_recv.at[r, c])
    for hf in range(2):
        groups = pl.ds(1 + 2 * hf, 2)
        for r in range(4):
            if r == 0:
                tokens = xr_ref[row_half, 6:14, groups]
            else:
                tokens = xall_ref[r - 1, hf]
            tokens = tokens.astype(F32).reshape(128, 512)
            to_lane = 256 * r + 128 * hf
            for i in range(4):
                xt_ref[128 * i : 128 * i + 128, to_lane : to_lane + 128] = (
                    tokens[:, 128 * i : 128 * i + 128].T.astype(BF16)
                )
    key_side(0)
    query_side(2)
    product_q(0)
    key_side(1)
    product_kv(0)
    query_side(3)
    share_q(1)
    go(attn_ref.at[other], attn_out.at[:, half_of(core)], a_send, a_recv, sibling)
    attn_own = pltpu.make_async_copy(attn_ref.at[core], attn_out.at[:, half_of(core)], o_sem.at[0])
    attn_own.start()
    product_kv(1)
    key_side(2)
    product_q(1)
    sum_x(0)
    sum_x(1)
    key_side(3)
    product_kv(2)
    sum_x(2)
    sum_x(3)
    spread(0)

    all_q = jnp.concatenate([dq_ref[h].reshape(256, 128) for h in range(4)], axis=1)
    all_k = jnp.concatenate([kv[h, 0].reshape(256, 128) for h in range(4)], axis=1)
    all_v = jnp.concatenate([kv[h, 1].reshape(256, 128) for h in range(4)], axis=1)

    def input_columns(i, carry):
        rows = pl.ds(pl.multiple_of(i * 256, 256), 256)
        part = [wg_ref[t, i // 2, pl.ds(4 * lax.rem(i, 2), 4)].reshape(256, 512) for t in range(3)]
        total = nt(all_q, part[0]) + nt(all_k, part[1]) + nt(all_v, part[2])
        gx[:, :, rows] = total.reshape(2, 128, 256)
        return carry

    lax.fori_loop(0, 4, input_columns, 0)
    go(gx.at[other], gxr, g_send, g_recv, sibling)
    product_kv(3)
    sum_z(0)
    deliver(range(3))
    sum_x(4)
    sum_x(5)
    spread(1)
    came(gxr, g_send, g_recv)
    gxo[...] = (gx[core] + gxr[...]).astype(BF16)
    gx_own = pltpu.make_async_copy(gxo, gx_out, o_sem.at[1])
    gx_own.start()
    sum_z(1)
    deliver((3,))

    attn_own.wait()
    gx_own.wait()
    came(attn_out.at[:, half_of(other)], a_send, a_recv)
    for c in range(2):
        for part in range(2):
            for a in range(2):
                landed = spots(c, part, a)
                own = (
                    (c == core) & (part == col_half) & (a == xh) & (row_half == xh) & (xl == core)
                )
                for i in range(4):

                    @pl.when(jnp.logical_not(own))
                    def _():
                        came(landed[i], f_send.at[i, 0, 0], f_recv.at[i, c, part, a])

    for here, away in kept:

        @pl.when(is_here)
        def _():
            here.wait()

        @pl.when(jnp.logical_not(is_here))
        def _():
            away.wait_send()

    for cp in sends:
        cp.wait_send()


def layer(x4, g4, weight, block_list, block_count):
    dma = pltpu.SemaphoreType.DMA
    vmem = lambda *shape: pltpu.VMEM(shape, F32)
    half = lambda *shape: pltpu.VMEM(shape, BF16)
    shape = jax.ShapeDtypeStruct
    smem = pl.BlockSpec(memory_space=pltpu.SMEM)
    return pl.pallas_call(
        layer_kernel,
        out_shape=(
            shape((128, 1024), BF16), shape((128, 1024), BF16), shape((32, 3072), F32),
        ),
        in_specs=[VM] * 3 + [smem] * 2,
        out_specs=(ANY,) * 3,
        scratch_shapes=[
            half(2, 20, 6, 8, 512), half(20, 6, 8, 512), half(3, 2, 8, 2, 32, 512),
            half(3, 2, 8, 2, 8, 512), vmem(2, 8, 128),
            vmem(3, 20, 6, 8, 512), half(20, 48, 512), half(20, 48, 512), half(20, 48, 512),
            half(20, 48, 512), half(2, 128, 512), half(2, 128, 512), half(2, 128, 512),
            half(2, 128, 512), vmem(2, 128, 128), vmem(8, 32, 128), vmem(4, 8, 256),
            half(4, 2, 128, 128), half(2, 128, 512), half(512, 1024),
            half(4, 6, 2, 128, 128), vmem(6, 8, 2, 2, 2, 8, 128), vmem(6, 3, 8, 2, 8, 128),
            vmem(8, 6, 2, 8, 128), vmem(7, 6, 2, 8, 128), vmem(2, 16, 128), vmem(2, 16, 256),
            half(4, 2, 2, 128, 128), vmem(4, 2, 8, 640), vmem(4, 3, 3, 8, 256), vmem(2, 128, 640),
            vmem(2, 128, 1024), vmem(128, 1024), half(128, 1024),
            dma((2, 3, 2, 2)), dma((2, 3, 4)), dma((2,)), dma, dma, dma, dma,
            dma((3,)), dma((3,)), dma((3,)), dma((3,)), dma((3,)),
            dma((2, 2, 4, 3)), dma((2, 2, 4, 3)), dma((3, 2)), dma((3, 2)),
            dma((4, 3, 3)), dma((4, 3, 3)), dma((2,)), dma, dma, dma, dma,
            dma((2, 3)), dma((2, 3)), dma((4, 3)), dma((4, 3)), dma((6, 3)), dma((6, 3)),
            dma((2, 7)), dma((2, 7)), dma((4, 4, 2)), dma((4, 2, 2, 2)), dma((4,)),
        ],
        compiler_params=pltpu.CompilerParams(
            collective_id=0, has_side_effects=True, vmem_limit_bytes=VMEM_LIMIT
        ),
        name="layer",
    )(x4, g4, weight, block_list, block_count)


def local(image_tokens, qkv_weight, block_list, block_count, out_grad):
    attn_out, grad_x, grad_w = layer(
        image_tokens.reshape(8, 2, 8, 1024), out_grad.reshape(8, 2, 8, 1024), qkv_weight,
        block_list, block_count,
    )
    return attn_out.reshape(8, 16, 1024), grad_x.reshape(8, 16, 1024), grad_w


def solution(mesh):
    placed = (
        P("narrow", "wide", None),
        P("wide", None),
        P("narrow", "wide"),
        P("narrow", "wide"),
        P("narrow", "wide", None),
    )
    return jax.shard_map(
        local,
        mesh=mesh,
        in_specs=placed,
        out_specs=(P("narrow", "wide", None), P("narrow", "wide", None), P("wide", None)),
        check_vma=False,
    )
```

```python
import functools
import math

import jax
import jax.numpy as jnp
from jax import lax
from jax.experimental import pallas as pl
from jax.experimental.pallas import tpu as pltpu
from jax.sharding import PartitionSpec as P

MESH = pl.DeviceIdType.MESH
F32 = jnp.float32
BF16 = jnp.bfloat16
RADIUS = 6
NEGATIVE = -1e30
HUGE = 1e30
SCALE = 0.125
VMEM_LIMIT = 60 * 1024 * 1024
ANY = pl.BlockSpec(memory_space=pl.ANY)
VM = pl.BlockSpec(memory_space=pltpu.VMEM)

ROWS = {-1: (0, 6, 14), 0: (0, 8, 6), 1: (2, 6, 0)}


def place():
    wide = lax.axis_index("wide")
    narrow = lax.axis_index("narrow")
    return narrow, wide // 2, wide % 2


def device(narrow, chip, core):
    return {"wide": lax.rem(chip, 16) * 2 + core, "narrow": lax.rem(narrow, 8)}


def remote(src, dst, send, recv, to):
    return pltpu.make_async_remote_copy(
        src_ref=src, dst_ref=dst, send_sem=send, recv_sem=recv, device_id=to, device_id_type=MESH
    )


def greet(devices):
    barrier = pltpu.get_barrier_semaphore()
    for to in devices:
        pl.semaphore_signal(barrier, inc=1, device_id=to, device_id_type=MESH)
    pl.semaphore_wait(barrier, len(devices))


def half_of(core):
    return pl.ds(pl.multiple_of(core * 512, 512), 512)


def window_bias(hf):
    n, chip, _ = place()
    shape = (128, 640)
    inner = lax.broadcasted_iota(jnp.int32, shape, 0)
    outer = lax.broadcasted_iota(jnp.int32, shape, 1)
    row, col = outer // 32, outer % 32
    down = row - RADIUS - inner // 16
    across = col - 8 - inner % 16
    grid_row = n * 8 - RADIUS + row
    grid_col = chip * 32 - 8 + 16 * hf + col
    ok = (jnp.abs(down) <= RADIUS) & (jnp.abs(across) <= RADIUS)
    ok = ok & (grid_row >= 0) & (grid_row < 64) & (grid_col >= 0) & (grid_col < 512)
    return jnp.where(ok, 0.0, NEGATIVE)


def nt(a, b):
    return lax.dot_general(a, b, (((1,), (1,)), ((), ())), preferred_element_type=F32)


def nn(a, b):
    return jnp.dot(a, b, preferred_element_type=F32)


def tn(a, b):
    return lax.dot_general(a, b, (((0,), (0,)), ((), ())), preferred_element_type=F32)


def stacked(pair, masks):
    return jnp.concatenate([pair * masks[0], pair * masks[1]], axis=0)


def head_masks():
    lane = lax.broadcasted_iota(jnp.int32, (128, 128), 1)
    low = lane < 64
    return low, (low.astype(F32).astype(BF16), (1.0 - low.astype(F32)).astype(BF16)), lane


XPEERS = ((0, 1), (1, 0), (1, 1))
NEAR = tuple((dn, dc) for dn in (-1, 0, 1) for dc in (-1, 0, 1) if (dn, dc) != (0, 0))


Q_BLOCKS = (0, 3)
KV_BLOCKS = (1, 2, 4, 5)


def layer_kernel(
    x_ref, g_ref, w_ref, list_ref, count_ref,
    attn_out, gx_out, gw_out,
    xr_ref, gr_ref, wg_ref, xall_ref, acts,
    acc, qr_ref, kr, vr, grs_ref, qown, kown_ref, vown_ref, gown, on_tokens, ldall, ld_ref,
    dq_ref, attn_ref, xt_ref,
    gall, p, rx, cz, rc, fin_q, fin_kv, kv, lds, ldb, bias, gx, gxr, gxo,
    h_send, h_recv, h_local, s_send, s_recv, act_send, act_recv,
    w_send, w_recv, w_local, p_send, p_recv, r_send, r_recv, e_send, e_recv,
    ld_send, ld_recv, o_sem, a_send, a_recv, g_send, g_recv,
    q_send, q_recv, k_send, k_recv, x_send, x_recv, c_send, c_recv, f_send, f_recv, f_local,
):
    n, chip, core = place()
    other = 1 - core
    z = lax.rem(chip, 8)
    xh = chip // 8
    y = n // 2
    xl = lax.rem(n, 2)
    row_half = y // 2
    col_half = lax.rem(y, 2)

    def at(xh_, z_, core_, y_, xl_):
        return device(y_ * 2 + xl_, xh_ * 8 + z_, core_)

    def ypeer(d):
        return lax.rem(y + d, 4)

    def zpeer(d):
        return lax.rem(z + d + 8, 8)

    def flip(value, by):
        return 1 - value if by else value

    for block in range(2):
        on = jnp.float32(0.0)
        for i in range(2):
            hit = (count_ref[0, 0] > i) & (list_ref[0, i] == block)
            on = jnp.maximum(on, jnp.where(hit, 1.0, 0.0))
        acts[core, block : block + 1, :] = jnp.full((1, 128), on, F32)

    sibling = at(xh, z, other, y, xl)
    up = at(xh, zpeer(1), core, y, xl)
    down = at(xh, zpeer(-1), core, y, xl)
    partner = at(1 - xh, z, core, y, 1 - xl)
    peers = [device(n + dn + 8, chip + dc + 16, c) for dn, dc in NEAR for c in (0, 1)]
    peers += [at(xh, zpeer(d), core, y, xl) for d in range(1, 8)]
    for a in (0, 1):
        for c in (0, 1):
            for d in range(4):
                for b in (0, 1):
                    if (a, c, d, b) != (0, 0, 0, 0):
                        peers.append(at(flip(xh, a), z, flip(core, c), ypeer(d), flip(xl, b)))
    greet(peers)

    sends = []

    def go(src, dst, send, recv, to):
        cp = remote(src, dst, send, recv, to)
        cp.start()
        sends.append(cp)

    def came(dst, send, recv):
        remote(dst, dst, send, recv, sibling).wait_recv()

    own = []
    for t in range(3):
        here = wg_ref.at[t, xh, z, core]
        go(
            w_ref.at[:, pl.ds(pl.multiple_of(t * 1024 + other * 512, 512), 512)],
            here, w_send.at[t], w_recv.at[t], sibling,
        )
        cp = pltpu.make_async_copy(
            w_ref.at[:, pl.ds(pl.multiple_of(t * 1024 + core * 512, 512), 512)], here, w_local.at[t]
        )
        cp.start()
        own.append(cp)
    go(acts.at[core], acts.at[core], act_send, act_recv, sibling)

    hops = {(0, 0): 4, (0, 1): 3, (1, 0): 3, (1, 1): 4}

    def slab(t, s, index):
        return wg_ref.at[t, xh if s == 0 else 1 - xh, lax.rem(index + 16, 8)]

    def forward(s, d, k, t):
        moved = slab(t, s, z - k if d == 0 else z + k)
        go(moved, moved, r_send.at[s, d, k, t], r_recv.at[s, d, k, t], up if d == 0 else down)

    def arrived(s, d, k, t):
        came(
            slab(t, s, z - 1 - k if d == 0 else z + 1 + k),
            r_send.at[s, d, k, t], r_recv.at[s, d, k, t],
        )

    for t in range(3):
        own[t].wait()
        came(wg_ref.at[t, xh, z, other], w_send.at[t], w_recv.at[t])
        mine = slab(t, 0, z)
        go(mine, mine, p_send.at[t], p_recv.at[t], partner)
        forward(0, 0, 0, t)
        forward(0, 1, 0, t)

    side_chip = chip + 2 * core - 1 + 16
    tensors = ((x_ref, lambda c: xr_ref.at[c]), (g_ref, lambda c: gr_ref))
    locals_ = []

    def send_region(i, dns):
        src, dst = tensors[i]
        for dn in dns:
            lo, count, to_row = ROWS[dn]
            for side in (0, 1):
                for rel in (0, 1):
                    c = core if rel == 0 else other
                    if side == 0:
                        source = src.at[pl.ds(lo, count), :, :, half_of(c)]
                        target = dst(c).at[pl.ds(to_row, count), pl.ds(1 + 2 * core, 2)]
                        slot = core
                        to = device(n + dn + 8, chip, c)
                    else:
                        source = src.at[pl.ds(lo, count), pl.ds(core, 1), :, half_of(c)]
                        target = dst(c).at[pl.ds(to_row, count), pl.ds(5 * other, 1)]
                        slot = 3 - core
                        to = device(n + dn + 8, side_chip, c)
                    if dn == 0 and side == 0 and rel == 0:
                        cp = pltpu.make_async_copy(source, target, h_local.at[i])
                        cp.start()
                        locals_.append(cp)
                    else:
                        go(
                            source, target, h_send.at[i, dn + 1, side, rel],
                            h_recv.at[i, dn + 1, slot], to,
                        )

    def region_came(i, dst, dn, piece):
        lo, count, to_row = ROWS[dn]
        if piece < 2:
            slot = other if dn == 0 else piece
            landed = dst.at[pl.ds(to_row, count), pl.ds(1 + 2 * slot, 2)]
        else:
            slot = piece
            landed = dst.at[pl.ds(to_row, count), pl.ds(0 if piece == 2 else 5, 1)]
        came(landed, h_send.at[i, dn + 1, 0, 0], h_recv.at[i, dn + 1, slot])

    pieces = [(dn, piece) for dn in (-1, 0, 1) for piece in range(4) if (dn, piece) != (0, 1)]
    send_region(0, (-1, 1, 0))
    for t in range(3):
        came(slab(t, 1, z), p_send.at[t], p_recv.at[t])
        forward(1, 0, 0, t)
        forward(1, 1, 0, t)
    send_region(1, (0,))
    for d in (2, 1, 3):
        want = ypeer(d) // 2
        for rel in (0, 1):
            go(
                x_ref.at[:, :, :, half_of(want)], xall_ref.at[3 - d, core],
                e_send.at[d - 1, rel], e_recv.at[3 - d, core],
                at(xh, z, core if rel == 0 else other, ypeer(d), xl),
            )

    def project(part, first):
        for t, region in enumerate((qr_ref, kr, vr)):

            def chunk(i, carry, t=t, region=region):
                rows = pl.ds(4 * i, 4)
                out = nn(xr_ref[part, rows].reshape(192, 512), wg_ref[t, part].reshape(512, 512))
                if first:
                    acc[t, rows] = out.reshape(4, 6, 8, 512)
                else:
                    out = out.reshape(4, 6, 8, 512) + acc[t, rows]
                    acc[t, rows] = out
                    region[rows] = out.astype(BF16).reshape(4, 48, 512)
                return carry

            lax.fori_loop(0, 5, chunk, 0)

    def hop(s, k):
        for t in range(3):
            for d in range(2):
                if k <= hops[s, d]:
                    arrived(s, d, k - 1, t)
                if k < hops[s, d]:
                    forward(s, d, k, t)

    hop(0, 1)
    hop(1, 1)
    hop(0, 2)
    locals_[0].wait()
    for dn, piece in pieces:
        region_came(0, xr_ref.at[core], dn, piece)
    go(xr_ref.at[core], xr_ref.at[core], s_send, s_recv, sibling)
    hop(1, 2)
    send_region(1, (-1, 1))
    hop(0, 3)
    hop(1, 3)
    hop(0, 4)
    for hf in range(2):
        bias[hf] = window_bias(hf)
    came(xr_ref.at[other], s_send, s_recv)
    project(xh, True)
    hop(1, 4)
    project(1 - xh, False)
    for t in range(3):
        for hf in range(2):
            own_t = acc[t, 6:14, 1 + 2 * hf : 3 + 2 * hf].reshape(128, 512).astype(BF16)
            if t == 0:
                qown[hf] = own_t * SCALE
            elif t == 1:
                kown_ref[hf] = own_t * SCALE
            else:
                vown_ref[hf] = own_t

    locals_[1].wait()
    region_came(1, gr_ref, 0, 0)
    came(acts.at[other], act_send, act_recv)
    inner = lax.broadcasted_iota(jnp.int32, (128, 128), 0)
    for hf in range(2):
        groups = pl.ds(1 + 2 * hf, 2)
        gown[hf] = gr_ref[6:14, groups].astype(F32).reshape(128, 512).astype(BF16)
        on_tokens[hf] = jnp.where(lax.rem(inner, 16) < 8, acts[hf, 0:1, :], acts[hf, 1:2, :])

    low, masks, lane = head_masks()

    def query_side(hp):
        lanes = slice(128 * hp, 128 * hp + 128)

        def side(hf, carry):
            window = pl.ds(pl.multiple_of(16 * hf, 16), 32)
            keys = kr[:, window, lanes].reshape(640, 128)
            values = vr[:, window, lanes].reshape(640, 128)
            query = qown[hf, :, lanes]
            grad = gown[hf, :, lanes]
            active = on_tokens[hf]
            on = active > 0.0
            s = nt(stacked(query, masks), keys)
            s = (s.reshape(2, 128, 640) + bias[hf]).reshape(256, 640)
            top = jnp.max(s, axis=1, keepdims=True)
            e = jnp.exp(s - top)
            total = jnp.sum(e, axis=1, keepdims=True)
            e = e * (1.0 / total)
            lse = top + jnp.log(total)
            out = nn(e.astype(BF16), values).astype(BF16).astype(F32)
            gm = stacked(grad, masks)
            delta = jnp.sum(gm.astype(F32) * out, axis=1, keepdims=True)
            dp = nt(gm, values)
            ds = (e * (dp - delta) * SCALE).astype(BF16)
            dqs = nn(ds, keys)
            ld = jnp.zeros((128, 128), F32)
            for j in range(2):
                rows = slice(128 * j, 128 * j + 128)
                ld = jnp.where(lane == j, jnp.where(on, lse[rows], HUGE), ld)
                ld = jnp.where(lane == j + 2, jnp.where(on, delta[rows], 0.0), ld)
            ldall[:, pl.ds(pl.multiple_of(16 * hf, 16), 16), :] = ld.reshape(8, 16, 128)
            attn_ref[hf, :, lanes] = (jnp.where(low, out[:128], out[128:]) * active).astype(BF16)
            dq_ref[hp, hf] = (jnp.where(low, dqs[:128], dqs[128:]) * active).astype(BF16)
            return carry

        lax.fori_loop(0, 2, side, 0)
        for i in range(2):
            ld_ref[hp, :, 128 * i : 128 * i + 128] = (
                ldall[4 * i : 4 * i + 4].reshape(128, 128).T[:8]
            )
        ldb[hp, 1, 1] = ld_ref[hp]
        for dn, dc in NEAR:
            go(
                ld_ref.at[hp], ldb.at[hp, 1 - dn, 1 - dc], ld_send.at[hp, dn + 1, dc + 1],
                ld_recv.at[hp, 1 - dn, 1 - dc], device(n + dn + 8, chip + dc + 16, core),
            )

    def share_q(j):
        for d in (2, 1, 3):
            go(
                dq_ref.at[2 * j + lax.rem(ypeer(d), 2)], gall.at[4 - d, Q_BLOCKS[j]],
                q_send.at[j, d - 1], q_recv.at[j, 3 - d], at(xh, z, core, ypeer(d), xl),
            )

    def share(hp):
        for d in (2, 1, 3):
            go(
                kv.at[hp, lax.rem(ypeer(d), 2)], gall.at[4 - d, KV_BLOCKS[hp]],
                k_send.at[hp, d - 1], k_recv.at[hp, 3 - d], at(xh, z, core, ypeer(d), xl),
            )

    def product(b):
        columns = gall[:, b].reshape(1024, 128)

        def rows(i, carry):
            out = nn(xt_ref[pl.ds(pl.multiple_of(i * 128, 128), 128), :], columns)
            p[b, pl.ds(2 * i, 2)] = out.reshape(2, 2, 2, 2, 8, 128)
            return carry

        lax.fori_loop(0, 4, rows, 0)
        for i in (2, 0, 1):
            a, l = flip(xh, XPEERS[i][0]), flip(xl, XPEERS[i][1])
            go(p.at[b, :, l, a], rx.at[b, i], x_send.at[b, i], x_recv.at[b, i], at(a, z, core, y, l))

    def product_q(j):
        b = Q_BLOCKS[j]
        for r in range(3):
            came(gall.at[r + 1, b], q_send.at[j, r], q_recv.at[j, r])
        gall[0, b] = dq_ref[2 * j + col_half]
        product(b)

    def product_kv(hp):
        b = KV_BLOCKS[hp]
        for r in range(3):
            came(gall.at[r + 1, b], k_send.at[hp, r], k_recv.at[hp, r])
        gall[0, b] = kv[hp, col_half]
        product(b)

    def sum_x(b):
        for i in range(3):
            came(rx.at[b, i], x_send.at[b, i], x_recv.at[b, i])
        for j in range(8):
            cz[j, b] = p[b, j, xl, xh] + rx[b, 0, j] + rx[b, 1, j] + rx[b, 2, j]

    batches = ((0, 4), (4, 2))

    def spread(h):
        lo, count = batches[h]
        for d in (4, 3, 5, 2, 6, 1, 7):
            go(
                cz.at[zpeer(d), pl.ds(lo, count)], rc.at[d - 1, pl.ds(lo, count)],
                c_send.at[h, d - 1], c_recv.at[h, d - 1], at(xh, zpeer(d), core, y, xl),
            )

    factor = 1.0 / math.sqrt(32768.0)

    def sum_z(h):
        lo, count = batches[h]
        for d in range(7):
            came(rc.at[d, pl.ds(lo, count)], c_send.at[h, d], c_recv.at[h, d])
        for b in range(lo, lo + count):
            total = cz[z, b]
            for d in range(7):
                total = total + rc[d, b]
            total = total.reshape(16, 128) * factor
            if b in Q_BLOCKS:
                fin_q[Q_BLOCKS.index(b)] = total
            else:
                hp = KV_BLOCKS.index(b)
                fin_kv[hp // 2, :, 128 * (hp % 2) : 128 * (hp % 2) + 128] = total

    column = lax.rem(lax.broadcasted_iota(jnp.int32, (8, 256), 1), 32)

    def totals_came(hp):
        for dn, dc in NEAR:
            came(
                ldb.at[hp, 1 - dn, 1 - dc], ld_send.at[hp, dn + 1, dc + 1],
                ld_recv.at[hp, 1 - dn, 1 - dc],
            )
        for hf in range(2):
            parts = []
            for r in range(3):
                left, mid, right = ldb[hp, r, 0], ldb[hp, r, 1], ldb[hp, r, 2]
                if hf == 0:
                    part = jnp.where(column < 8, pltpu.roll(left, 232, 1), pltpu.roll(mid, 8, 1))
                else:
                    part = jnp.where(column < 24, pltpu.roll(mid, 248, 1), pltpu.roll(right, 24, 1))
                parts.append(part)
            lds[hp, hf] = pltpu.roll(jnp.concatenate(parts, axis=1), 768 - 64, 1)[:, :640]

    def key_side(hp):
        lanes = slice(128 * hp, 128 * hp + 128)
        totals_came(hp)

        def side(hf, carry):
            window = pl.ds(pl.multiple_of(16 * hf, 16), 32)
            query = qr_ref[:, window, lanes].reshape(640, 128)
            grad = grs_ref[:, window, lanes].reshape(640, 128)
            keys = kown_ref[hf, :, lanes]
            values = vown_ref[hf, :, lanes]
            s = nt(stacked(keys, masks), query).reshape(2, 128, 640) + bias[hf]
            e = jnp.exp(s - lds[hp, hf, 0:2].reshape(2, 1, 640))
            dvs = nn(e.astype(BF16).reshape(256, 640), grad)
            dp = nt(stacked(values, masks), grad).reshape(2, 128, 640)
            ds = (e * (dp - lds[hp, hf, 2:4].reshape(2, 1, 640)) * SCALE).astype(BF16)
            dks = nn(ds.reshape(256, 640), query)
            kv[hp, 0, hf] = jnp.where(low, dks[:128], dks[128:]).astype(BF16)
            kv[hp, 1, hf] = jnp.where(low, dvs[:128], dvs[128:]).astype(BF16)
            return carry

        lax.fori_loop(0, 2, side, 0)
        share(hp)

    def spots(c, part, a):
        rows = pl.ds(pl.multiple_of(16 * a, 16), 16)
        q_at = c * 512 + part * 128
        kv_at = (1 + part) * 1024 + c * 512
        return [
            gw_out.at[rows, pl.ds(pl.multiple_of(first, 128), count)]
            for first, count in ((q_at, 128), (q_at + 256, 128), (kv_at, 256), (kv_at + 256, 256))
        ]

    finals = [fin_q.at[0], fin_q.at[1], fin_kv.at[0], fin_kv.at[1]]
    mine_at = spots(core, col_half, xh)
    is_here = (core == xl) & (row_half == xh)
    kept = []

    def deliver(which):
        for i in which:
            fin, spot, recv = finals[i], mine_at[i], f_recv.at[i, core, col_half, xh]
            for d in (2, 1, 3):
                for b in (0, 1):
                    go(fin, spot, f_send.at[i, d, b], recv, at(row_half, z, xl, ypeer(d), flip(xl, b)))
            go(fin, spot, f_send.at[i, 0, 1], recv, at(row_half, z, xl, y, 1 - xl))
            away = remote(fin, spot, f_send.at[i, 0, 0], recv, at(row_half, z, xl, y, xl))
            here = pltpu.make_async_copy(fin, spot, f_local.at[i])

            kept.append((here, away))

            @pl.when(is_here)
            def _():
                here.start()

            @pl.when(jnp.logical_not(is_here))
            def _():
                away.start()

    query_side(0)
    query_side(1)
    share_q(0)
    for dn, piece in pieces:
        if (dn, piece) != (0, 0):
            region_came(1, gr_ref, dn, piece)

    def regroup(i, carry):
        rows = gr_ref[pl.ds(4 * i, 4)].astype(F32).reshape(192, 512)
        grs_ref[pl.ds(4 * i, 4)] = rows.astype(BF16).reshape(4, 48, 512)
        return carry

    lax.fori_loop(0, 5, regroup, 0)
    for r in range(3):
        for c in range(2):
            came(xall_ref.at[r, c], e_send.at[r, c], e_recv.at[r, c])
    for hf in range(2):
        groups = pl.ds(1 + 2 * hf, 2)
        for r in range(4):
            if r == 0:
                tokens = xr_ref[row_half, 6:14, groups]
            else:
                tokens = xall_ref[r - 1, hf]
            tokens = tokens.astype(F32).reshape(128, 512)
            to_lane = 256 * r + 128 * hf
            for i in range(4):
                xt_ref[128 * i : 128 * i + 128, to_lane : to_lane + 128] = (
                    tokens[:, 128 * i : 128 * i + 128].T.astype(BF16)
                )
    key_side(0)
    query_side(2)
    product_q(0)
    key_side(1)
    product_kv(0)
    query_side(3)
    share_q(1)
    go(attn_ref.at[other], attn_out.at[:, half_of(core)], a_send, a_recv, sibling)
    attn_own = pltpu.make_async_copy(attn_ref.at[core], attn_out.at[:, half_of(core)], o_sem.at[0])
    attn_own.start()
    product_kv(1)
    key_side(2)
    product_q(1)
    sum_x(0)
    sum_x(1)
    key_side(3)
    product_kv(2)
    sum_x(2)
    sum_x(3)
    spread(0)

    all_q = jnp.concatenate([dq_ref[h].reshape(256, 128) for h in range(4)], axis=1)
    all_k = jnp.concatenate([kv[h, 0].reshape(256, 128) for h in range(4)], axis=1)
    all_v = jnp.concatenate([kv[h, 1].reshape(256, 128) for h in range(4)], axis=1)

    def input_columns(i, carry):
        rows = pl.ds(pl.multiple_of(i * 256, 256), 256)
        part = [wg_ref[t, i // 2, pl.ds(4 * lax.rem(i, 2), 4)].reshape(256, 512) for t in range(3)]
        total = nt(all_q, part[0]) + nt(all_k, part[1]) + nt(all_v, part[2])
        gx[:, :, rows] = total.reshape(2, 128, 256)
        return carry

    lax.fori_loop(0, 4, input_columns, 0)
    go(gx.at[other], gxr, g_send, g_recv, sibling)
    product_kv(3)
    sum_x(4)
    sum_z(0)
    sum_x(5)
    spread(1)
    deliver(range(3))
    came(gxr, g_send, g_recv)
    gxo[...] = (gx[core] + gxr[...]).astype(BF16)
    gx_own = pltpu.make_async_copy(gxo, gx_out, o_sem.at[1])
    gx_own.start()
    sum_z(1)
    deliver((3,))

    attn_own.wait()
    gx_own.wait()
    came(attn_out.at[:, half_of(other)], a_send, a_recv)
    for c in range(2):
        for part in range(2):
            for a in range(2):
                landed = spots(c, part, a)
                own = (
                    (c == core) & (part == col_half) & (a == xh) & (row_half == xh) & (xl == core)
                )
                for i in range(4):

                    @pl.when(jnp.logical_not(own))
                    def _():
                        came(landed[i], f_send.at[i, 0, 0], f_recv.at[i, c, part, a])

    for here, away in kept:

        @pl.when(is_here)
        def _():
            here.wait()

        @pl.when(jnp.logical_not(is_here))
        def _():
            away.wait_send()

    for cp in sends:
        cp.wait_send()


def layer(x4, g4, weight, block_list, block_count):
    dma = pltpu.SemaphoreType.DMA
    vmem = lambda *shape: pltpu.VMEM(shape, F32)
    half = lambda *shape: pltpu.VMEM(shape, BF16)
    shape = jax.ShapeDtypeStruct
    smem = pl.BlockSpec(memory_space=pltpu.SMEM)
    return pl.pallas_call(
        layer_kernel,
        out_shape=(
            shape((128, 1024), BF16), shape((128, 1024), BF16), shape((32, 3072), F32),
        ),
        in_specs=[VM] * 3 + [smem] * 2,
        out_specs=(ANY,) * 3,
        scratch_shapes=[
            half(2, 20, 6, 8, 512), half(20, 6, 8, 512), half(3, 2, 8, 2, 32, 512),
            half(3, 2, 8, 2, 8, 512), vmem(2, 8, 128),
            vmem(3, 20, 6, 8, 512), half(20, 48, 512), half(20, 48, 512), half(20, 48, 512),
            half(20, 48, 512), half(2, 128, 512), half(2, 128, 512), half(2, 128, 512),
            half(2, 128, 512), vmem(2, 128, 128), vmem(8, 32, 128), vmem(4, 8, 256),
            half(4, 2, 128, 128), half(2, 128, 512), half(512, 1024),
            half(4, 6, 2, 128, 128), vmem(6, 8, 2, 2, 2, 8, 128), vmem(6, 3, 8, 2, 8, 128),
            vmem(8, 6, 2, 8, 128), vmem(7, 6, 2, 8, 128), vmem(2, 16, 128), vmem(2, 16, 256),
            half(4, 2, 2, 128, 128), vmem(4, 2, 8, 640), vmem(4, 3, 3, 8, 256), vmem(2, 128, 640),
            vmem(2, 128, 1024), vmem(128, 1024), half(128, 1024),
            dma((2, 3, 2, 2)), dma((2, 3, 4)), dma((2,)), dma, dma, dma, dma,
            dma((3,)), dma((3,)), dma((3,)), dma((3,)), dma((3,)),
            dma((2, 2, 4, 3)), dma((2, 2, 4, 3)), dma((3, 2)), dma((3, 2)),
            dma((4, 3, 3)), dma((4, 3, 3)), dma((2,)), dma, dma, dma, dma,
            dma((2, 3)), dma((2, 3)), dma((4, 3)), dma((4, 3)), dma((6, 3)), dma((6, 3)),
            dma((2, 7)), dma((2, 7)), dma((4, 4, 2)), dma((4, 2, 2, 2)), dma((4,)),
        ],
        compiler_params=pltpu.CompilerParams(
            collective_id=0, has_side_effects=True, vmem_limit_bytes=VMEM_LIMIT
        ),
        name="layer",
    )(x4, g4, weight, block_list, block_count)


def local(image_tokens, qkv_weight, block_list, block_count, out_grad):
    attn_out, grad_x, grad_w = layer(
        image_tokens.reshape(8, 2, 8, 1024), out_grad.reshape(8, 2, 8, 1024), qkv_weight,
        block_list, block_count,
    )
    return attn_out.reshape(8, 16, 1024), grad_x.reshape(8, 16, 1024), grad_w


def solution(mesh):
    placed = (
        P("narrow", "wide", None),
        P("wide", None),
        P("narrow", "wide"),
        P("narrow", "wide"),
        P("narrow", "wide", None),
    )
    return jax.shard_map(
        local,
        mesh=mesh,
        in_specs=placed,
        out_specs=(P("narrow", "wide", None), P("narrow", "wide", None), P("wide", None)),
        check_vma=False,
    )
```
